32 devices in a mesh: cuts: 2 (over x), frame: 8 (over z, y), coil: 2 (over core).
Axes of the slice: x: 2, y: 2, z: 4, core: 2. Of those that a mesh axis runs over, the one named last changes fastest.
Arguments:
- spatial: bfloat16 [512, 32, 512], P(('cuts', 'coil', 'frame')), parts along dimension 0, may hold values from -6 to 6
- temporal: bfloat16 [32, 64], P(('cuts', 'frame')), parts along dimension 0, may hold values from -0.75 to 0.75
- kspace: bfloat16 [32, 32, 256, 512], P(('cuts', 'frame'), 'coil'), parts along dimension 0, may hold values from -2 to 2
- sampled: int32 [32, 256], P(('cuts', 'frame')), parts along dimension 0, may hold values 0 or 1
- sensitivity: bfloat16 [64, 256, 512], P(('cuts', 'coil')), parts along dimension 0, may hold values from -1 to 1
Outputs:
- spatial_grad: float32 [512, 32, 512], P(('cuts', 'coil', 'frame')), parts along dimension 0
- temporal_grad: float32 [32, 64], P(('cuts', 'frame')), parts along dimension 0
The draws below stay inside these ranges and needn't reach their ends.
There are 2 independent parts, one for each index of `cuts`. The reference program is written for one: setup_inputs(seed, part) draws one part's arguments, and reference() takes and returns one part's arrays. A program takes and returns all parts, laid end to end along the dimension named above; each array names one. Nothing has to cross between parts.
All inputs are finite; a program needn't handle non-finite values. No bound on the sum of `sampled` on one device may be relied on, other than what follows from the above.
Results may differ from the reference program's by a relative error of at most 0.003.
Values may be sent and summed in bfloat16 or wider, within the bound.
No kernel may reach another device: no remote copies, remote signals or barrier semaphores. Data moves between devices by JAX's collectives and lax.ppermute only.
A program may use at most 128 MiB of HBM per device.

```python
import math
import jax
import jax.numpy as jnp
from jax import lax

NX = 256
NY = 256
RANK = 32
COILS = 32
FRAMES = 16


def plant(array, own_key, least, high):
    extent = array.shape
    place = [jax.random.randint(jax.random.fold_in(own_key, axis), (), 0, extent[axis]) for axis in range(len(extent))]
    array = array.at[tuple(place)].set(least)
    longest = extent.index(max(extent))
    place[longest] = (place[longest] + 1) % extent[longest]
    return array.at[tuple(place)].set(high)


def steps_of(rng, extent, shards, low, largest):
    level = 1.0
    for axis_at, shards_of in shards:
        draws = jax.random.uniform(jax.random.fold_in(jax.random.fold_in(rng, 6), axis_at), (shards_of,), jnp.float32, low / len(shards), largest / len(shards))
        level = level * jnp.repeat(jnp.exp(draws), extent[axis_at] // shards_of).reshape((-1,) + (1,) * (len(extent) - 1 - axis_at))
    return level


def centred(own_key, extent, spread, bound, pieces=(), held_as=jnp.bfloat16):
    gain = steps_of(own_key, extent, pieces, -0.22, 0.18) if pieces else 1.0
    values = jax.random.normal(own_key, extent, jnp.float32) * spread * gain
    return jnp.minimum(jnp.maximum(values, -bound), bound).astype(held_as)


def setup_inputs(seed: int = 0, part: int = 0) -> dict:
    seeds = jax.random.split(jax.random.key(seed), 6)
    part_splits = jax.random.split(jax.random.fold_in(seeds[5], part), 6)
    spatial = centred(part_splits[0], (NX, RANK, 2 * NY), 1.0, 6.0, ((0, 16),))
    temporal = centred(part_splits[1], (FRAMES, 2 * RANK), (2 * RANK) ** -0.5, 0.75, ((0, 8),))
    kspace = centred(part_splits[2], (FRAMES, COILS, NX, 2 * NY), 0.3, 2.0, ((0, 8), (1, 2)))
    sampled = plant((jax.random.randint(part_splits[3], (FRAMES, NY), 0, 3) < 1).astype(jnp.int32), jax.random.fold_in(part_splits[3], 1), 0, 1)
    sensitivity = centred(part_splits[4], (COILS, NX, 2 * NY), 0.18, 1.0, ((0, 2),))
    return {"spatial": spatial, "temporal": temporal, "kspace": kspace, "sampled": sampled, "sensitivity": sensitivity}


def split_parts(values):
    half_width = values.shape[-1] // 2
    return (values[..., :half_width], values[..., half_width:])

def dft_block(length):
    index = jnp.arange(length, dtype=jnp.int32)
    angles = (index[:, None] * index[None, :] % length).astype(jnp.float32) * (2.0 * math.pi / length)
    norm_factor = 1.0 / math.sqrt(length)
    cosine = jnp.cos(angles) * norm_factor
    sine_part = -jnp.sin(angles) * norm_factor
    upper_rows = jnp.concatenate([cosine, sine_part], 1)
    lower_rows = jnp.concatenate([-sine_part, cosine], 1)
    return jnp.concatenate([upper_rows, lower_rows], 0).astype(jnp.bfloat16)

def coil_adjoint(image, measured, sampled_row, sensitivity, block):
    image_real, image_imag = split_parts(image.astype(jnp.float32))
    sens_real, sens_imag = split_parts(sensitivity.astype(jnp.float32))
    coil_real = sens_real * image_real[None] - sens_imag * image_imag[None]
    coil_imag = sens_real * image_imag[None] + sens_imag * image_real[None]
    coil_image = jnp.concatenate([coil_real, coil_imag], -1).astype(jnp.bfloat16)
    coil_count, row_count, full_width = coil_image.shape
    spectrum = jnp.dot(coil_image.reshape(coil_count * row_count, full_width), block, preferred_element_type=jnp.float32).reshape(coil_count, row_count, full_width)
    line_keep = jnp.concatenate([sampled_row, sampled_row]).astype(jnp.float32)
    misfit = (line_keep * (spectrum - measured.astype(jnp.float32))).astype(jnp.bfloat16)
    adjoint = jnp.dot(misfit.reshape(coil_count * row_count, full_width), block.T, preferred_element_type=jnp.float32).reshape(coil_count, row_count, full_width)
    back_real, back_imag = split_parts(adjoint)
    grad_real = lax.optimization_barrier(jnp.sum(sens_real * back_real + sens_imag * back_imag, axis=0))
    grad_imag = lax.optimization_barrier(jnp.sum(sens_real * back_imag - sens_imag * back_real, axis=0))
    return jnp.concatenate([grad_real, grad_imag], -1)

def reference(spatial, temporal, kspace, sampled, sensitivity):
    spat = spatial.astype(jnp.float32)
    temp = temporal.astype(jnp.float32)
    spat_real, spat_imag = split_parts(spat)
    temp_real, temp_imag = split_parts(temp)
    image_real = jnp.einsum('tr,xry->txy', temp_real, spat_real) - jnp.einsum('tr,xry->txy', temp_imag, spat_imag)
    image_imag = jnp.einsum('tr,xry->txy', temp_real, spat_imag) + jnp.einsum('tr,xry->txy', temp_imag, spat_real)
    image = jnp.concatenate([image_real, image_imag], -1).astype(jnp.bfloat16)
    block = dft_block(spatial.shape[2] // 2)
    grads = lax.map(lambda frame_item: coil_adjoint(frame_item[0], frame_item[1], frame_item[2], sensitivity, block), (image, kspace, sampled))
    grad_image = grads.astype(jnp.bfloat16).astype(jnp.float32)
    grad_real, grad_imag = split_parts(grad_image)
    spatial_real = jnp.einsum('tr,txy->xry', temp_real, grad_real) + jnp.einsum('tr,txy->xry', temp_imag, grad_imag)
    spatial_imag = jnp.einsum('tr,txy->xry', temp_real, grad_imag) - jnp.einsum('tr,txy->xry', temp_imag, grad_real)
    spatial_grad = jnp.concatenate([spatial_real, spatial_imag], -1)
    temporal_real = jnp.einsum('xry,txy->tr', spat_real, grad_real) + jnp.einsum('xry,txy->tr', spat_imag, grad_imag)
    temporal_imag = jnp.einsum('xry,txy->tr', spat_real, grad_imag) - jnp.einsum('xry,txy->tr', spat_imag, grad_real)
    temporal_grad = jnp.concatenate([temporal_real, temporal_imag], -1)
    return (spatial_grad, temporal_grad)
```

```python
import functools
import math

import jax
import jax.numpy as jnp
from jax import lax
from jax.experimental import pallas as pl
from jax.experimental.pallas import tpu as pltpu
from jax.sharding import PartitionSpec as P

F32 = jnp.float32
BF16 = jnp.bfloat16


def dft_block(length):
    index = jnp.arange(length, dtype=jnp.int32)
    angles = (index[:, None] * index[None, :] % length).astype(F32) * (2.0 * math.pi / length)
    norm_factor = 1.0 / math.sqrt(length)
    cosine = jnp.cos(angles) * norm_factor
    sine_part = -jnp.sin(angles) * norm_factor
    upper_rows = jnp.concatenate([cosine, sine_part], 1)
    lower_rows = jnp.concatenate([-sine_part, cosine], 1)
    return jnp.concatenate([upper_rows, lower_rows], 0).astype(BF16)


def dot(a, b):
    return jnp.dot(a, b, preferred_element_type=F32)


def dot_t(a, b):
    return lax.dot_general(a, b, (((1,), (1,)), ((), ())), preferred_element_type=F32)


def iota(shape, axis):
    return lax.broadcasted_iota(jnp.int32, shape, axis)


def spread(factors, total, rows, rank):
    groups, lanes = factors.shape
    per = total // groups
    height = 2 * total * rows
    frame = iota((height, groups), 0) // rows % total
    pick = jnp.where(frame // per == iota((height, groups), 1), 1.0, 0.0).astype(BF16)
    picked = dot(pick, factors)
    row = iota((height, lanes), 0)
    lane = iota((height, lanes), 1)
    mine = (lane // rank) == (row // rows % total % per) * 2 + row // (total * rows)
    return jnp.where(mine, picked, 0.0).astype(BF16)


def image_kernel(total, rows, rank, factors_ref, spatial_ref, image_ref):
    mid = spread(factors_ref[...], total, rows, rank)
    lanes = mid.shape[1]
    width = rows * rank
    tile = jnp.where(iota((lanes, width), 0) % rank == iota((lanes, width), 1) % rank, 1.0, 0.0)
    wide = dot(mid, tile.astype(BF16))
    height = wide.shape[0]
    same = iota((height, width), 0) % rows == iota((height, width), 1) // rank
    wide = jnp.where(same, wide, 0.0).astype(BF16)
    product = dot(wide, spatial_ref[...])
    half = height // 2
    mid_col = product.shape[1] // 2
    image_ref[:, :mid_col] = (product[:half, :mid_col] - product[half:, mid_col:]).astype(BF16)
    image_ref[:, mid_col:] = (product[:half, mid_col:] + product[half:, :mid_col]).astype(BF16)


def both_parts(grad):
    half = grad.shape[1] // 2
    turned = jnp.concatenate([grad[:, half:], -grad[:, :half]], 1)
    return jnp.concatenate([grad, turned], 0)


def spatial_kernel(total, rows, rank, factors_ref, grad_ref, out_ref):
    mid = spread(factors_ref[...], total, rows, rank)
    lanes = mid.shape[1]
    width = rows * rank
    tile = jnp.where(iota((width, lanes), 0) % rank == iota((width, lanes), 1) % rank, 1.0, 0.0)
    wide = dot_t(tile.astype(BF16), mid)
    height = mid.shape[0]
    same = iota((width, height), 1) % rows == iota((width, height), 0) // rank
    wide = jnp.where(same, wide, 0.0).astype(BF16)
    out_ref[...] = dot(wide, both_parts(grad_ref[...]))


def temporal_kernel(total, rows, rank, spatial_ref, grad_ref, out_ref):
    product = dot_t(both_parts(grad_ref[...]), spatial_ref[...])
    height, width = product.shape
    same = iota((height, width), 0) % rows == iota((height, width), 1) // rank
    product = jnp.where(same, product, 0.0)
    lanes = 128
    fold = product[:, :lanes]
    for start in range(lanes, width, lanes):
        fold = fold + product[:, start : start + lanes]
    if rows % 8 == 0:
        fold = jnp.sum(fold.reshape(2 * total, rows, lanes), axis=1)
    else:
        pick = iota((2 * total, height), 0) == iota((2 * total, height), 1) // rows
        fold = jnp.dot(
            jnp.where(pick, 1.0, 0.0), fold, precision=lax.Precision.HIGHEST, preferred_element_type=F32
        )
    shift = lanes // 2
    while shift >= rank:
        fold = fold + pltpu.roll(fold, shift, 1)
        shift //= 2
    lane = iota((total, lanes), 1)
    both = jnp.where(lane < rank, fold[:total], fold[total:])
    groups, copies, per, span = out_ref.shape
    for group in range(groups):
        for copy in range(copies):
            out_ref[group, copy] = both[group * per : (group + 1) * per, :span]


def conj_sum(adjoint, sens_r, sens_i):
    half = sens_r.shape[-1]
    back_r, back_i = adjoint[..., :half], adjoint[..., half:]
    return (
        jnp.sum(sens_r * back_r + sens_i * back_i, axis=0),
        jnp.sum(sens_r * back_i - sens_i * back_r, axis=0),
    )


def data_kernel(kspace_ref, sens_ref, back_ref, out_ref):
    frames, coils, rows, width = kspace_ref.shape
    half = width // 2
    sens = sens_ref[...].astype(F32)
    sens_r, sens_i = sens[..., :half], sens[..., half:]
    for t in range(frames):
        adjoint = dot(kspace_ref[t].reshape(coils * rows, width), back_ref[t])
        real, imag = conj_sum(adjoint.reshape(coils, rows, width), sens_r, sens_i)
        out_ref[t, :, :half] = real
        out_ref[t, :, half:] = imag


def normal_kernel(part_ref, image_ref, sens_ref, normal_ref, data_ref, out_ref):
    groups, frames, per, width = image_ref.shape
    coils, rows, _ = sens_ref.shape
    half = width // 2
    sens = sens_ref[...].astype(F32)
    sens_r, sens_i = sens[..., :half], sens[..., half:]
    for t in range(frames):
        image = image_ref[:, t].reshape(rows, width).astype(F32)
        image_r, image_i = image[:, :half], image[:, half:]
        coil_r = (sens_r * image_r - sens_i * image_i).astype(BF16)
        coil_i = (sens_r * image_i + sens_i * image_r).astype(BF16)
        coil = jnp.concatenate([coil_r, coil_i], -1).reshape(coils * rows, width)
        adjoint = dot(coil, normal_ref[t])
        real, imag = conj_sum(adjoint.reshape(coils, rows, width), sens_r, sens_i)
        out_ref[:, t, :, :half] = (real - data_ref[t, :, :half]).reshape(groups, per, half)
        out_ref[:, t, :, half:] = (imag - data_ref[t, :, half:]).reshape(groups, per, half)


def whole(shape):
    return pl.BlockSpec(shape, lambda *_: (0,) * len(shape))


def cost(flops, moved):
    return pl.CostEstimate(flops=int(flops), bytes_accessed=int(moved), transcendentals=0)


def data_term(kspace, sens, back, tile):
    frames, coils, rows, width = kspace.shape
    return pl.pallas_call(
        data_kernel,
        grid=(rows // tile,),
        in_specs=[
            pl.BlockSpec((frames, coils, tile, width), lambda i: (0, 0, i, 0)),
            pl.BlockSpec((coils, tile, width), lambda i: (0, i, 0)),
            whole(back.shape),
        ],
        out_specs=pl.BlockSpec((frames, tile, width), lambda i: (0, i, 0)),
        out_shape=jax.ShapeDtypeStruct((frames, rows, width), F32),
        cost_estimate=cost(2 * frames * coils * rows * width * width, 2 * kspace.size + 2 * sens.size),
        name="data_term",
    )(kspace, sens, back)


def normal_term(part, image, sens, normal, data, tile):
    groups, frames, per, width = image.shape
    coils = sens.shape[0]
    step = tile // per
    steps = groups // step
    return pl.pallas_call(
        normal_kernel,
        grid_spec=pltpu.PrefetchScalarGridSpec(
            num_scalar_prefetch=1,
            grid=(steps,),
            in_specs=[
                pl.BlockSpec((step, frames, per, width), lambda i, part_ref: (i, 0, 0, 0)),
                pl.BlockSpec((coils, tile, width), lambda i, part_ref: (0, part_ref[0] * steps + i, 0)),
                pl.BlockSpec(normal.shape, lambda i, part_ref: (0, 0, 0)),
                pl.BlockSpec((frames, tile, width), lambda i, part_ref: (0, part_ref[0] * steps + i, 0)),
            ],
            out_specs=pl.BlockSpec((step, frames, per, width), lambda i, part_ref: (i, 0, 0, 0)),
        ),
        out_shape=jax.ShapeDtypeStruct((groups, frames, per, width), F32),
        cost_estimate=cost(
            2 * frames * coils * groups * per * width * width, coils * groups * per * width * 2
        ),
        name="normal_term",
    )(part, image, sens, normal, data)


def on_device(frame_size, coil_size, spatial, temporal, kspace, sampled, sensitivity):
    rows, rank, width = spatial.shape
    per = temporal.shape[0]
    total = per * frame_size
    half_rows = rows * frame_size
    swap = [(i, (i + 1) % coil_size) for i in range(coil_size)]
    own = lax.axis_index("coil")
    other = (own + 1) % coil_size
    spatial2 = spatial.reshape(rows * rank, width)

    lanes = per * 2 * rank
    factors = lax.all_to_all(
        jnp.broadcast_to(temporal.reshape(1, lanes), (frame_size, lanes)), "frame", 0, 0, tiled=True
    )

    block = dft_block(width // 2)
    keep = jnp.concatenate([sampled, sampled], 1).astype(BF16)
    back = block.T[None] * keep[:, :, None]
    normal = jnp.einsum("ij,tjk->tik", block, back, preferred_element_type=F32).astype(BF16)
    data = data_term(kspace, sensitivity, back, 32)

    image = pl.pallas_call(
        functools.partial(image_kernel, total, rows, rank),
        out_shape=jax.ShapeDtypeStruct((total * rows, width), BF16),
        name="image_rows",
    )(factors, spatial2)
    image = lax.all_to_all(
        image.reshape(frame_size, per, rows, width), "frame", 0, 0, tiled=True
    )
    regroup = rows % 16 != 0
    if regroup:
        image = image.transpose(1, 0, 2, 3).reshape(per, half_rows // 16, 16, width).transpose(1, 0, 2, 3)
    image_other = lax.ppermute(image, "coil", swap)
    send = normal_term(other.reshape(1), image_other, sensitivity, normal, data, 32)
    received = lax.ppermute(send, "coil", swap)
    keep_own = normal_term(own.reshape(1), image, sensitivity, normal, data, 32)
    grad = (keep_own + received).astype(BF16)
    if regroup:
        grad = grad.transpose(1, 0, 2, 3).reshape(per, frame_size, rows, width).transpose(1, 0, 2, 3)
    grad = lax.all_to_all(grad, "frame", 0, 0, tiled=True).reshape(total * rows, width)

    partial = pl.pallas_call(
        functools.partial(temporal_kernel, total, rows, rank),
        out_shape=jax.ShapeDtypeStruct((frame_size, coil_size, per, 2 * rank), F32),
        name="temporal_rows",
    )(spatial2, grad)
    partial = partial.reshape(frame_size * coil_size, per, 2 * rank)
    partial = lax.all_to_all(partial, ("frame", "coil"), 0, 0, tiled=True)
    spatial_grad = pl.pallas_call(
        functools.partial(spatial_kernel, total, rows, rank),
        out_shape=jax.ShapeDtypeStruct((rows * rank, width), F32),
        name="spatial_rows",
    )(factors, grad)
    return (spatial_grad.reshape(rows, rank, width), jnp.sum(partial, axis=0))


def solution(mesh):
    placed = (
        P(("cuts", "coil", "frame"), None, None),
        P(("cuts", "frame"), None),
        P(("cuts", "frame"), "coil", None, None),
        P(("cuts", "frame"), None),
        P(("cuts", "coil"), None, None),
    )
    return jax.shard_map(
        functools.partial(on_device, mesh.shape["frame"], mesh.shape["coil"]),
        mesh=mesh,
        in_specs=placed,
        out_specs=(P(("cuts", "coil", "frame"), None, None), P(("cuts", "frame"), None)),
        check_vma=False,
    )
```

```python
import functools
import math

import jax
import jax.numpy as jnp
import numpy as np
from jax import lax
from jax.experimental import pallas as pl
from jax.experimental.pallas import tpu as pltpu
from jax.sharding import PartitionSpec as P

F32 = jnp.float32
BF16 = jnp.bfloat16


def dft_block(length):
    index = np.arange(length)
    angles = (index[:, None] * index[None, :] % length) * (2.0 * math.pi / length)
    cosine = np.cos(angles) / math.sqrt(length)
    sine_part = -np.sin(angles) / math.sqrt(length)
    block = np.block([[cosine, sine_part], [-sine_part, cosine]])
    return block.astype(np.float32).astype(BF16)


def dot(a, b):
    return jnp.dot(a, b, preferred_element_type=F32)


def dot_t(a, b):
    return lax.dot_general(a, b, (((1,), (1,)), ((), ())), preferred_element_type=F32)


def iota(shape, axis):
    return lax.broadcasted_iota(jnp.int32, shape, axis)


def spread(factors_ref, total, rows, rank):
    groups, per, lanes = factors_ref.shape
    height = 2 * total * rows
    frame = iota((height, groups), 0) // rows % total
    factors = factors_ref[...].astype(F32)
    picked = jnp.zeros((height, lanes), F32)
    for t in range(per):
        pick = jnp.where(frame == iota((height, groups), 1) * per + t, 1.0, 0.0).astype(BF16)
        picked = picked + dot(pick, factors[:, t].astype(BF16))
    mine = iota((height, lanes), 1) // rank == iota((height, lanes), 0) // (total * rows)
    return jnp.where(mine, picked, 0.0).astype(BF16)


def image_kernel(total, rows, rank, factors_ref, spatial_ref, image_ref):
    mid = spread(factors_ref, total, rows, rank)
    lanes = mid.shape[1]
    width = rows * rank
    tile = jnp.where(iota((lanes, width), 0) % rank == iota((lanes, width), 1) % rank, 1.0, 0.0)
    wide = dot(mid, tile.astype(BF16))
    height = wide.shape[0]
    same = iota((height, width), 0) % rows == iota((height, width), 1) // rank
    wide = jnp.where(same, wide, 0.0).astype(BF16)
    product = dot(wide, spatial_ref[...])
    half = height // 2
    mid_col = product.shape[1] // 2
    image_ref[:, :mid_col] = (product[:half, :mid_col] - product[half:, mid_col:]).astype(BF16)
    image_ref[:, mid_col:] = (product[:half, mid_col:] + product[half:, :mid_col]).astype(BF16)


def both_parts(grad):
    half = grad.shape[1] // 2
    turned = jnp.concatenate([grad[:, half:], -grad[:, :half]], 1)
    return jnp.concatenate([grad, turned], 0)


def spatial_kernel(total, rows, rank, factors_ref, grad_ref, out_ref):
    mid = spread(factors_ref, total, rows, rank)
    lanes = mid.shape[1]
    width = rows * rank
    tile = jnp.where(iota((width, lanes), 0) % rank == iota((width, lanes), 1) % rank, 1.0, 0.0)
    wide = dot_t(tile.astype(BF16), mid)
    height = mid.shape[0]
    same = iota((width, height), 1) % rows == iota((width, height), 0) // rank
    wide = jnp.where(same, wide, 0.0).astype(BF16)
    out_ref[...] = dot(wide, both_parts(grad_ref[...]))


def temporal_kernel(total, rows, rank, spatial_ref, grad_ref, out_ref):
    product = dot_t(both_parts(grad_ref[...]), spatial_ref[...])
    height, width = product.shape
    same = iota((height, width), 0) % rows == iota((height, width), 1) // rank
    product = jnp.where(same, product, 0.0)
    lanes = 128
    fold = product[:, :lanes]
    for start in range(lanes, width, lanes):
        fold = fold + product[:, start : start + lanes]
    if rows % 8 == 0:
        fold = jnp.sum(fold.reshape(2 * total, rows, lanes), axis=1)
    else:
        pick = iota((2 * total, height), 0) == iota((2 * total, height), 1) // rows
        fold = jnp.dot(
            jnp.where(pick, 1.0, 0.0), fold, precision=lax.Precision.HIGHEST, preferred_element_type=F32
        )
    shift = lanes // 2
    while shift >= rank:
        fold = fold + pltpu.roll(fold, shift, 1)
        shift //= 2
    lane = iota((total, lanes), 1)
    both = jnp.where(lane // rank % 2 == 0, fold[:total], fold[total:])
    groups, _, span = out_ref.shape
    per = span // (2 * rank)
    copies = groups * per // total
    place = iota((1, span), 1) // (2 * rank)
    for group in range(groups // copies):
        line = both[group * per : group * per + 1, :span]
        for t in range(1, per):
            line = jnp.where(place == t, both[group * per + t : group * per + t + 1, :span], line)
        for copy in range(copies):
            out_ref[group * copies + copy] = line


def sum_kernel(parts_ref, out_ref):
    line = jnp.sum(parts_ref[...], axis=0)
    per, span = out_ref.shape
    for t in range(per):
        out_ref[t : t + 1, :] = line[:, t * span : (t + 1) * span]


def conj_sum(adjoint, sens_r, sens_i):
    half = sens_r.shape[-1]
    back_r, back_i = adjoint[..., :half], adjoint[..., half:]
    return (
        jnp.sum(sens_r * back_r + sens_i * back_i, axis=0),
        jnp.sum(sens_r * back_i - sens_i * back_r, axis=0),
    )


def masked(block, sampled_ref, t):
    keep = sampled_ref[t : t + 1, :].astype(F32)
    return (block.astype(F32) * jnp.concatenate([keep, keep], 1)).astype(BF16)


def prepare_kernel(sampled_ref, block_ref, spatial_ref, normal_ref, staged_ref, sem):
    staging = pltpu.make_async_copy(spatial_ref, staged_ref, sem)
    staging.start()
    block = block_ref[...]
    for t in range(sampled_ref.shape[0]):
        normal_ref[t] = dot_t(masked(block, sampled_ref, t), block).astype(BF16)
    staging.wait()


def data_kernel(tile, ahead, sampled_ref, block_ref, kspace_ref, sens_ref, out_ref,
                block_held, back_held, kspace_held, sens_held, block_sem, kspace_sem, sens_sem):
    frames, coils, rows, width = kspace_ref.shape
    half = width // 2
    steps = rows // tile

    def fetch(step):
        slot = lax.rem(step, ahead + 1)
        place = pl.ds(step * tile, tile)
        return (
            pltpu.make_async_copy(kspace_ref.at[:, :, place], kspace_held.at[slot], kspace_sem.at[slot]),
            pltpu.make_async_copy(sens_ref.at[:, place], sens_held.at[slot], sens_sem.at[slot]),
        )

    def begin(step):
        for copy in fetch(step):
            copy.start()

    table = pltpu.make_async_copy(block_ref, block_held, block_sem)
    table.start()
    for step in range(min(ahead, steps)):
        begin(step)
    table.wait()
    block = block_held[...]
    for t in range(frames):
        back_held[t] = masked(block, sampled_ref, t).T

    @pl.loop(0, steps)
    def _(step):
        @pl.when(step + ahead < steps)
        def _():
            begin(step + ahead)

        for copy in fetch(step):
            copy.wait()
        place = pl.ds(step * tile, tile)
        slot = lax.rem(step, ahead + 1)
        sens = sens_held[slot].astype(F32)
        sens_r, sens_i = sens[..., :half], sens[..., half:]
        for t in range(frames):
            adjoint = dot(kspace_held[slot, t].reshape(coils * tile, width), back_held[t])
            real, imag = conj_sum(adjoint.reshape(coils, tile, width), sens_r, sens_i)
            out_ref[t, place, :half] = real
            out_ref[t, place, half:] = imag


def normal_kernel(tile, part_ref, image_ref, sens_ref, normal_ref, data_ref, out_ref, sens_held, sem):
    groups, frames, per, width = image_ref.shape
    coils = sens_ref.shape[0]
    half = width // 2
    step_groups = tile // per
    steps = groups // step_groups

    def spot(step):
        return pl.ds(pl.multiple_of(part_ref[0] * (groups * per) + step * tile, tile), tile)

    def fetch(step):
        return pltpu.make_async_copy(sens_ref.at[:, spot(step)], sens_held.at[step], sem.at[step])

    for step in range(steps):
        fetch(step).start()

    @pl.loop(0, steps)
    def _(step):
        place = spot(step)
        group = pl.ds(step * step_groups, step_groups)
        fetch(step).wait()
        sens = sens_held[step].astype(F32)
        sens_r, sens_i = sens[..., :half], sens[..., half:]
        for t in range(frames):
            image = image_ref[group, t].reshape(tile, width).astype(F32)
            image_r, image_i = image[:, :half], image[:, half:]
            coil_r = (sens_r * image_r - sens_i * image_i).astype(BF16)
            coil_i = (sens_r * image_i + sens_i * image_r).astype(BF16)
            coil = jnp.concatenate([coil_r, coil_i], -1).reshape(coils * tile, width)
            adjoint = dot(coil, normal_ref[t])
            real, imag = conj_sum(adjoint.reshape(coils, tile, width), sens_r, sens_i)
            shape = (step_groups, per, half)
            out_ref[group, t, :, :half] = (real - data_ref[t, place, :half]).reshape(shape)
            out_ref[group, t, :, half:] = (imag - data_ref[t, place, half:]).reshape(shape)


def cost(flops, moved):
    return pl.CostEstimate(flops=int(flops), bytes_accessed=int(moved), transcendentals=0)


VMEM = pl.BlockSpec(memory_space=pltpu.VMEM)
SMEM = pl.BlockSpec(memory_space=pltpu.SMEM)
HBM = pl.BlockSpec(memory_space=pltpu.HBM)
MIB = 1 << 20


def local(array):
    return pltpu.with_memory_space_constraint(array, pltpu.VMEM)


def remote(array):
    return pltpu.with_memory_space_constraint(array, pltpu.HBM)


def grant(mib):
    return pltpu.CompilerParams(vmem_limit_bytes=mib * MIB)


def prepare(sampled, block, spatial):
    frames = sampled.shape[0]
    return pl.pallas_call(
        prepare_kernel,
        in_specs=[VMEM, VMEM, HBM],
        out_specs=[VMEM, VMEM],
        out_shape=[pltpu.VMEM((frames, *block.shape), BF16), pltpu.VMEM(spatial.shape, BF16)],
        scratch_shapes=[pltpu.SemaphoreType.DMA],
        cost_estimate=cost(2 * frames * block.shape[0] ** 3, 4 * block.size),
        compiler_params=grant(12),
        name="prepare",
    )(sampled, block, remote(spatial))


def data_term(sampled, block, kspace, sens, tile, ahead):
    frames, coils, rows, width = kspace.shape
    return pl.pallas_call(
        functools.partial(data_kernel, tile, ahead),
        in_specs=[VMEM, HBM, HBM, HBM],
        out_specs=VMEM,
        out_shape=pltpu.VMEM((frames, rows, width), F32),
        scratch_shapes=[
            pltpu.VMEM((width, width), BF16),
            pltpu.VMEM((frames, width, width), BF16),
            pltpu.VMEM((ahead + 1, frames, coils, tile, width), BF16),
            pltpu.VMEM((ahead + 1, coils, tile, width), BF16),
            pltpu.SemaphoreType.DMA,
            pltpu.SemaphoreType.DMA((ahead + 1,)),
            pltpu.SemaphoreType.DMA((ahead + 1,)),
        ],
        cost_estimate=cost(2 * frames * coils * rows * width * width, 2 * kspace.size),
        compiler_params=grant(24),
        name="data_term",
    )(sampled, remote(block), remote(kspace), remote(sens))


def normal_term(part, image, sens, normal, data, tile):
    groups, frames, per, width = image.shape
    coils = sens.shape[0]
    steps = groups * per // tile
    return pl.pallas_call(
        functools.partial(normal_kernel, tile),
        in_specs=[SMEM, VMEM, HBM, VMEM, VMEM],
        out_specs=VMEM,
        out_shape=pltpu.VMEM((groups, frames, per, width), F32),
        scratch_shapes=[pltpu.VMEM((steps, coils, tile, width), BF16), pltpu.SemaphoreType.DMA((steps,))],
        cost_estimate=cost(
            2 * frames * coils * groups * per * width * width, coils * groups * per * width * 2
        ),
        compiler_params=grant(20),
        name="normal_term",
    )(part, image, remote(sens), normal, data)


def on_device(frame_size, coil_size, spatial, temporal, kspace, sampled, sensitivity):
    rows, rank, width = spatial.shape
    per = temporal.shape[0]
    total = per * frame_size
    half_rows = rows * frame_size
    swap = [(i, (i + 1) % coil_size) for i in range(coil_size)]
    own = lax.axis_index("coil")
    other = (own + 1) % coil_size
    spatial2 = spatial.reshape(rows * rank, width)

    factors = lax.all_to_all(
        jnp.broadcast_to(temporal[None], (frame_size, per, 2 * rank)), "frame", 0, 0, tiled=True
    )
    block = jnp.asarray(dft_block(width // 2))
    normal, spatial2 = prepare(sampled, block, spatial2)

    image = pl.pallas_call(
        functools.partial(image_kernel, total, rows, rank),
        in_specs=[VMEM, VMEM],
        out_specs=VMEM,
        out_shape=pltpu.VMEM((total * rows, width), BF16),
        compiler_params=grant(12),
        name="image_rows",
    )(local(factors), spatial2)
    image, sampled = lax.optimization_barrier((image, sampled))
    image = lax.all_to_all(image.reshape(frame_size, per, rows, width), "frame", 0, 0, tiled=True)
    data = data_term(sampled, block, kspace, sensitivity, 32, 3)
    image, data = lax.optimization_barrier((image, data))
    regroup = rows % 16 != 0
    if regroup:
        image = image.transpose(1, 0, 2, 3).reshape(per, half_rows // 16, 16, width).transpose(1, 0, 2, 3)
    image_other = lax.ppermute(image, "coil", swap)
    send = normal_term(other.reshape(1), local(image_other), sensitivity, normal, data, 32)
    received = lax.ppermute(send, "coil", swap)
    keep_own = normal_term(own.reshape(1), local(image), sensitivity, normal, data, 32)
    grad = (keep_own + received).astype(BF16)
    if regroup:
        grad = grad.transpose(1, 0, 2, 3).reshape(per, frame_size, rows, width).transpose(1, 0, 2, 3)
    grad = lax.all_to_all(grad, "frame", 0, 0, tiled=True).reshape(total * rows, width)
    grad = local(grad)

    partial = pl.pallas_call(
        functools.partial(temporal_kernel, total, rows, rank),
        in_specs=[VMEM, VMEM],
        out_specs=VMEM,
        out_shape=pltpu.VMEM((frame_size * coil_size, 1, per * 2 * rank), F32),
        compiler_params=grant(12),
        name="temporal_rows",
    )(spatial2, grad)
    partial = lax.all_to_all(partial, ("frame", "coil"), 0, 0, tiled=True)
    spatial_grad = pl.pallas_call(
        functools.partial(spatial_kernel, total, rows, rank),
        in_specs=[VMEM, VMEM],
        out_specs=VMEM,
        out_shape=jax.ShapeDtypeStruct((rows * rank, width), F32),
        compiler_params=grant(12),
        name="spatial_rows",
    )(local(factors), grad)
    temporal_grad = pl.pallas_call(
        sum_kernel,
        in_specs=[VMEM],
        out_specs=VMEM,
        out_shape=jax.ShapeDtypeStruct((per, 2 * rank), F32),
        compiler_params=grant(2),
        name="temporal_sum",
    )(partial)
    return (spatial_grad.reshape(rows, rank, width), temporal_grad)


def solution(mesh):
    placed = (
        P(("cuts", "coil", "frame"), None, None),
        P(("cuts", "frame"), None),
        P(("cuts", "frame"), "coil", None, None),
        P(("cuts", "frame"), None),
        P(("cuts", "coil"), None, None),
    )
    return jax.shard_map(
        functools.partial(on_device, mesh.shape["frame"], mesh.shape["coil"]),
        mesh=mesh,
        in_specs=placed,
        out_specs=(P(("cuts", "coil", "frame"), None, None), P(("cuts", "frame"), None)),
        check_vma=False,
    )
```

```python
import functools
import math

import jax
import jax.numpy as jnp
import numpy as np
from jax import lax
from jax.experimental import pallas as pl
from jax.experimental.pallas import tpu as pltpu
from jax.sharding import PartitionSpec as P

F32 = jnp.float32
BF16 = jnp.bfloat16


def dft_block(length):
    index = np.arange(length)
    angles = (index[:, None] * index[None, :] % length) * (2.0 * math.pi / length)
    cosine = np.cos(angles) / math.sqrt(length)
    sine_part = -np.sin(angles) / math.sqrt(length)
    block = np.block([[cosine, sine_part], [-sine_part, cosine]])
    return block.astype(np.float32).astype(BF16)


def dot(a, b):
    return jnp.dot(a, b, preferred_element_type=F32)


def dot_t(a, b):
    return lax.dot_general(a, b, (((1,), (1,)), ((), ())), preferred_element_type=F32)


def iota(shape, axis):
    return lax.broadcasted_iota(jnp.int32, shape, axis)


def spread(factors_ref, total, rows, rank):
    groups, per, lanes = factors_ref.shape
    height = 2 * total * rows
    frame = iota((height, groups), 0) // rows % total
    factors = factors_ref[...].astype(F32)
    picked = jnp.zeros((height, lanes), F32)
    for t in range(per):
        pick = jnp.where(frame == iota((height, groups), 1) * per + t, 1.0, 0.0).astype(BF16)
        picked = picked + dot(pick, factors[:, t].astype(BF16))
    mine = iota((height, lanes), 1) // rank == iota((height, lanes), 0) // (total * rows)
    return jnp.where(mine, picked, 0.0).astype(BF16)


def image_kernel(total, rows, rank, factors_ref, spatial_ref, image_ref, staged_ref, sem):
    staging = pltpu.make_async_copy(spatial_ref, staged_ref, sem)
    staging.start()
    mid = spread(factors_ref, total, rows, rank)
    lanes = mid.shape[1]
    width = rows * rank
    tile = jnp.where(iota((lanes, width), 0) % rank == iota((lanes, width), 1) % rank, 1.0, 0.0)
    wide = dot(mid, tile.astype(BF16))
    height = wide.shape[0]
    same = iota((height, width), 0) % rows == iota((height, width), 1) // rank
    wide = jnp.where(same, wide, 0.0).astype(BF16)
    staging.wait()
    product = dot(wide, staged_ref[...])
    half = height // 2
    mid_col = product.shape[1] // 2
    image_ref[:, :mid_col] = (product[:half, :mid_col] - product[half:, mid_col:]).astype(BF16)
    image_ref[:, mid_col:] = (product[:half, mid_col:] + product[half:, :mid_col]).astype(BF16)


def both_parts(grad):
    half = grad.shape[1] // 2
    turned = jnp.concatenate([grad[:, half:], -grad[:, :half]], 1)
    return jnp.concatenate([grad, turned], 0)


def spatial_kernel(total, rows, rank, factors_ref, grad_ref, out_ref):
    mid = spread(factors_ref, total, rows, rank)
    lanes = mid.shape[1]
    width = rows * rank
    tile = jnp.where(iota((width, lanes), 0) % rank == iota((width, lanes), 1) % rank, 1.0, 0.0)
    wide = dot_t(tile.astype(BF16), mid)
    height = mid.shape[0]
    same = iota((width, height), 1) % rows == iota((width, height), 0) // rank
    wide = jnp.where(same, wide, 0.0).astype(BF16)
    out_ref[...] = dot(wide, both_parts(grad_ref[...]))


def temporal_kernel(total, rows, rank, spatial_ref, grad_ref, out_ref):
    product = dot_t(both_parts(grad_ref[...]), spatial_ref[...])
    height, width = product.shape
    same = iota((height, width), 0) % rows == iota((height, width), 1) // rank
    product = jnp.where(same, product, 0.0)
    lanes = 128
    fold = product[:, :lanes]
    for start in range(lanes, width, lanes):
        fold = fold + product[:, start : start + lanes]
    if rows % 8 == 0:
        fold = jnp.sum(fold.reshape(2 * total, rows, lanes), axis=1)
    else:
        pick = iota((2 * total, height), 0) == iota((2 * total, height), 1) // rows
        fold = jnp.dot(
            jnp.where(pick, 1.0, 0.0), fold, precision=lax.Precision.HIGHEST, preferred_element_type=F32
        )
    shift = lanes // 2
    while shift >= rank:
        fold = fold + pltpu.roll(fold, shift, 1)
        shift //= 2
    lane = iota((total, lanes), 1)
    both = jnp.where(lane // rank % 2 == 0, fold[:total], fold[total:])
    groups, _, span = out_ref.shape
    per = span // (2 * rank)
    copies = groups * per // total
    place = iota((1, span), 1) // (2 * rank)
    for group in range(groups // copies):
        line = both[group * per : group * per + 1, :span]
        for t in range(1, per):
            line = jnp.where(place == t, both[group * per + t : group * per + t + 1, :span], line)
        for copy in range(copies):
            out_ref[group * copies + copy] = line


def sum_kernel(parts_ref, out_ref):
    line = jnp.sum(parts_ref[...], axis=0)
    per, span = out_ref.shape
    for t in range(per):
        out_ref[t : t + 1, :] = line[:, t * span : (t + 1) * span]


def conj_sum(adjoint, sens_r, sens_i):
    half = sens_r.shape[-1]
    back_r, back_i = adjoint[..., :half], adjoint[..., half:]
    return (
        jnp.sum(sens_r * back_r + sens_i * back_i, axis=0),
        jnp.sum(sens_r * back_i - sens_i * back_r, axis=0),
    )


def masked(block, sampled_ref, t):
    keep = sampled_ref[t : t + 1, :].astype(F32)
    return (block.astype(F32) * jnp.concatenate([keep, keep], 1)).astype(BF16)


def prepare_kernel(sampled_ref, block_ref, normal_ref):
    block = block_ref[...]
    for t in range(sampled_ref.shape[0]):
        normal_ref[t] = dot_t(masked(block, sampled_ref, t), block).astype(BF16)


def data_kernel(tile, ahead, sampled_ref, block_ref, kspace_ref, sens_ref, out_ref, block_held, sampled_held,
                back_held, kspace_held, sens_held, sampled_sem, block_sem, kspace_sem, sens_sem):
    frames, coils, rows, width = kspace_ref.shape
    half = width // 2
    steps = rows // tile

    def fetch_sens(step):
        slot = lax.rem(step, ahead + 1)
        place = pl.ds(step * tile, tile)
        return pltpu.make_async_copy(sens_ref.at[:, place], sens_held.at[slot], sens_sem.at[slot])

    def fetch_kspace(step, t):
        slot = lax.rem(step, ahead + 1)
        place = pl.ds(step * tile, tile)
        return pltpu.make_async_copy(
            kspace_ref.at[t, :, place], kspace_held.at[slot, t], kspace_sem.at[slot, t]
        )

    def begin(step):
        fetch_sens(step).start()
        for t in range(frames):
            fetch_kspace(step, t).start()

    table = pltpu.make_async_copy(block_ref, block_held, block_sem)
    mask = pltpu.make_async_copy(sampled_ref, sampled_held, sampled_sem)
    table.start()
    mask.start()
    for step in range(min(ahead, steps)):
        begin(step)
    table.wait()
    mask.wait()
    block = block_held[...]
    for t in range(frames):
        back_held[t] = masked(block, sampled_held, t).T

    @pl.loop(0, steps)
    def _(step):
        @pl.when(step + ahead < steps)
        def _():
            begin(step + ahead)

        fetch_sens(step).wait()
        place = pl.ds(step * tile, tile)
        slot = lax.rem(step, ahead + 1)
        sens = sens_held[slot].astype(F32)
        sens_r, sens_i = sens[..., :half], sens[..., half:]
        for t in range(frames):
            fetch_kspace(step, t).wait()
            adjoint = dot(kspace_held[slot, t].reshape(coils * tile, width), back_held[t])
            real, imag = conj_sum(adjoint.reshape(coils, tile, width), sens_r, sens_i)
            out_ref[t, place, :half] = real
            out_ref[t, place, half:] = imag


def normal_kernel(tile, part_ref, image_ref, sens_ref, normal_ref, data_ref, out_ref, sens_held, sem):
    groups, frames, per, width = image_ref.shape
    coils = sens_ref.shape[0]
    half = width // 2
    step_groups = tile // per
    steps = groups // step_groups

    def spot(step):
        return pl.ds(pl.multiple_of(part_ref[0] * (groups * per) + step * tile, tile), tile)

    def fetch(step):
        return pltpu.make_async_copy(sens_ref.at[:, spot(step)], sens_held.at[step], sem.at[step])

    for step in range(steps):
        fetch(step).start()

    @pl.loop(0, steps)
    def _(step):
        place = spot(step)
        group = pl.ds(step * step_groups, step_groups)
        fetch(step).wait()
        sens = sens_held[step].astype(F32)
        sens_r, sens_i = sens[..., :half], sens[..., half:]
        for t in range(frames):
            image = image_ref[group, t].reshape(tile, width).astype(F32)
            image_r, image_i = image[:, :half], image[:, half:]
            coil_r = (sens_r * image_r - sens_i * image_i).astype(BF16)
            coil_i = (sens_r * image_i + sens_i * image_r).astype(BF16)
            coil = jnp.concatenate([coil_r, coil_i], -1).reshape(coils * tile, width)
            adjoint = dot(coil, normal_ref[t])
            real, imag = conj_sum(adjoint.reshape(coils, tile, width), sens_r, sens_i)
            shape = (step_groups, per, half)
            out_ref[group, t, :, :half] = (real - data_ref[t, place, :half]).reshape(shape)
            out_ref[group, t, :, half:] = (imag - data_ref[t, place, half:]).reshape(shape)


def cost(flops, moved):
    return pl.CostEstimate(flops=int(flops), bytes_accessed=int(moved), transcendentals=0)


VMEM = pl.BlockSpec(memory_space=pltpu.VMEM)
SMEM = pl.BlockSpec(memory_space=pltpu.SMEM)
HBM = pl.BlockSpec(memory_space=pltpu.HBM)
MIB = 1 << 20


def local(array):
    return pltpu.with_memory_space_constraint(array, pltpu.VMEM)


def remote(array):
    return pltpu.with_memory_space_constraint(array, pltpu.HBM)


def grant(mib):
    return pltpu.CompilerParams(vmem_limit_bytes=mib * MIB)


def prepare(sampled, block):
    frames = sampled.shape[0]
    return pl.pallas_call(
        prepare_kernel,
        in_specs=[VMEM, VMEM],
        out_specs=VMEM,
        out_shape=pltpu.VMEM((frames, *block.shape), BF16),
        cost_estimate=cost(2 * frames * block.shape[0] ** 3, 4 * block.size),
        compiler_params=grant(12),
        name="prepare",
    )(sampled, block)


def data_term(sampled, block, kspace, sens, tile, ahead):
    frames, coils, rows, width = kspace.shape
    return pl.pallas_call(
        functools.partial(data_kernel, tile, ahead),
        in_specs=[HBM, HBM, HBM, HBM],
        out_specs=[VMEM, VMEM],
        out_shape=[pltpu.VMEM((frames, rows, width), F32), pltpu.VMEM(block.shape, BF16)],
        scratch_shapes=[
            pltpu.VMEM(sampled.shape, jnp.int32),
            pltpu.VMEM((frames, width, width), BF16),
            pltpu.VMEM((ahead + 1, frames, coils, tile, width), BF16),
            pltpu.VMEM((ahead + 1, coils, tile, width), BF16),
            pltpu.SemaphoreType.DMA,
            pltpu.SemaphoreType.DMA,
            pltpu.SemaphoreType.DMA((ahead + 1, frames)),
            pltpu.SemaphoreType.DMA((ahead + 1,)),
        ],
        cost_estimate=cost(2 * frames * coils * rows * width * width, 2 * kspace.size),
        compiler_params=grant(32),
        name="data_term",
    )(remote(sampled), remote(block), remote(kspace), remote(sens))


def normal_term(part, image, sens, normal, data, tile):
    groups, frames, per, width = image.shape
    coils = sens.shape[0]
    steps = groups * per // tile
    return pl.pallas_call(
        functools.partial(normal_kernel, tile),
        in_specs=[SMEM, VMEM, HBM, VMEM, VMEM],
        out_specs=VMEM,
        out_shape=pltpu.VMEM((groups, frames, per, width), F32),
        scratch_shapes=[pltpu.VMEM((steps, coils, tile, width), BF16), pltpu.SemaphoreType.DMA((steps,))],
        cost_estimate=cost(
            2 * frames * coils * groups * per * width * width, coils * groups * per * width * 2
        ),
        compiler_params=grant(20),
        name="normal_term",
    )(part, image, remote(sens), normal, data)


def on_device(frame_size, coil_size, spatial, temporal, kspace, sampled, sensitivity):
    rows, rank, width = spatial.shape
    per = temporal.shape[0]
    total = per * frame_size
    half_rows = rows * frame_size
    swap = [(i, (i + 1) % coil_size) for i in range(coil_size)]
    own = lax.axis_index("coil")
    other = (own + 1) % coil_size
    spatial2 = spatial.reshape(rows * rank, width)

    factors = lax.all_to_all(
        jnp.broadcast_to(temporal[None], (frame_size, per, 2 * rank)), "frame", 0, 0, tiled=True
    )
    block = jnp.asarray(dft_block(width // 2))
    image, spatial2 = pl.pallas_call(
        functools.partial(image_kernel, total, rows, rank),
        in_specs=[VMEM, HBM],
        out_specs=[VMEM, VMEM],
        out_shape=[pltpu.VMEM((total * rows, width), BF16), pltpu.VMEM(spatial2.shape, BF16)],
        scratch_shapes=[pltpu.SemaphoreType.DMA],
        compiler_params=grant(12),
        name="image_rows",
    )(local(factors), remote(spatial2))
    image, sampled = lax.optimization_barrier((image, sampled))
    image = lax.all_to_all(image.reshape(frame_size, per, rows, width), "frame", 0, 0, tiled=True)
    data, block = data_term(sampled, block, kspace, sensitivity, 64, 2)
    image, data, block = lax.optimization_barrier((image, data, block))
    normal = prepare(sampled, block)
    regroup = rows % 16 != 0
    if regroup:
        image = image.transpose(1, 0, 2, 3).reshape(per, half_rows // 16, 16, width).transpose(1, 0, 2, 3)
    image_other = lax.ppermute(image, "coil", swap)
    send = normal_term(other.reshape(1), local(image_other), sensitivity, normal, data, 32)
    received = lax.ppermute(send, "coil", swap)
    keep_own = normal_term(own.reshape(1), local(image), sensitivity, normal, data, 32)
    grad = (keep_own + received).astype(BF16)
    if regroup:
        grad = grad.transpose(1, 0, 2, 3).reshape(per, frame_size, rows, width).transpose(1, 0, 2, 3)
    grad = lax.all_to_all(grad, "frame", 0, 0, tiled=True).reshape(total * rows, width)
    grad = local(grad)

    partial = pl.pallas_call(
        functools.partial(temporal_kernel, total, rows, rank),
        in_specs=[VMEM, VMEM],
        out_specs=VMEM,
        out_shape=pltpu.VMEM((frame_size * coil_size, 1, per * 2 * rank), F32),
        compiler_params=grant(12),
        name="temporal_rows",
    )(spatial2, grad)
    partial = lax.all_to_all(partial, ("frame", "coil"), 0, 0, tiled=True)
    spatial_grad = pl.pallas_call(
        functools.partial(spatial_kernel, total, rows, rank),
        in_specs=[VMEM, VMEM],
        out_specs=VMEM,
        out_shape=jax.ShapeDtypeStruct((rows * rank, width), F32),
        compiler_params=grant(12),
        name="spatial_rows",
    )(local(factors), grad)
    temporal_grad = pl.pallas_call(
        sum_kernel,
        in_specs=[VMEM],
        out_specs=VMEM,
        out_shape=jax.ShapeDtypeStruct((per, 2 * rank), F32),
        compiler_params=grant(2),
        name="temporal_sum",
    )(partial)
    return (spatial_grad.reshape(rows, rank, width), temporal_grad)


def solution(mesh):
    placed = (
        P(("cuts", "coil", "frame"), None, None),
        P(("cuts", "frame"), None),
        P(("cuts", "frame"), "coil", None, None),
        P(("cuts", "frame"), None),
        P(("cuts", "coil"), None, None),
    )
    return jax.shard_map(
        functools.partial(on_device, mesh.shape["frame"], mesh.shape["coil"]),
        mesh=mesh,
        in_specs=placed,
        out_specs=(P(("cuts", "coil", "frame"), None, None), P(("cuts", "frame"), None)),
        check_vma=False,
    )
```

```python
import functools
import math

import jax
import jax.numpy as jnp
import numpy as np
from jax import lax
from jax.experimental import pallas as pl
from jax.experimental.pallas import tpu as pltpu
from jax.sharding import PartitionSpec as P

F32 = jnp.float32
BF16 = jnp.bfloat16


def dft_half(length):
    index = np.arange(length)
    angles = (index[:, None] * index[None, :] % length) * (2.0 * math.pi / length)
    cosine = np.cos(angles) / math.sqrt(length)
    sine_part = -np.sin(angles) / math.sqrt(length)
    return np.concatenate([cosine, sine_part], 1).astype(np.float32).astype(BF16)


def dot(a, b):
    return jnp.dot(a, b, preferred_element_type=F32)


def dot_t(a, b):
    return lax.dot_general(a, b, (((1,), (1,)), ((), ())), preferred_element_type=F32)


def iota(shape, axis):
    return lax.broadcasted_iota(jnp.int32, shape, axis)


def spread(factors_ref, total, rows, rank):
    groups, per, lanes = factors_ref.shape
    height = 2 * total * rows
    frame = iota((height, groups), 0) // rows % total
    factors = factors_ref[...].astype(F32)
    picked = jnp.zeros((height, lanes), F32)
    for t in range(per):
        pick = jnp.where(frame == iota((height, groups), 1) * per + t, 1.0, 0.0).astype(BF16)
        picked = picked + dot(pick, factors[:, t].astype(BF16))
    mine = iota((height, lanes), 1) // rank == iota((height, lanes), 0) // (total * rows)
    return jnp.where(mine, picked, 0.0).astype(BF16)


def image_kernel(total, rows, rank, factors_ref, spatial_ref, image_ref):
    mid = spread(factors_ref, total, rows, rank)
    lanes = mid.shape[1]
    width = rows * rank
    tile = jnp.where(iota((lanes, width), 0) % rank == iota((lanes, width), 1) % rank, 1.0, 0.0)
    wide = dot(mid, tile.astype(BF16))
    height = wide.shape[0]
    same = iota((height, width), 0) % rows == iota((height, width), 1) // rank
    wide = jnp.where(same, wide, 0.0).astype(BF16)
    product = dot(wide, spatial_ref[...])
    half = height // 2
    mid_col = product.shape[1] // 2
    image_ref[:, :mid_col] = (product[:half, :mid_col] - product[half:, mid_col:]).astype(BF16)
    image_ref[:, mid_col:] = (product[:half, mid_col:] + product[half:, :mid_col]).astype(BF16)


def both_parts(grad):
    half = grad.shape[1] // 2
    turned = jnp.concatenate([grad[:, half:], -grad[:, :half]], 1)
    return jnp.concatenate([grad, turned], 0)


def spatial_kernel(total, rows, rank, factors_ref, grad_ref, out_ref):
    mid = spread(factors_ref, total, rows, rank)
    lanes = mid.shape[1]
    width = rows * rank
    tile = jnp.where(iota((width, lanes), 0) % rank == iota((width, lanes), 1) % rank, 1.0, 0.0)
    wide = dot_t(tile.astype(BF16), mid)
    height = mid.shape[0]
    same = iota((width, height), 1) % rows == iota((width, height), 0) // rank
    wide = jnp.where(same, wide, 0.0).astype(BF16)
    out_ref[...] = dot(wide, both_parts(grad_ref[...]))


def temporal_kernel(total, rows, rank, spatial_ref, grad_ref, out_ref):
    product = dot_t(both_parts(grad_ref[...]), spatial_ref[...])
    height, width = product.shape
    same = iota((height, width), 0) % rows == iota((height, width), 1) // rank
    product = jnp.where(same, product, 0.0)
    lanes = 128
    fold = product[:, :lanes]
    for start in range(lanes, width, lanes):
        fold = fold + product[:, start : start + lanes]
    if rows % 8 == 0:
        fold = jnp.sum(fold.reshape(2 * total, rows, lanes), axis=1)
    else:
        pick = iota((2 * total, height), 0) == iota((2 * total, height), 1) // rows
        fold = jnp.dot(
            jnp.where(pick, 1.0, 0.0), fold, precision=lax.Precision.HIGHEST, preferred_element_type=F32
        )
    shift = lanes // 2
    while shift >= rank:
        fold = fold + pltpu.roll(fold, shift, 1)
        shift //= 2
    lane = iota((total, lanes), 1)
    both = jnp.where(lane // rank % 2 == 0, fold[:total], fold[total:])
    groups, _, span = out_ref.shape
    per = span // (2 * rank)
    copies = groups * per // total
    place = iota((1, span), 1) // (2 * rank)
    for group in range(groups // copies):
        line = both[group * per : group * per + 1, :span]
        for t in range(1, per):
            line = jnp.where(place == t, both[group * per + t : group * per + t + 1, :span], line)
        for copy in range(copies):
            out_ref[group * copies + copy] = line


def sum_kernel(parts_ref, out_ref):
    line = jnp.sum(parts_ref[...], axis=0)
    per, span = out_ref.shape
    for t in range(per):
        out_ref[t : t + 1, :] = line[:, t * span : (t + 1) * span]


def conj_sum(adjoint, sens_r, sens_i):
    half = sens_r.shape[-1]
    back_r, back_i = adjoint[..., :half], adjoint[..., half:]
    return (
        jnp.sum(sens_r * back_r + sens_i * back_i, axis=0),
        jnp.sum(sens_r * back_i - sens_i * back_r, axis=0),
    )


def stage_kernel(sampled_ref, block_ref, spatial_ref, mask_out, block_out, spatial_out, sems):
    copies = [
        pltpu.make_async_copy(sampled_ref, mask_out, sems.at[0]),
        pltpu.make_async_copy(block_ref, block_out, sems.at[1]),
        pltpu.make_async_copy(spatial_ref, spatial_out, sems.at[2]),
    ]
    for copy in copies:
        copy.start()
    for copy in copies:
        copy.wait()


def data_kernel(tile, ahead, starts_ref, mask_ref, block_ref, kspace_ref, sens_ref,
                first_ref, normal_ref, other_ref, own_ref,
                back, kspace_held, sens_held, own_held, kspace_sem, sens_sem, first_sem, own_sem):
    frames, coils, rows, width = kspace_ref.shape
    groups, _, per, _ = own_ref.shape
    half = width // 2
    steps = rows // tile
    part_steps = steps // 2
    step_groups = tile // per

    def fetch(step):
        slot = lax.rem(step, ahead + 1)
        start = starts_ref[1 - step // part_steps] + lax.rem(step, part_steps) * tile
        place = pl.ds(pl.multiple_of(start, tile), tile)
        copies = [pltpu.make_async_copy(sens_ref.at[:, place], sens_held.at[slot], sens_sem.at[slot])]
        for t in range(frames):
            source = kspace_ref.at[t, :, place]
            copies.append(
                pltpu.make_async_copy(source, kspace_held.at[slot, t], kspace_sem.at[slot, t])
            )
        return copies

    for step in range(min(ahead, steps)):
        for copy in fetch(step):
            copy.start()
    start = pl.ds(pl.multiple_of(starts_ref[0], tile), tile)
    staging = pltpu.make_async_copy(sens_ref.at[:, start], first_ref, first_sem)
    staging.start()
    block = block_ref[...]
    for t in range(frames):
        keep = mask_ref[t : t + 1, :].astype(F32)
        cosine = (block[:, :half].astype(F32) * keep).astype(BF16).T
        sine_part = (block[:, half:].astype(F32) * keep).astype(BF16).T
        back[t, :half, :half] = cosine
        back[t, :half, half:] = -sine_part
        back[t, half:, :half] = sine_part
        back[t, half:, half:] = cosine
        normal_ref[t] = dot(block, back[t]).astype(BF16)

    def part(first_step, store):
        @pl.loop(0, part_steps)
        def _(k):
            step = first_step + k

            @pl.when(step + ahead < steps)
            def _():
                for copy in fetch(step + ahead):
                    copy.start()

            copies = fetch(step)
            copies[0].wait()
            slot = lax.rem(step, ahead + 1)
            sens = sens_held[slot].astype(F32)
            sens_r, sens_i = sens[..., :half], sens[..., half:]
            for t in range(frames):
                copies[1 + t].wait()
                adjoint = dot(kspace_held[slot, t].reshape(coils * tile, width), back[t])
                store(k, t, *conj_sum(adjoint.reshape(coils, tile, width), sens_r, sens_i))

    def store_own(k, t, real, imag):
        group = pl.ds(k * step_groups, step_groups)
        own_held[group, t, :, :half] = real.reshape(step_groups, per, half)
        own_held[group, t, :, half:] = imag.reshape(step_groups, per, half)

    def store_other(k, t, real, imag):
        place = pl.ds(k * tile, tile)
        other_ref[t, place, :half] = real
        other_ref[t, place, half:] = imag

    part(0, store_own)
    leaving = pltpu.make_async_copy(own_held, own_ref, own_sem)
    leaving.start()
    part(part_steps, store_other)
    staging.wait()
    leaving.wait()


def normal_kernel(other, starts_ref, image_ref, first_ref, sens_ref, normal_ref, *rest):
    if other:
        data_ref, out_ref, next_ref, table, sens_held, sem, next_sem = rest
    else:
        out_ref, table, sens_held, sem = rest
    groups, frames, per, width = image_ref.shape
    coils, tile, _ = first_ref.shape
    half = width // 2
    step_groups = tile // per
    steps = groups // step_groups

    def spot(step, which):
        return pl.ds(pl.multiple_of(starts_ref[which] + step * tile, tile), tile)

    def fetch(step):
        source = sens_ref.at[:, spot(step, 0 if other else 1)]
        return pltpu.make_async_copy(source, sens_held.at[step - 1], sem.at[step - 1])

    for step in range(1, steps):
        fetch(step).start()
    if other:
        staging = pltpu.make_async_copy(sens_ref.at[:, spot(0, 1)], next_ref, next_sem)
        staging.start()
    for t in range(frames):
        table[t, :half] = normal_ref[t]
        table[t, half:, :half] = -normal_ref[t, :, half:]
        table[t, half:, half:] = normal_ref[t, :, :half]

    def work(step, sens):
        place = pl.ds(step * tile, tile)
        group = pl.ds(step * step_groups, step_groups)
        sens = sens.astype(F32)
        sens_r, sens_i = sens[..., :half], sens[..., half:]
        for t in range(frames):
            image = image_ref[group, t].reshape(tile, width).astype(F32)
            image_r, image_i = image[:, :half], image[:, half:]
            coil_r = (sens_r * image_r - sens_i * image_i).astype(BF16)
            coil_i = (sens_r * image_i + sens_i * image_r).astype(BF16)
            coil = jnp.concatenate([coil_r, coil_i], -1).reshape(coils * tile, width)
            adjoint = dot(coil, table[t])
            real, imag = conj_sum(adjoint.reshape(coils, tile, width), sens_r, sens_i)
            if other:
                real = real - data_ref[t, place, :half]
                imag = imag - data_ref[t, place, half:]
            out_ref[group, t, :, :half] = real.reshape(step_groups, per, half)
            out_ref[group, t, :, half:] = imag.reshape(step_groups, per, half)

    work(0, first_ref[...])

    @pl.loop(1, steps)
    def _(step):
        fetch(step).wait()
        work(step, sens_held[step - 1])

    if other:
        staging.wait()


def cost(flops, moved):
    return pl.CostEstimate(flops=int(flops), bytes_accessed=int(moved), transcendentals=0)


VMEM = pl.BlockSpec(memory_space=pltpu.VMEM)
SMEM = pl.BlockSpec(memory_space=pltpu.SMEM)
HBM = pl.BlockSpec(memory_space=pltpu.HBM)
MIB = 1 << 20


def local(array):
    return pltpu.with_memory_space_constraint(array, pltpu.VMEM)


def remote(array):
    return pltpu.with_memory_space_constraint(array, pltpu.HBM)


def grant(mib):
    return pltpu.CompilerParams(vmem_limit_bytes=mib * MIB)


def stage(sampled, block, spatial):
    return pl.pallas_call(
        stage_kernel,
        in_specs=[HBM, HBM, HBM],
        out_specs=[VMEM, VMEM, VMEM],
        out_shape=[
            pltpu.VMEM(sampled.shape, jnp.int32),
            pltpu.VMEM(block.shape, BF16),
            pltpu.VMEM(spatial.shape, BF16),
        ],
        scratch_shapes=[pltpu.SemaphoreType.DMA((3,))],
        cost_estimate=cost(0, 8 * block.size),
        compiler_params=grant(12),
        name="stage",
    )(remote(sampled), remote(block), remote(spatial))


def data_term(starts, mask, block, kspace, sens, per, tile, ahead):
    frames, coils, rows, width = kspace.shape
    own = (rows // 2 // per, frames, per, width)
    return pl.pallas_call(
        functools.partial(data_kernel, tile, ahead),
        in_specs=[SMEM, VMEM, VMEM, HBM, HBM],
        out_specs=[VMEM, VMEM, VMEM, HBM],
        out_shape=[
            pltpu.VMEM((coils, tile, width), BF16),
            pltpu.VMEM((frames, width // 2, width), BF16),
            pltpu.VMEM((frames, rows // 2, width), F32),
            pltpu.HBM(own, F32),
        ],
        scratch_shapes=[
            pltpu.VMEM((frames, width, width), BF16),
            pltpu.VMEM((ahead + 1, frames, coils, tile, width), BF16),
            pltpu.VMEM((ahead + 1, coils, tile, width), BF16),
            pltpu.VMEM(own, F32),
            pltpu.SemaphoreType.DMA((ahead + 1, frames)),
            pltpu.SemaphoreType.DMA((ahead + 1,)),
            pltpu.SemaphoreType.DMA,
            pltpu.SemaphoreType.DMA,
        ],
        cost_estimate=cost(2 * frames * coils * rows * width * width, 2 * kspace.size),
        compiler_params=grant(32),
        name="data_term",
    )(starts, mask, block, remote(kspace), remote(sens))


def normal_term(starts, image, first, sens, normal, data=None):
    groups, frames, per, width = image.shape
    coils, tile, _ = first.shape
    steps = groups * per // tile
    other = data is not None
    outs = [pltpu.VMEM((groups, frames, per, width), F32)]
    scratch = [
        pltpu.VMEM((frames, width, width), BF16),
        pltpu.VMEM((steps - 1, coils, tile, width), BF16),
        pltpu.SemaphoreType.DMA((steps - 1,)),
    ]
    if other:
        outs.append(pltpu.VMEM(first.shape, BF16))
        scratch.append(pltpu.SemaphoreType.DMA)
    return pl.pallas_call(
        functools.partial(normal_kernel, other),
        in_specs=[SMEM, VMEM, VMEM, HBM, VMEM] + [VMEM] * other,
        out_specs=[VMEM] * len(outs),
        out_shape=outs,
        scratch_shapes=scratch,
        cost_estimate=cost(
            2 * frames * coils * groups * per * width * width, coils * groups * per * width * 2
        ),
        compiler_params=grant(20),
        name="normal_other" if other else "normal_own",
    )(starts, image, first, remote(sens), normal, *([data] if other else []))


def on_device(frame_size, coil_size, spatial, temporal, kspace, sampled, sensitivity):
    rows, rank, width = spatial.shape
    per = temporal.shape[0]
    total = per * frame_size
    half_rows = rows * frame_size
    swap = [(i, (i + 1) % coil_size) for i in range(coil_size)]
    own = lax.axis_index("coil") * half_rows
    starts = jnp.stack([(own + half_rows) % (coil_size * half_rows), own])
    spatial2 = spatial.reshape(rows * rank, width)

    factors = lax.all_to_all(
        jnp.broadcast_to(temporal[None], (frame_size, per, 2 * rank)), "frame", 0, 0, tiled=True
    )
    mask, block, near = stage(sampled, jnp.asarray(dft_half(width // 2)), spatial2)
    image = pl.pallas_call(
        functools.partial(image_kernel, total, rows, rank),
        in_specs=[VMEM, VMEM],
        out_specs=VMEM,
        out_shape=pltpu.VMEM((total * rows, width), BF16),
        compiler_params=grant(12),
        name="image_rows",
    )(local(factors), near)
    image, kspace = lax.optimization_barrier((image, kspace))
    image = lax.all_to_all(image.reshape(frame_size, per, rows, width), "frame", 0, 0, tiled=True)
    regroup = rows % 16 != 0
    first, normal, data_other, data_own = data_term(
        starts, mask, block, kspace, sensitivity, 16 if regroup else rows, 32, 3
    )
    image, normal = lax.optimization_barrier((image, normal))
    if regroup:
        image = image.transpose(1, 0, 2, 3).reshape(per, half_rows // 16, 16, width).transpose(1, 0, 2, 3)
    image_other = lax.ppermute(image, "coil", swap)
    send, first = normal_term(starts, local(image_other), first, sensitivity, normal, data_other)
    received = lax.ppermute(send, "coil", swap)
    (keep_own,) = normal_term(starts, local(image), first, sensitivity, normal)
    grad = (keep_own + received - data_own).astype(BF16)
    if regroup:
        grad = grad.transpose(1, 0, 2, 3).reshape(per, frame_size, rows, width).transpose(1, 0, 2, 3)
    grad = lax.all_to_all(grad, "frame", 0, 0, tiled=True).reshape(total * rows, width)
    grad = local(grad)

    partial = pl.pallas_call(
        functools.partial(temporal_kernel, total, rows, rank),
        in_specs=[VMEM, VMEM],
        out_specs=VMEM,
        out_shape=pltpu.VMEM((frame_size * coil_size, 1, per * 2 * rank), F32),
        compiler_params=grant(12),
        name="temporal_rows",
    )(local(spatial2), grad)
    partial = lax.all_to_all(partial, ("frame", "coil"), 0, 0, tiled=True)
    spatial_grad = pl.pallas_call(
        functools.partial(spatial_kernel, total, rows, rank),
        in_specs=[VMEM, VMEM],
        out_specs=VMEM,
        out_shape=jax.ShapeDtypeStruct((rows * rank, width), F32),
        compiler_params=grant(12),
        name="spatial_rows",
    )(local(factors), grad)
    temporal_grad = pl.pallas_call(
        sum_kernel,
        in_specs=[VMEM],
        out_specs=VMEM,
        out_shape=jax.ShapeDtypeStruct((per, 2 * rank), F32),
        compiler_params=grant(2),
        name="temporal_sum",
    )(partial)
    return (spatial_grad.reshape(rows, rank, width), temporal_grad)


def solution(mesh):
    placed = (
        P(("cuts", "coil", "frame"), None, None),
        P(("cuts", "frame"), None),
        P(("cuts", "frame"), "coil", None, None),
        P(("cuts", "frame"), None),
        P(("cuts", "coil"), None, None),
    )
    return jax.shard_map(
        functools.partial(on_device, mesh.shape["frame"], mesh.shape["coil"]),
        mesh=mesh,
        in_specs=placed,
        out_specs=(P(("cuts", "coil", "frame"), None, None), P(("cuts", "frame"), None)),
        check_vma=False,
    )
```

```python
import functools
import math

import jax
import jax.numpy as jnp
import numpy as np
from jax import lax
from jax.experimental import pallas as pl
from jax.experimental.pallas import tpu as pltpu
from jax.sharding import PartitionSpec as P

F32 = jnp.float32
BF16 = jnp.bfloat16


def dft_half(length):
    index = np.arange(length)
    angles = (index[:, None] * index[None, :] % length) * (2.0 * math.pi / length)
    cosine = np.cos(angles) / math.sqrt(length)
    sine_part = -np.sin(angles) / math.sqrt(length)
    return np.concatenate([cosine, sine_part], 1).astype(np.float32).astype(BF16)


def dot(a, b):
    return jnp.dot(a, b, preferred_element_type=F32)


def dot_t(a, b):
    return lax.dot_general(a, b, (((1,), (1,)), ((), ())), preferred_element_type=F32)


def iota(shape, axis):
    return lax.broadcasted_iota(jnp.int32, shape, axis)


def spread(factors_ref, total, rows, rank):
    groups, per, lanes = factors_ref.shape
    height = 2 * total * rows
    frame = iota((height, groups), 0) // rows % total
    factors = factors_ref[...].astype(F32)
    picked = jnp.zeros((height, lanes), F32)
    for t in range(per):
        pick = jnp.where(frame == iota((height, groups), 1) * per + t, 1.0, 0.0).astype(BF16)
        picked = picked + dot(pick, factors[:, t].astype(BF16))
    mine = iota((height, lanes), 1) // rank == iota((height, lanes), 0) // (total * rows)
    return jnp.where(mine, picked, 0.0).astype(BF16)


def image_kernel(total, rows, rank, factors_ref, spatial_ref, image_ref):
    mid = spread(factors_ref, total, rows, rank)
    lanes = mid.shape[1]
    width = rows * rank
    tile = jnp.where(iota((lanes, width), 0) % rank == iota((lanes, width), 1) % rank, 1.0, 0.0)
    wide = dot(mid, tile.astype(BF16))
    height = wide.shape[0]
    same = iota((height, width), 0) % rows == iota((height, width), 1) // rank
    wide = jnp.where(same, wide, 0.0).astype(BF16)
    product = dot(wide, spatial_ref[...])
    half = height // 2
    mid_col = product.shape[1] // 2
    image_ref[:, :mid_col] = (product[:half, :mid_col] - product[half:, mid_col:]).astype(BF16)
    image_ref[:, mid_col:] = (product[:half, mid_col:] + product[half:, :mid_col]).astype(BF16)


def both_parts(grad):
    half = grad.shape[1] // 2
    turned = jnp.concatenate([grad[:, half:], -grad[:, :half]], 1)
    return jnp.concatenate([grad, turned], 0)


def spatial_kernel(total, rows, rank, factors_ref, grad_ref, out_ref):
    mid = spread(factors_ref, total, rows, rank)
    lanes = mid.shape[1]
    width = rows * rank
    tile = jnp.where(iota((width, lanes), 0) % rank == iota((width, lanes), 1) % rank, 1.0, 0.0)
    wide = dot_t(tile.astype(BF16), mid)
    height = mid.shape[0]
    same = iota((width, height), 1) % rows == iota((width, height), 0) // rank
    wide = jnp.where(same, wide, 0.0).astype(BF16)
    out_ref[...] = dot(wide, both_parts(grad_ref[...]))


def temporal_kernel(total, rows, rank, spatial_ref, grad_ref, out_ref):
    product = dot_t(both_parts(grad_ref[...]), spatial_ref[...])
    height, width = product.shape
    same = iota((height, width), 0) % rows == iota((height, width), 1) // rank
    product = jnp.where(same, product, 0.0)
    lanes = 128
    fold = product[:, :lanes]
    for start in range(lanes, width, lanes):
        fold = fold + product[:, start : start + lanes]
    if rows % 8 == 0:
        fold = jnp.sum(fold.reshape(2 * total, rows, lanes), axis=1)
    else:
        pick = iota((2 * total, height), 0) == iota((2 * total, height), 1) // rows
        fold = jnp.dot(
            jnp.where(pick, 1.0, 0.0), fold, precision=lax.Precision.HIGHEST, preferred_element_type=F32
        )
    shift = lanes // 2
    while shift >= rank:
        fold = fold + pltpu.roll(fold, shift, 1)
        shift //= 2
    lane = iota((total, lanes), 1)
    both = jnp.where(lane // rank % 2 == 0, fold[:total], fold[total:])
    groups, _, span = out_ref.shape
    per = span // (2 * rank)
    copies = groups * per // total
    place = iota((1, span), 1) // (2 * rank)
    for group in range(groups // copies):
        line = both[group * per : group * per + 1, :span]
        for t in range(1, per):
            line = jnp.where(place == t, both[group * per + t : group * per + t + 1, :span], line)
        for copy in range(copies):
            out_ref[group * copies + copy] = line


def sum_kernel(parts_ref, out_ref):
    line = jnp.sum(parts_ref[...], axis=0)
    per, span = out_ref.shape
    for t in range(per):
        out_ref[t : t + 1, :] = line[:, t * span : (t + 1) * span]


def conj_sum(adjoint, sens_r, sens_i):
    half = sens_r.shape[-1]
    back_r, back_i = adjoint[..., :half], adjoint[..., half:]
    return (
        jnp.sum(sens_r * back_r + sens_i * back_i, axis=0),
        jnp.sum(sens_r * back_i - sens_i * back_r, axis=0),
    )


def stage_kernel(starts_ref, sampled_ref, block_ref, spatial_ref, sens_ref, kspace_ref,
                 mask_out, block_out, spatial_out, sens_out, kspace_out, sems):
    tile = sens_out.shape[1]
    start = pl.ds(pl.multiple_of(starts_ref[0], tile), tile)
    copies = [
        pltpu.make_async_copy(spatial_ref, spatial_out, sems.at[0]),
        pltpu.make_async_copy(sampled_ref, mask_out, sems.at[1]),
        pltpu.make_async_copy(block_ref, block_out, sems.at[2]),
        pltpu.make_async_copy(sens_ref.at[:, start], sens_out, sems.at[3]),
        pltpu.make_async_copy(kspace_ref.at[:, :, start], kspace_out, sems.at[4]),
    ]
    for copy in copies:
        copy.start()
    for copy in copies:
        copy.wait()


def data_plan(rows, tile):
    own = [(1, 0, tile)]
    own += [(1, at, min(2 * tile, rows - at)) for at in range(tile, rows, 2 * tile)]
    other = [(0, tile, tile)] if rows > tile else []
    other += [(0, at, min(2 * tile, rows - at)) for at in range(2 * tile, rows, 2 * tile)]
    return [(0, 0, tile)] + own + other


def data_kernel(plan, starts_ref, mask_ref, block_ref, first_ref, kspace_first_ref, kspace_ref, sens_ref,
                normal_ref, other_ref, own_ref, back, own_held, own_sem, *held):
    frames, coils, rows, width = kspace_ref.shape
    groups, _, per, _ = own_ref.shape
    half = width // 2
    pieces = [held[4 * k : 4 * k + 4] for k in range(len(plan) - 1)]

    def fetch(step):
        part, at, size = plan[step]
        kspace_held, sens_held, kspace_sem, sens_sem = pieces[step - 1]
        place = pl.ds(pl.multiple_of(starts_ref[part] + at, plan[0][2]), size)
        copies = [pltpu.make_async_copy(sens_ref.at[:, place], sens_held, sens_sem)]
        for t in range(frames):
            copies.append(
                pltpu.make_async_copy(kspace_ref.at[t, :, place], kspace_held.at[t], kspace_sem.at[t])
            )
        return copies

    def begin(step):
        if step < len(plan):
            for copy in fetch(step):
                copy.start()

    begin(1)
    block = block_ref[...]
    for t in range(frames):
        keep = mask_ref[t : t + 1, :].astype(F32)
        cosine = (block[:, :half].astype(F32) * keep).astype(BF16).T
        sine_part = (block[:, half:].astype(F32) * keep).astype(BF16).T
        back[t, :half, :half] = cosine
        back[t, :half, half:] = -sine_part
        back[t, half:, :half] = sine_part
        back[t, half:, half:] = cosine
        normal_ref[t] = dot(block, back[t]).astype(BF16)
    begin(2)
    own_left = sum(part == 1 for part, _, _ in plan)
    leaving = pltpu.make_async_copy(own_held, own_ref, own_sem)
    for step, (part, at, size) in enumerate(plan):
        if step:
            begin(step + 2)
            copies = fetch(step)
            copies[0].wait()
            kspace_held, sens_held = pieces[step - 1][:2]
        else:
            kspace_held, sens_held = kspace_first_ref, first_ref
        sens = sens_held[...].astype(F32)
        sens_r, sens_i = sens[..., :half], sens[..., half:]
        for t in range(frames):
            if step:
                copies[1 + t].wait()
            adjoint = dot(kspace_held[t].reshape(coils * size, width), back[t])
            real, imag = conj_sum(adjoint.reshape(coils, size, width), sens_r, sens_i)
            if part:
                group = slice(at // per, (at + size) // per)
                own_held[group, t, :, :half] = real.reshape(size // per, per, half)
                own_held[group, t, :, half:] = imag.reshape(size // per, per, half)
            else:
                other_ref[t, at : at + size, :half] = real
                other_ref[t, at : at + size, half:] = imag
        own_left -= part
        if part and own_left == 0:
            leaving.start()
    leaving.wait()


def normal_kernel(other, starts_ref, image_ref, first_ref, sens_ref, normal_ref, *rest):
    if other:
        data_ref, out_ref, next_ref, table, sens_held, sem, next_sem = rest
    else:
        out_ref, table, sens_held, sem = rest
    groups, frames, per, width = image_ref.shape
    coils, tile, _ = first_ref.shape
    half = width // 2
    step_groups = tile // per
    steps = groups // step_groups

    def spot(step, which):
        return pl.ds(pl.multiple_of(starts_ref[which] + step * tile, tile), tile)

    def fetch(step):
        source = sens_ref.at[:, spot(step, 0 if other else 1)]
        return pltpu.make_async_copy(source, sens_held.at[step - 1], sem.at[step - 1])

    for step in range(1, steps):
        fetch(step).start()
    if other:
        staging = pltpu.make_async_copy(sens_ref.at[:, spot(0, 1)], next_ref, next_sem)
        staging.start()
    for t in range(frames):
        table[t, :half] = normal_ref[t]
        table[t, half:, :half] = -normal_ref[t, :, half:]
        table[t, half:, half:] = normal_ref[t, :, :half]

    def work(step, sens):
        place = pl.ds(step * tile, tile)
        group = pl.ds(step * step_groups, step_groups)
        sens = sens.astype(F32)
        sens_r, sens_i = sens[..., :half], sens[..., half:]
        for t in range(frames):
            image = image_ref[group, t].reshape(tile, width).astype(F32)
            image_r, image_i = image[:, :half], image[:, half:]
            coil_r = (sens_r * image_r - sens_i * image_i).astype(BF16)
            coil_i = (sens_r * image_i + sens_i * image_r).astype(BF16)
            coil = jnp.concatenate([coil_r, coil_i], -1).reshape(coils * tile, width)
            adjoint = dot(coil, table[t])
            real, imag = conj_sum(adjoint.reshape(coils, tile, width), sens_r, sens_i)
            if other:
                real = real - data_ref[t, place, :half]
                imag = imag - data_ref[t, place, half:]
            out_ref[group, t, :, :half] = real.reshape(step_groups, per, half)
            out_ref[group, t, :, half:] = imag.reshape(step_groups, per, half)

    work(0, first_ref[...])

    @pl.loop(1, steps)
    def _(step):
        fetch(step).wait()
        work(step, sens_held[step - 1])

    if other:
        staging.wait()


def cost(flops, moved):
    return pl.CostEstimate(flops=int(flops), bytes_accessed=int(moved), transcendentals=0)


VMEM = pl.BlockSpec(memory_space=pltpu.VMEM)
SMEM = pl.BlockSpec(memory_space=pltpu.SMEM)
HBM = pl.BlockSpec(memory_space=pltpu.HBM)
MIB = 1 << 20


def local(array):
    return pltpu.with_memory_space_constraint(array, pltpu.VMEM)


def remote(array):
    return pltpu.with_memory_space_constraint(array, pltpu.HBM)


def grant(mib):
    return pltpu.CompilerParams(vmem_limit_bytes=mib * MIB)


def stage(starts, sampled, block, spatial, sens, kspace, tile):
    frames, coils, _, width = kspace.shape
    return pl.pallas_call(
        stage_kernel,
        in_specs=[SMEM] + [HBM] * 5,
        out_specs=[VMEM] * 5,
        out_shape=[
            pltpu.VMEM(sampled.shape, jnp.int32),
            pltpu.VMEM(block.shape, BF16),
            pltpu.VMEM(spatial.shape, BF16),
            pltpu.VMEM((coils, tile, width), BF16),
            pltpu.VMEM((frames, coils, tile, width), BF16),
        ],
        scratch_shapes=[pltpu.SemaphoreType.DMA((5,))],
        cost_estimate=cost(0, 8 * block.size),
        compiler_params=grant(12),
        name="stage",
    )(starts, remote(sampled), remote(block), remote(spatial), remote(sens), remote(kspace))


def data_term(starts, mask, block, first, kspace_first, kspace, sens, per):
    frames, coils, rows, width = kspace.shape
    own = (rows // 2 // per, frames, per, width)
    plan = data_plan(rows // 2, first.shape[1])
    scratch = [pltpu.VMEM((frames, width, width), BF16), pltpu.VMEM(own, F32), pltpu.SemaphoreType.DMA]
    for _, _, size in plan[1:]:
        scratch += [
            pltpu.VMEM((frames, coils, size, width), BF16),
            pltpu.VMEM((coils, size, width), BF16),
            pltpu.SemaphoreType.DMA((frames,)),
            pltpu.SemaphoreType.DMA,
        ]
    return pl.pallas_call(
        functools.partial(data_kernel, plan),
        in_specs=[SMEM] + [VMEM] * 4 + [HBM] * 2,
        out_specs=[VMEM, VMEM, HBM],
        out_shape=[
            pltpu.VMEM((frames, width // 2, width), BF16),
            pltpu.VMEM((frames, rows // 2, width), F32),
            pltpu.HBM(own, F32),
        ],
        scratch_shapes=scratch,
        cost_estimate=cost(2 * frames * coils * rows * width * width, 2 * kspace.size),
        compiler_params=grant(36),
        name="data_term",
    )(starts, mask, block, first, kspace_first, remote(kspace), remote(sens))


def normal_term(starts, image, first, sens, normal, data=None):
    groups, frames, per, width = image.shape
    coils, tile, _ = first.shape
    steps = groups * per // tile
    other = data is not None
    outs = [pltpu.VMEM((groups, frames, per, width), F32)]
    scratch = [
        pltpu.VMEM((frames, width, width), BF16),
        pltpu.VMEM((steps - 1, coils, tile, width), BF16),
        pltpu.SemaphoreType.DMA((steps - 1,)),
    ]
    if other:
        outs.append(pltpu.VMEM(first.shape, BF16))
        scratch.append(pltpu.SemaphoreType.DMA)
    return pl.pallas_call(
        functools.partial(normal_kernel, other),
        in_specs=[SMEM, VMEM, VMEM, HBM, VMEM] + [VMEM] * other,
        out_specs=[VMEM] * len(outs),
        out_shape=outs,
        scratch_shapes=scratch,
        cost_estimate=cost(
            2 * frames * coils * groups * per * width * width, coils * groups * per * width * 2
        ),
        compiler_params=grant(20),
        name="normal_other" if other else "normal_own",
    )(starts, image, first, remote(sens), normal, *([data] if other else []))


def on_device(frame_size, coil_size, spatial, temporal, kspace, sampled, sensitivity):
    rows, rank, width = spatial.shape
    per = temporal.shape[0]
    total = per * frame_size
    half_rows = rows * frame_size
    swap = [(i, (i + 1) % coil_size) for i in range(coil_size)]
    own = lax.axis_index("coil") * half_rows
    starts = jnp.stack([(own + half_rows) % (coil_size * half_rows), own])
    spatial2 = spatial.reshape(rows * rank, width)

    factors = lax.all_to_all(
        jnp.broadcast_to(temporal[None], (frame_size, per, 2 * rank)), "frame", 0, 0, tiled=True
    )
    mask, block, near, first, kspace_first = stage(
        starts, sampled, jnp.asarray(dft_half(width // 2)), spatial2, sensitivity, kspace, 32
    )
    image = pl.pallas_call(
        functools.partial(image_kernel, total, rows, rank),
        in_specs=[VMEM, VMEM],
        out_specs=VMEM,
        out_shape=pltpu.VMEM((total * rows, width), BF16),
        compiler_params=grant(12),
        name="image_rows",
    )(local(factors), near)
    image, kspace = lax.optimization_barrier((image, kspace))
    image = lax.all_to_all(image.reshape(frame_size, per, rows, width), "frame", 0, 0, tiled=True)
    regroup = rows % 16 != 0
    normal, data_other, data_own = data_term(
        starts, mask, block, first, kspace_first, kspace, sensitivity, 16 if regroup else rows
    )
    image, normal = lax.optimization_barrier((image, normal))
    if regroup:
        image = image.transpose(1, 0, 2, 3).reshape(per, half_rows // 16, 16, width).transpose(1, 0, 2, 3)
    image_other = lax.ppermute(image, "coil", swap)
    send, first = normal_term(starts, local(image_other), first, sensitivity, normal, data_other)
    received = lax.ppermute(send, "coil", swap)
    (keep_own,) = normal_term(starts, local(image), first, sensitivity, normal)
    grad = (keep_own + received - data_own).astype(BF16)
    if regroup:
        grad = grad.transpose(1, 0, 2, 3).reshape(per, frame_size, rows, width).transpose(1, 0, 2, 3)
    grad = lax.all_to_all(grad, "frame", 0, 0, tiled=True).reshape(total * rows, width)
    grad = local(grad)

    partial = pl.pallas_call(
        functools.partial(temporal_kernel, total, rows, rank),
        in_specs=[VMEM, VMEM],
        out_specs=VMEM,
        out_shape=pltpu.VMEM((frame_size * coil_size, 1, per * 2 * rank), F32),
        compiler_params=grant(12),
        name="temporal_rows",
    )(local(spatial2), grad)
    partial = lax.all_to_all(partial, ("frame", "coil"), 0, 0, tiled=True)
    spatial_grad = pl.pallas_call(
        functools.partial(spatial_kernel, total, rows, rank),
        in_specs=[VMEM, VMEM],
        out_specs=VMEM,
        out_shape=jax.ShapeDtypeStruct((rows * rank, width), F32),
        compiler_params=grant(12),
        name="spatial_rows",
    )(local(factors), grad)
    temporal_grad = pl.pallas_call(
        sum_kernel,
        in_specs=[VMEM],
        out_specs=VMEM,
        out_shape=jax.ShapeDtypeStruct((per, 2 * rank), F32),
        compiler_params=grant(2),
        name="temporal_sum",
    )(partial)
    return (spatial_grad.reshape(rows, rank, width), temporal_grad)


def solution(mesh):
    placed = (
        P(("cuts", "coil", "frame"), None, None),
        P(("cuts", "frame"), None),
        P(("cuts", "frame"), "coil", None, None),
        P(("cuts", "frame"), None),
        P(("cuts", "coil"), None, None),
    )
    return jax.shard_map(
        functools.partial(on_device, mesh.shape["frame"], mesh.shape["coil"]),
        mesh=mesh,
        in_specs=placed,
        out_specs=(P(("cuts", "coil", "frame"), None, None), P(("cuts", "frame"), None)),
        check_vma=False,
    )
```

```python
import functools
import math

import jax
import jax.numpy as jnp
import numpy as np
from jax import lax
from jax.experimental import pallas as pl
from jax.experimental.pallas import tpu as pltpu
from jax.sharding import PartitionSpec as P

F32 = jnp.float32
BF16 = jnp.bfloat16


def dft_half(length):
    index = np.arange(length)
    angles = (index[:, None] * index[None, :] % length) * (2.0 * math.pi / length)
    cosine = np.cos(angles) / math.sqrt(length)
    sine_part = -np.sin(angles) / math.sqrt(length)
    return np.concatenate([cosine, sine_part], 1).astype(np.float32).astype(BF16)


def dot(a, b):
    return jnp.dot(a, b, preferred_element_type=F32)


def dot_t(a, b):
    return lax.dot_general(a, b, (((1,), (1,)), ((), ())), preferred_element_type=F32)


def iota(shape, axis):
    return lax.broadcasted_iota(jnp.int32, shape, axis)


def spread(factors_ref, total, rows, rank):
    groups, per, lanes = factors_ref.shape
    height = 2 * total * rows
    frame = iota((height, groups), 0) // rows % total
    factors = factors_ref[...].astype(F32)
    picked = jnp.zeros((height, lanes), F32)
    for t in range(per):
        pick = jnp.where(frame == iota((height, groups), 1) * per + t, 1.0, 0.0).astype(BF16)
        picked = picked + dot(pick, factors[:, t].astype(BF16))
    mine = iota((height, lanes), 1) // rank == iota((height, lanes), 0) // (total * rows)
    return jnp.where(mine, picked, 0.0).astype(BF16)


def image_kernel(total, rows, rank, factors_ref, spatial_ref, image_ref):
    mid = spread(factors_ref, total, rows, rank)
    lanes = mid.shape[1]
    width = rows * rank
    tile = jnp.where(iota((lanes, width), 0) % rank == iota((lanes, width), 1) % rank, 1.0, 0.0)
    wide = dot(mid, tile.astype(BF16))
    height = wide.shape[0]
    same = iota((height, width), 0) % rows == iota((height, width), 1) // rank
    wide = jnp.where(same, wide, 0.0).astype(BF16)
    product = dot(wide, spatial_ref[...])
    half = height // 2
    mid_col = product.shape[1] // 2
    image_ref[:, :mid_col] = (product[:half, :mid_col] - product[half:, mid_col:]).astype(BF16)
    image_ref[:, mid_col:] = (product[:half, mid_col:] + product[half:, :mid_col]).astype(BF16)


def both_parts(grad):
    half = grad.shape[1] // 2
    turned = jnp.concatenate([grad[:, half:], -grad[:, :half]], 1)
    return jnp.concatenate([grad, turned], 0)


def spatial_kernel(total, rows, rank, factors_ref, grad_ref, out_ref):
    mid = spread(factors_ref, total, rows, rank)
    lanes = mid.shape[1]
    width = rows * rank
    tile = jnp.where(iota((width, lanes), 0) % rank == iota((width, lanes), 1) % rank, 1.0, 0.0)
    wide = dot_t(tile.astype(BF16), mid)
    height = mid.shape[0]
    same = iota((width, height), 1) % rows == iota((width, height), 0) // rank
    wide = jnp.where(same, wide, 0.0).astype(BF16)
    out_ref[...] = dot(wide, both_parts(grad_ref[...]))


def temporal_kernel(total, rows, rank, spatial_ref, grad_ref, out_ref):
    product = dot_t(both_parts(grad_ref[...]), spatial_ref[...])
    height, width = product.shape
    same = iota((height, width), 0) % rows == iota((height, width), 1) // rank
    product = jnp.where(same, product, 0.0)
    lanes = 128
    fold = product[:, :lanes]
    for start in range(lanes, width, lanes):
        fold = fold + product[:, start : start + lanes]
    if rows % 8 == 0:
        fold = jnp.sum(fold.reshape(2 * total, rows, lanes), axis=1)
    else:
        pick = iota((2 * total, height), 0) == iota((2 * total, height), 1) // rows
        fold = jnp.dot(
            jnp.where(pick, 1.0, 0.0), fold, precision=lax.Precision.HIGHEST, preferred_element_type=F32
        )
    shift = lanes // 2
    while shift >= rank:
        fold = fold + pltpu.roll(fold, shift, 1)
        shift //= 2
    lane = iota((total, lanes), 1)
    both = jnp.where(lane // rank % 2 == 0, fold[:total], fold[total:])
    groups, _, span = out_ref.shape
    per = span // (2 * rank)
    copies = groups * per // total
    place = iota((1, span), 1) // (2 * rank)
    for group in range(groups // copies):
        line = both[group * per : group * per + 1, :span]
        for t in range(1, per):
            line = jnp.where(place == t, both[group * per + t : group * per + t + 1, :span], line)
        for copy in range(copies):
            out_ref[group * copies + copy] = line


def sum_kernel(parts_ref, out_ref):
    line = jnp.sum(parts_ref[...], axis=0)
    per, span = out_ref.shape
    for t in range(per):
        out_ref[t : t + 1, :] = line[:, t * span : (t + 1) * span]


def conj_sum(adjoint, sens_r, sens_i):
    half = sens_r.shape[-1]
    back_r, back_i = adjoint[..., :half], adjoint[..., half:]
    return (
        jnp.sum(sens_r * back_r + sens_i * back_i, axis=0),
        jnp.sum(sens_r * back_i - sens_i * back_r, axis=0),
    )


def stage_kernel(starts_ref, sampled_ref, block_ref, spatial_ref, sens_ref, kspace_ref,
                 mask_out, block_out, spatial_out, sens_out, kspace_out, sems):
    start = pl.multiple_of(starts_ref[0], sens_out.shape[1])
    copies = [
        pltpu.make_async_copy(spatial_ref, spatial_out, sems.at[0]),
        pltpu.make_async_copy(sampled_ref, mask_out, sems.at[1]),
        pltpu.make_async_copy(block_ref, block_out, sems.at[2]),
        pltpu.make_async_copy(sens_ref.at[:, pl.ds(start, sens_out.shape[1])], sens_out, sems.at[3]),
        pltpu.make_async_copy(kspace_ref.at[0, :, pl.ds(start, kspace_out.shape[1])], kspace_out, sems.at[4]),
    ]
    for copy in copies:
        copy.start()
    for copy in copies:
        copy.wait()


def data_plan(rows, tile):
    own = [(1, at, tile) for at in range(0, rows // 2, tile)] + [(1, rows // 2, rows // 2)]
    return [(0, 0, tile)] + own + [(0, tile, rows - tile)]


def data_kernel(plan, starts_ref, mask_ref, block_ref, first_ref, kspace_first_ref, kspace_ref, sens_ref,
                normal_ref, other_ref, own_ref, back, own_held, own_sem, late_held, late_sem, *held):
    frames, coils, rows, width = kspace_ref.shape
    groups, _, per, _ = own_ref.shape
    half = width // 2
    quarter = half // 2
    pieces = [held[4 * k : 4 * k + 4] for k in range(len(plan) - 1)]

    def fetch(step):
        part, at, size = plan[step]
        kspace_held, sens_held, kspace_sem, sens_sem = pieces[step - 1]
        place = pl.ds(pl.multiple_of(starts_ref[part] + at, plan[0][2]), size)
        copies = [pltpu.make_async_copy(sens_ref.at[:, place], sens_held, sens_sem)]
        for t in range(frames):
            copies.append(
                pltpu.make_async_copy(kspace_ref.at[t, :, place], kspace_held.at[t], kspace_sem.at[t])
            )
        return copies

    def begin(step):
        if step < len(plan):
            for copy in fetch(step):
                copy.start()

    late = []
    for t in range(1, frames):
        place = pl.ds(pl.multiple_of(starts_ref[0], plan[0][2]), plan[0][2])
        late.append(
            pltpu.make_async_copy(kspace_ref.at[t, :, place], late_held.at[t - 1], late_sem.at[t - 1])
        )
    for copy in late:
        copy.start()
    begin(1)
    block = block_ref[...]
    for t in range(frames):
        keep = mask_ref[t : t + 1, :].astype(F32)
        cosine = (block[:, :half].astype(F32) * keep).astype(BF16).T
        sine_part = (block[:, half:].astype(F32) * keep).astype(BF16).T
        back[t, :half, :half] = cosine
        back[t, :half, half:] = -sine_part
        back[t, half:, :half] = sine_part
        back[t, half:, half:] = cosine
        near = dot(block[:quarter], back[t])
        for k in range(2):
            for part in range(2):
                at = part * half
                low, high = near[:, at : at + quarter], near[:, at + quarter : at + half]
                table = (0.5 * (low + high if k == 0 else low - high)).astype(BF16)
                normal_ref[t, k, :, part * quarter : (part + 1) * quarter] = table
        if t == 0:
            begin(2)
    own_left = sum(part == 1 for part, _, _ in plan)
    leaving = pltpu.make_async_copy(own_held, own_ref, own_sem)
    for step, (part, at, size) in enumerate(plan):
        if step:
            begin(step + 2)
            for copy in fetch(step):
                copy.wait()
            kspace_held, sens_held = pieces[step - 1][:2]
        else:
            kspace_held = [kspace_first_ref] + [late_held.at[t] for t in range(frames - 1)]
            sens_held = first_ref.at[:, :size]
        sens = sens_held[...].astype(F32)
        sens_r, sens_i = sens[..., :half], sens[..., half:]
        for t in range(frames):
            if step == 0 and t:
                late[t - 1].wait()
            kspace = kspace_held[t][...] if step == 0 else kspace_held[t]
            adjoint = dot(kspace.reshape(coils * size, width), back[t])
            real, imag = conj_sum(adjoint.reshape(coils, size, width), sens_r, sens_i)
            if part:
                group = slice(at // per, (at + size) // per)
                own_held[group, t, :, :half] = real.reshape(size // per, per, half)
                own_held[group, t, :, half:] = imag.reshape(size // per, per, half)
            else:
                other_ref[t, at : at + size, :half] = real
                other_ref[t, at : at + size, half:] = imag
        own_left -= part
        if part and own_left == 0:
            leaving.start()
    leaving.wait()


def normal_kernel(other, starts_ref, image_ref, first_ref, sens_ref, normal_ref, *rest):
    if other:
        data_ref, out_ref, next_ref, table, sens_held, sem, next_sem = rest
    else:
        out_ref, table, sens_held, sem = rest
    groups, frames, per, width = image_ref.shape
    coils, tile, _ = first_ref.shape
    half = width // 2
    quarter = half // 2
    step_groups = tile // per
    steps = groups // step_groups

    def spot(step, which):
        return pl.ds(pl.multiple_of(starts_ref[which] + step * tile, tile), tile)

    def fetch(step):
        source = sens_ref.at[:, spot(step, 0 if other else 1)]
        return pltpu.make_async_copy(source, sens_held.at[step - 1], sem.at[step - 1])

    for step in range(1, steps):
        fetch(step).start()
    if other:
        staging = pltpu.make_async_copy(sens_ref.at[:, spot(0, 1)], next_ref, next_sem)
        staging.start()
    for t in range(frames):
        for k in range(2):
            near = normal_ref[t, k]
            table[t, k, :quarter] = near
            table[t, k, quarter:, :quarter] = -near[:, quarter:]
            table[t, k, quarter:, quarter:] = near[:, :quarter]

    def work(step, sens):
        place = pl.ds(step * tile, tile)
        group = pl.ds(step * step_groups, step_groups)
        sens = sens.astype(F32)
        sens_r, sens_i = sens[..., :half], sens[..., half:]
        for t in range(frames):
            image = image_ref[group, t].reshape(tile, width).astype(F32)
            image_r, image_i = image[:, :half], image[:, half:]
            coil_r = sens_r * image_r - sens_i * image_i
            coil_i = sens_r * image_i + sens_i * image_r
            low_r, high_r = coil_r[..., :quarter], coil_r[..., quarter:]
            low_i, high_i = coil_i[..., :quarter], coil_i[..., quarter:]
            plus = jnp.concatenate([low_r + high_r, low_i + high_i], -1).astype(BF16)
            minus = jnp.concatenate([low_r - high_r, low_i - high_i], -1).astype(BF16)
            plus = dot(plus.reshape(coils * tile, half), table[t, 0]).reshape(coils, tile, half)
            minus = dot(minus.reshape(coils * tile, half), table[t, 1]).reshape(coils, tile, half)
            for k, both in enumerate((plus + minus, plus - minus)):
                lanes = slice(k * quarter, (k + 1) * quarter)
                real, imag = conj_sum(both, sens_r[..., lanes], sens_i[..., lanes])
                low = slice(k * quarter, (k + 1) * quarter)
                high = slice(half + k * quarter, half + (k + 1) * quarter)
                if other:
                    real = real - data_ref[t, place, low]
                    imag = imag - data_ref[t, place, high]
                out_ref[group, t, :, low] = real.reshape(step_groups, per, quarter)
                out_ref[group, t, :, high] = imag.reshape(step_groups, per, quarter)

    work(0, first_ref[...])

    @pl.loop(1, steps)
    def _(step):
        fetch(step).wait()
        work(step, sens_held[step - 1])

    if other:
        staging.wait()


def cost(flops, moved):
    return pl.CostEstimate(flops=int(flops), bytes_accessed=int(moved), transcendentals=0)


VMEM = pl.BlockSpec(memory_space=pltpu.VMEM)
SMEM = pl.BlockSpec(memory_space=pltpu.SMEM)
HBM = pl.BlockSpec(memory_space=pltpu.HBM)
MIB = 1 << 20


def local(array):
    return pltpu.with_memory_space_constraint(array, pltpu.VMEM)


def remote(array):
    return pltpu.with_memory_space_constraint(array, pltpu.HBM)


def grant(mib):
    return pltpu.CompilerParams(vmem_limit_bytes=mib * MIB)


def stage(starts, sampled, block, spatial, sens, kspace, tile):
    _, coils, _, width = kspace.shape
    return pl.pallas_call(
        stage_kernel,
        in_specs=[SMEM] + [HBM] * 5,
        out_specs=[VMEM] * 5,
        out_shape=[
            pltpu.VMEM(sampled.shape, jnp.int32),
            pltpu.VMEM(block.shape, BF16),
            pltpu.VMEM(spatial.shape, BF16),
            pltpu.VMEM((coils, 2 * tile, width), BF16),
            pltpu.VMEM((coils, tile, width), BF16),
        ],
        scratch_shapes=[pltpu.SemaphoreType.DMA((5,))],
        cost_estimate=cost(0, 8 * block.size),
        compiler_params=grant(12),
        name="stage",
    )(starts, remote(sampled), remote(block), remote(spatial), remote(sens), remote(kspace))


def data_term(starts, mask, block, first, kspace_first, kspace, sens, per):
    frames, coils, rows, width = kspace.shape
    own = (rows // 2 // per, frames, per, width)
    plan = data_plan(rows // 2, kspace_first.shape[1])
    scratch = [
        pltpu.VMEM((frames, width, width), BF16),
        pltpu.VMEM(own, F32),
        pltpu.SemaphoreType.DMA,
        pltpu.VMEM((max(frames - 1, 1), coils, plan[0][2], width), BF16),
        pltpu.SemaphoreType.DMA((max(frames - 1, 1),)),
    ]
    for _, _, size in plan[1:]:
        scratch += [
            pltpu.VMEM((frames, coils, size, width), BF16),
            pltpu.VMEM((coils, size, width), BF16),
            pltpu.SemaphoreType.DMA((frames,)),
            pltpu.SemaphoreType.DMA,
        ]
    return pl.pallas_call(
        functools.partial(data_kernel, plan),
        in_specs=[SMEM] + [VMEM] * 4 + [HBM] * 2,
        out_specs=[VMEM, VMEM, HBM],
        out_shape=[
            pltpu.VMEM((frames, 2, width // 4, width // 2), BF16),
            pltpu.VMEM((frames, rows // 2, width), F32),
            pltpu.HBM(own, F32),
        ],
        scratch_shapes=scratch,
        cost_estimate=cost(2 * frames * coils * rows * width * width, 2 * kspace.size),
        compiler_params=grant(36),
        name="data_term",
    )(starts, mask, block, first, kspace_first, remote(kspace), remote(sens))


def normal_term(starts, image, first, sens, normal, data=None):
    groups, frames, per, width = image.shape
    coils, tile, _ = first.shape
    steps = groups * per // tile
    other = data is not None
    outs = [pltpu.VMEM((groups, frames, per, width), F32)]
    scratch = [
        pltpu.VMEM((frames, 2, width // 2, width // 2), BF16),
        pltpu.VMEM((steps - 1, coils, tile, width), BF16),
        pltpu.SemaphoreType.DMA((steps - 1,)),
    ]
    if other:
        outs.append(pltpu.VMEM(first.shape, BF16))
        scratch.append(pltpu.SemaphoreType.DMA)
    return pl.pallas_call(
        functools.partial(normal_kernel, other),
        in_specs=[SMEM, VMEM, VMEM, HBM, VMEM] + [VMEM] * other,
        out_specs=[VMEM] * len(outs),
        out_shape=outs,
        scratch_shapes=scratch,
        cost_estimate=cost(
            2 * frames * coils * groups * per * width * width, coils * groups * per * width * 2
        ),
        compiler_params=grant(20),
        name="normal_other" if other else "normal_own",
    )(starts, image, first, remote(sens), normal, *([data] if other else []))


def on_device(frame_size, coil_size, spatial, temporal, kspace, sampled, sensitivity):
    rows, rank, width = spatial.shape
    per = temporal.shape[0]
    total = per * frame_size
    half_rows = rows * frame_size
    swap = [(i, (i + 1) % coil_size) for i in range(coil_size)]
    own = lax.axis_index("coil") * half_rows
    starts = jnp.stack([(own + half_rows) % (coil_size * half_rows), own])
    spatial2 = spatial.reshape(rows * rank, width)

    factors = lax.all_to_all(
        jnp.broadcast_to(temporal[None], (frame_size, per, 2 * rank)), "frame", 0, 0, tiled=True
    )
    mask, block, near, first, kspace_first = stage(
        starts, sampled, jnp.asarray(dft_half(width // 2)), spatial2, sensitivity, kspace, 32
    )
    image = pl.pallas_call(
        functools.partial(image_kernel, total, rows, rank),
        in_specs=[VMEM, VMEM],
        out_specs=VMEM,
        out_shape=pltpu.VMEM((total * rows, width), BF16),
        compiler_params=grant(12),
        name="image_rows",
    )(local(factors), near)
    image, kspace = lax.optimization_barrier((image, kspace))
    image = lax.all_to_all(image.reshape(frame_size, per, rows, width), "frame", 0, 0, tiled=True)
    regroup = rows % 16 != 0
    normal, data_other, data_own = data_term(
        starts, mask, block, first, kspace_first, kspace, sensitivity, 16 if regroup else rows
    )
    image, normal = lax.optimization_barrier((image, normal))
    if regroup:
        image = image.transpose(1, 0, 2, 3).reshape(per, half_rows // 16, 16, width).transpose(1, 0, 2, 3)
    image_other = lax.ppermute(image, "coil", swap)
    send, first = normal_term(starts, local(image_other), first, sensitivity, normal, data_other)
    received = lax.ppermute(send, "coil", swap)
    (keep_own,) = normal_term(starts, local(image), first, sensitivity, normal)
    grad = (keep_own + received - data_own).astype(BF16)
    if regroup:
        grad = grad.transpose(1, 0, 2, 3).reshape(per, frame_size, rows, width).transpose(1, 0, 2, 3)
    grad = lax.all_to_all(grad, "frame", 0, 0, tiled=True).reshape(total * rows, width)
    grad = local(grad)

    partial = pl.pallas_call(
        functools.partial(temporal_kernel, total, rows, rank),
        in_specs=[VMEM, VMEM],
        out_specs=VMEM,
        out_shape=pltpu.VMEM((frame_size * coil_size, 1, per * 2 * rank), F32),
        compiler_params=grant(12),
        name="temporal_rows",
    )(local(spatial2), grad)
    partial = lax.all_to_all(partial, ("frame", "coil"), 0, 0, tiled=True)
    spatial_grad = pl.pallas_call(
        functools.partial(spatial_kernel, total, rows, rank),
        in_specs=[VMEM, VMEM],
        out_specs=VMEM,
        out_shape=jax.ShapeDtypeStruct((rows * rank, width), F32),
        compiler_params=grant(12),
        name="spatial_rows",
    )(local(factors), grad)
    temporal_grad = pl.pallas_call(
        sum_kernel,
        in_specs=[VMEM],
        out_specs=VMEM,
        out_shape=jax.ShapeDtypeStruct((per, 2 * rank), F32),
        compiler_params=grant(2),
        name="temporal_sum",
    )(partial)
    return (spatial_grad.reshape(rows, rank, width), temporal_grad)


def solution(mesh):
    placed = (
        P(("cuts", "coil", "frame"), None, None),
        P(("cuts", "frame"), None),
        P(("cuts", "frame"), "coil", None, None),
        P(("cuts", "frame"), None),
        P(("cuts", "coil"), None, None),
    )
    return jax.shard_map(
        functools.partial(on_device, mesh.shape["frame"], mesh.shape["coil"]),
        mesh=mesh,
        in_specs=placed,
        out_specs=(P(("cuts", "coil", "frame"), None, None), P(("cuts", "frame"), None)),
        check_vma=False,
    )
```

```python
import functools
import math

import jax
import jax.numpy as jnp
import numpy as np
from jax import lax
from jax.experimental import pallas as pl
from jax.experimental.pallas import tpu as pltpu
from jax.sharding import PartitionSpec as P

F32 = jnp.float32
BF16 = jnp.bfloat16


def dft_half(length):
    index = np.arange(length)
    angles = (index[:, None] * index[None, :] % length) * (2.0 * math.pi / length)
    cosine = np.cos(angles) / math.sqrt(length)
    sine_part = -np.sin(angles) / math.sqrt(length)
    return np.concatenate([cosine, sine_part], 1).astype(np.float32).astype(BF16)


def dot(a, b):
    return jnp.dot(a, b, preferred_element_type=F32)


def dot_t(a, b):
    return lax.dot_general(a, b, (((1,), (1,)), ((), ())), preferred_element_type=F32)


def iota(shape, axis):
    return lax.broadcasted_iota(jnp.int32, shape, axis)


def spread(factors_ref, total, rows, rank):
    groups, per, lanes = factors_ref.shape
    height = 2 * total * rows
    frame = iota((height, groups), 0) // rows % total
    factors = factors_ref[...].astype(F32)
    picked = jnp.zeros((height, lanes), F32)
    for t in range(per):
        pick = jnp.where(frame == iota((height, groups), 1) * per + t, 1.0, 0.0).astype(BF16)
        picked = picked + dot(pick, factors[:, t].astype(BF16))
    mine = iota((height, lanes), 1) // rank == iota((height, lanes), 0) // (total * rows)
    return jnp.where(mine, picked, 0.0).astype(BF16)


def image_kernel(total, rows, rank, factors_ref, spatial_ref, image_ref):
    mid = spread(factors_ref, total, rows, rank)
    lanes = mid.shape[1]
    width = rows * rank
    tile = jnp.where(iota((lanes, width), 0) % rank == iota((lanes, width), 1) % rank, 1.0, 0.0)
    wide = dot(mid, tile.astype(BF16))
    height = wide.shape[0]
    same = iota((height, width), 0) % rows == iota((height, width), 1) // rank
    wide = jnp.where(same, wide, 0.0).astype(BF16)
    product = dot(wide, spatial_ref[...])
    half = height // 2
    mid_col = product.shape[1] // 2
    image_ref[:, :mid_col] = (product[:half, :mid_col] - product[half:, mid_col:]).astype(BF16)
    image_ref[:, mid_col:] = (product[:half, mid_col:] + product[half:, :mid_col]).astype(BF16)


def both_parts(grad):
    half = grad.shape[1] // 2
    turned = jnp.concatenate([grad[:, half:], -grad[:, :half]], 1)
    return jnp.concatenate([grad, turned], 0)


def spatial_kernel(total, rows, rank, factors_ref, grad_ref, out_ref):
    mid = spread(factors_ref, total, rows, rank)
    lanes = mid.shape[1]
    width = rows * rank
    tile = jnp.where(iota((width, lanes), 0) % rank == iota((width, lanes), 1) % rank, 1.0, 0.0)
    wide = dot_t(tile.astype(BF16), mid)
    height = mid.shape[0]
    same = iota((width, height), 1) % rows == iota((width, height), 0) // rank
    wide = jnp.where(same, wide, 0.0).astype(BF16)
    out_ref[...] = dot(wide, both_parts(grad_ref[...]))


def temporal_kernel(total, rows, rank, spatial_ref, grad_ref, out_ref):
    product = dot_t(both_parts(grad_ref[...]), spatial_ref[...])
    height, width = product.shape
    same = iota((height, width), 0) % rows == iota((height, width), 1) // rank
    product = jnp.where(same, product, 0.0)
    lanes = 128
    fold = product[:, :lanes]
    for start in range(lanes, width, lanes):
        fold = fold + product[:, start : start + lanes]
    if rows % 8 == 0:
        fold = jnp.sum(fold.reshape(2 * total, rows, lanes), axis=1)
    else:
        pick = iota((2 * total, height), 0) == iota((2 * total, height), 1) // rows
        fold = jnp.dot(
            jnp.where(pick, 1.0, 0.0), fold, precision=lax.Precision.HIGHEST, preferred_element_type=F32
        )
    shift = lanes // 2
    while shift >= rank:
        fold = fold + pltpu.roll(fold, shift, 1)
        shift //= 2
    lane = iota((total, lanes), 1)
    both = jnp.where(lane // rank % 2 == 0, fold[:total], fold[total:])
    groups, _, span = out_ref.shape
    per = span // (2 * rank)
    copies = groups * per // total
    place = iota((1, span), 1) // (2 * rank)
    for group in range(groups // copies):
        line = both[group * per : group * per + 1, :span]
        for t in range(1, per):
            line = jnp.where(place == t, both[group * per + t : group * per + t + 1, :span], line)
        for copy in range(copies):
            out_ref[group * copies + copy] = line


def sum_kernel(parts_ref, out_ref):
    line = jnp.sum(parts_ref[...], axis=0)
    per, span = out_ref.shape
    for t in range(per):
        out_ref[t : t + 1, :] = line[:, t * span : (t + 1) * span]


def conj_sum(adjoint, sens_r, sens_i):
    half = sens_r.shape[-1]
    back_r, back_i = adjoint[..., :half], adjoint[..., half:]
    return (
        jnp.sum(sens_r * back_r + sens_i * back_i, axis=0),
        jnp.sum(sens_r * back_i - sens_i * back_r, axis=0),
    )


def stage_kernel(starts_ref, sampled_ref, block_ref, spatial_ref, sens_ref, kspace_ref,
                 mask_out, block_out, spatial_out, sens_out, kspace_out, sems):
    start = pl.multiple_of(starts_ref[1], sens_out.shape[1])
    copies = [
        pltpu.make_async_copy(spatial_ref, spatial_out, sems.at[0]),
        pltpu.make_async_copy(sampled_ref, mask_out, sems.at[1]),
        pltpu.make_async_copy(block_ref, block_out, sems.at[2]),
        pltpu.make_async_copy(sens_ref.at[:, pl.ds(start, sens_out.shape[1])], sens_out, sems.at[3]),
        pltpu.make_async_copy(kspace_ref.at[0, :, pl.ds(start, kspace_out.shape[1])], kspace_out, sems.at[4]),
    ]
    for copy in copies:
        copy.start()
    for copy in copies:
        copy.wait()


def data_plan(rows, tile):
    own = [(1, at, tile) for at in range(0, rows // 2, tile)]
    return own + [(0, 0, tile), (1, rows // 2, rows // 2), (0, tile, rows - tile)]


def data_kernel(plan, starts_ref, mask_ref, block_ref, first_ref, kspace_first_ref, kspace_ref, sens_ref,
                normal_ref, other_ref, own_ref, back, own_held, own_sem, late_held, late_sem, *held):
    frames, coils, rows, width = kspace_ref.shape
    groups, _, per, _ = own_ref.shape
    half = width // 2
    quarter = half // 2
    pieces = [held[4 * k : 4 * k + 4] for k in range(len(plan) - 1)]

    def fetch(step):
        part, at, size = plan[step]
        kspace_held, sens_held, kspace_sem, sens_sem = pieces[step - 1]
        place = pl.ds(pl.multiple_of(starts_ref[part] + at, plan[0][2]), size)
        copies = [pltpu.make_async_copy(sens_ref.at[:, place], sens_held, sens_sem)]
        for t in range(frames):
            copies.append(
                pltpu.make_async_copy(kspace_ref.at[t, :, place], kspace_held.at[t], kspace_sem.at[t])
            )
        return copies

    def begin(step):
        if step < len(plan):
            for copy in fetch(step):
                copy.start()

    late = []
    for t in range(1, frames):
        place = pl.ds(pl.multiple_of(starts_ref[plan[0][0]], plan[0][2]), plan[0][2])
        late.append(
            pltpu.make_async_copy(kspace_ref.at[t, :, place], late_held.at[t - 1], late_sem.at[t - 1])
        )
    for copy in late:
        copy.start()
    begin(1)
    block = block_ref[...]
    for t in range(frames):
        keep = mask_ref[t : t + 1, :].astype(F32)
        cosine = (block[:, :half].astype(F32) * keep).astype(BF16).T
        sine_part = (block[:, half:].astype(F32) * keep).astype(BF16).T
        back[t, :half, :half] = cosine
        back[t, :half, half:] = -sine_part
        back[t, half:, :half] = sine_part
        back[t, half:, half:] = cosine
        near = dot(block[:quarter], back[t])
        for k in range(2):
            for part in range(2):
                at = part * half
                low, high = near[:, at : at + quarter], near[:, at + quarter : at + half]
                table = (0.5 * (low + high if k == 0 else low - high)).astype(BF16)
                normal_ref[t, k, :, part * quarter : (part + 1) * quarter] = table
        if t == 0:
            begin(2)
    own_left = sum(part == 1 for part, _, _ in plan)
    leaving = pltpu.make_async_copy(own_held, own_ref, own_sem)
    for step, (part, at, size) in enumerate(plan):
        if step:
            begin(step + 2)
            for copy in fetch(step):
                copy.wait()
            kspace_held, sens_held = pieces[step - 1][:2]
        else:
            kspace_held = [kspace_first_ref] + [late_held.at[t] for t in range(frames - 1)]
            sens_held = first_ref.at[:, :size]
        sens = sens_held[...].astype(F32)
        sens_r, sens_i = sens[..., :half], sens[..., half:]
        for t in range(frames):
            if step == 0 and t:
                late[t - 1].wait()
            kspace = kspace_held[t][...] if step == 0 else kspace_held[t]
            adjoint = dot(kspace.reshape(coils * size, width), back[t])
            real, imag = conj_sum(adjoint.reshape(coils, size, width), sens_r, sens_i)
            if part:
                group = slice(at // per, (at + size) // per)
                own_held[group, t, :, :half] = real.reshape(size // per, per, half)
                own_held[group, t, :, half:] = imag.reshape(size // per, per, half)
            else:
                other_ref[t, at : at + size, :half] = real
                other_ref[t, at : at + size, half:] = imag
        own_left -= part
        if part and own_left == 0:
            leaving.start()
    leaving.wait()


def normal_kernel(part, begin, end, following, starts_ref, image_ref, first_ref, sens_ref, normal_ref, *rest):
    data_ref = rest[0] if part == 0 else None
    rest = list(rest[1:]) if part == 0 or begin else list(rest)
    if following:
        out_ref, next_ref, table, sens_held, sem, next_sem = rest
    else:
        out_ref, table, sens_held, sem = rest
    _, frames, per, width = image_ref.shape
    coils, tile, _ = first_ref.shape
    half = width // 2
    quarter = half // 2
    step_groups = tile // per
    steps = (end - begin) // tile

    def spot(which, at):
        return pl.ds(pl.multiple_of(starts_ref[which] + at, tile), tile)

    def fetch(step):
        source = sens_ref.at[:, spot(part, begin + step * tile)]
        return pltpu.make_async_copy(source, sens_held.at[step - 1], sem.at[step - 1])

    for step in range(1, steps):
        fetch(step).start()
    if following:
        staging = pltpu.make_async_copy(sens_ref.at[:, spot(*following)], next_ref, next_sem)
        staging.start()
    for t in range(frames):
        for k in range(2):
            near = normal_ref[t, k]
            table[t, k, :quarter] = near
            table[t, k, quarter:, :quarter] = -near[:, quarter:]
            table[t, k, quarter:, quarter:] = near[:, :quarter]

    def work(step, sens):
        place = pl.ds(begin + step * tile, tile)
        group = pl.ds(begin // per + step * step_groups, step_groups)
        sens = sens.astype(F32)
        sens_r, sens_i = sens[..., :half], sens[..., half:]
        for t in range(frames):
            image = image_ref[group, t].reshape(tile, width).astype(F32)
            image_r, image_i = image[:, :half], image[:, half:]
            coil_r = sens_r * image_r - sens_i * image_i
            coil_i = sens_r * image_i + sens_i * image_r
            low_r, high_r = coil_r[..., :quarter], coil_r[..., quarter:]
            low_i, high_i = coil_i[..., :quarter], coil_i[..., quarter:]
            plus = jnp.concatenate([low_r + high_r, low_i + high_i], -1).astype(BF16)
            minus = jnp.concatenate([low_r - high_r, low_i - high_i], -1).astype(BF16)
            plus = dot(plus.reshape(coils * tile, half), table[t, 0]).reshape(coils, tile, half)
            minus = dot(minus.reshape(coils * tile, half), table[t, 1]).reshape(coils, tile, half)
            for k, both in enumerate((plus + minus, plus - minus)):
                lanes = slice(k * quarter, (k + 1) * quarter)
                real, imag = conj_sum(both, sens_r[..., lanes], sens_i[..., lanes])
                low = slice(k * quarter, (k + 1) * quarter)
                high = slice(half + k * quarter, half + (k + 1) * quarter)
                if part == 0:
                    real = real - data_ref[t, place, low]
                    imag = imag - data_ref[t, place, high]
                out_ref[group, t, :, low] = real.reshape(step_groups, per, quarter)
                out_ref[group, t, :, high] = imag.reshape(step_groups, per, quarter)

    work(0, first_ref[...])

    @pl.loop(1, steps)
    def _(step):
        fetch(step).wait()
        work(step, sens_held[step - 1])

    if following:
        staging.wait()


def cost(flops, moved):
    return pl.CostEstimate(flops=int(flops), bytes_accessed=int(moved), transcendentals=0)


VMEM = pl.BlockSpec(memory_space=pltpu.VMEM)
SMEM = pl.BlockSpec(memory_space=pltpu.SMEM)
HBM = pl.BlockSpec(memory_space=pltpu.HBM)
MIB = 1 << 20


def local(array):
    return pltpu.with_memory_space_constraint(array, pltpu.VMEM)


def remote(array):
    return pltpu.with_memory_space_constraint(array, pltpu.HBM)


def grant(mib):
    return pltpu.CompilerParams(vmem_limit_bytes=mib * MIB)


def stage(starts, sampled, block, spatial, sens, kspace, tile):
    _, coils, _, width = kspace.shape
    return pl.pallas_call(
        stage_kernel,
        in_specs=[SMEM] + [HBM] * 5,
        out_specs=[VMEM] * 5,
        out_shape=[
            pltpu.VMEM(sampled.shape, jnp.int32),
            pltpu.VMEM(block.shape, BF16),
            pltpu.VMEM(spatial.shape, BF16),
            pltpu.VMEM((coils, 2 * tile, width), BF16),
            pltpu.VMEM((coils, tile, width), BF16),
        ],
        scratch_shapes=[pltpu.SemaphoreType.DMA((5,))],
        cost_estimate=cost(0, 8 * block.size),
        compiler_params=grant(12),
        name="stage",
    )(starts, remote(sampled), remote(block), remote(spatial), remote(sens), remote(kspace))


def data_term(starts, mask, block, first, kspace_first, kspace, sens, per):
    frames, coils, rows, width = kspace.shape
    own = (rows // 2 // per, frames, per, width)
    plan = data_plan(rows // 2, kspace_first.shape[1])
    scratch = [
        pltpu.VMEM((frames, width, width), BF16),
        pltpu.VMEM(own, F32),
        pltpu.SemaphoreType.DMA,
        pltpu.VMEM((max(frames - 1, 1), coils, plan[0][2], width), BF16),
        pltpu.SemaphoreType.DMA((max(frames - 1, 1),)),
    ]
    for _, _, size in plan[1:]:
        scratch += [
            pltpu.VMEM((frames, coils, size, width), BF16),
            pltpu.VMEM((coils, size, width), BF16),
            pltpu.SemaphoreType.DMA((frames,)),
            pltpu.SemaphoreType.DMA,
        ]
    return pl.pallas_call(
        functools.partial(data_kernel, plan),
        in_specs=[SMEM] + [VMEM] * 4 + [HBM] * 2,
        out_specs=[VMEM, VMEM, HBM],
        out_shape=[
            pltpu.VMEM((frames, 2, width // 4, width // 2), BF16),
            pltpu.VMEM((frames, rows // 2, width), F32),
            pltpu.HBM(own, F32),
        ],
        scratch_shapes=scratch,
        cost_estimate=cost(2 * frames * coils * rows * width * width, 2 * kspace.size),
        compiler_params=grant(36),
        name="data_term",
    )(starts, mask, block, first, kspace_first, remote(kspace), remote(sens))


def normal_term(part, begin, end, following, starts, image, first, sens, normal, more=()):
    groups, frames, per, width = image.shape
    coils, tile, _ = first.shape
    steps = (end - begin) // tile
    spare = max(steps - 1, 1)
    outs = [pltpu.VMEM((groups, frames, per, width), F32)]
    scratch = [
        pltpu.VMEM((frames, 2, width // 2, width // 2), BF16),
        pltpu.VMEM((spare, coils, tile, width), BF16),
        pltpu.SemaphoreType.DMA((spare,)),
    ]
    if following:
        outs.append(pltpu.VMEM(first.shape, BF16))
        scratch.append(pltpu.SemaphoreType.DMA)
    return pl.pallas_call(
        functools.partial(normal_kernel, part, begin, end, following),
        in_specs=[SMEM, VMEM, VMEM, HBM, VMEM] + [VMEM] * len(more),
        out_specs=[VMEM] * len(outs),
        out_shape=outs,
        scratch_shapes=scratch,
        input_output_aliases={5: 0} if part and begin else {},
        cost_estimate=cost(
            frames * coils * (end - begin) * width * width, coils * (end - begin) * width * 2
        ),
        compiler_params=grant(32),
        name="normal_term",
    )(starts, image, first, remote(sens), normal, *more)


def on_device(frame_size, coil_size, spatial, temporal, kspace, sampled, sensitivity):
    rows, rank, width = spatial.shape
    per = temporal.shape[0]
    total = per * frame_size
    half_rows = rows * frame_size
    swap = [(i, (i + 1) % coil_size) for i in range(coil_size)]
    own = lax.axis_index("coil") * half_rows
    starts = jnp.stack([(own + half_rows) % (coil_size * half_rows), own])
    spatial2 = spatial.reshape(rows * rank, width)

    factors = lax.all_to_all(
        jnp.broadcast_to(temporal[None], (frame_size, per, 2 * rank)), "frame", 0, 0, tiled=True
    )
    mask, block, near, first, kspace_first = stage(
        starts, sampled, jnp.asarray(dft_half(width // 2)), spatial2, sensitivity, kspace, 32
    )
    image = pl.pallas_call(
        functools.partial(image_kernel, total, rows, rank),
        in_specs=[VMEM, VMEM],
        out_specs=VMEM,
        out_shape=pltpu.VMEM((total * rows, width), BF16),
        compiler_params=grant(12),
        name="image_rows",
    )(local(factors), near)
    image, kspace = lax.optimization_barrier((image, kspace))
    image = lax.all_to_all(image.reshape(frame_size, per, rows, width), "frame", 0, 0, tiled=True)
    regroup = rows % 16 != 0
    normal, data_other, data_own = data_term(
        starts, mask, block, first, kspace_first, kspace, sensitivity, 16 if regroup else rows
    )
    image, normal = lax.optimization_barrier((image, normal))
    if regroup:
        image = image.transpose(1, 0, 2, 3).reshape(per, half_rows // 16, 16, width).transpose(1, 0, 2, 3)
    image_other = lax.ppermute(image, "coil", swap)
    middle = half_rows // 2
    image = local(image)
    keep_own, first = normal_term(1, 0, middle, (0, 0), starts, image, first, sensitivity, normal)
    image_other, keep_own = lax.optimization_barrier((image_other, keep_own))
    send, first = normal_term(
        0, 0, half_rows, (1, middle), starts, local(image_other), first, sensitivity, normal, (data_other,)
    )
    received = lax.ppermute(send, "coil", swap)
    (keep_own,) = normal_term(
        1, middle, half_rows, None, starts, image, first, sensitivity, normal, (keep_own,)
    )
    grad = (keep_own + received - data_own).astype(BF16)
    if regroup:
        grad = grad.transpose(1, 0, 2, 3).reshape(per, frame_size, rows, width).transpose(1, 0, 2, 3)
    grad = lax.all_to_all(grad, "frame", 0, 0, tiled=True).reshape(total * rows, width)
    grad = local(grad)

    partial = pl.pallas_call(
        functools.partial(temporal_kernel, total, rows, rank),
        in_specs=[VMEM, VMEM],
        out_specs=VMEM,
        out_shape=pltpu.VMEM((frame_size * coil_size, 1, per * 2 * rank), F32),
        compiler_params=grant(12),
        name="temporal_rows",
    )(local(spatial2), grad)
    partial = lax.all_to_all(partial, ("frame", "coil"), 0, 0, tiled=True)
    spatial_grad = pl.pallas_call(
        functools.partial(spatial_kernel, total, rows, rank),
        in_specs=[VMEM, VMEM],
        out_specs=VMEM,
        out_shape=jax.ShapeDtypeStruct((rows * rank, width), F32),
        compiler_params=grant(12),
        name="spatial_rows",
    )(local(factors), grad)
    temporal_grad = pl.pallas_call(
        sum_kernel,
        in_specs=[VMEM],
        out_specs=VMEM,
        out_shape=jax.ShapeDtypeStruct((per, 2 * rank), F32),
        compiler_params=grant(2),
        name="temporal_sum",
    )(partial)
    return (spatial_grad.reshape(rows, rank, width), temporal_grad)


def solution(mesh):
    placed = (
        P(("cuts", "coil", "frame"), None, None),
        P(("cuts", "frame"), None),
        P(("cuts", "frame"), "coil", None, None),
        P(("cuts", "frame"), None),
        P(("cuts", "coil"), None, None),
    )
    return jax.shard_map(
        functools.partial(on_device, mesh.shape["frame"], mesh.shape["coil"]),
        mesh=mesh,
        in_specs=placed,
        out_specs=(P(("cuts", "coil", "frame"), None, None), P(("cuts", "frame"), None)),
        check_vma=False,
    )
```

```python
import functools
import math

import jax
import jax.numpy as jnp
import numpy as np
from jax import lax
from jax.experimental import pallas as pl
from jax.experimental.pallas import tpu as pltpu
from jax.sharding import PartitionSpec as P

F32 = jnp.float32
BF16 = jnp.bfloat16


def dft_half(length):
    index = np.arange(length)
    angles = (index[:, None] * index[None, :] % length) * (2.0 * math.pi / length)
    cosine = np.cos(angles) / math.sqrt(length)
    sine_part = -np.sin(angles) / math.sqrt(length)
    return np.concatenate([cosine, sine_part], 1).astype(np.float32).astype(BF16)


def dot(a, b):
    return jnp.dot(a, b, preferred_element_type=F32)


def dot_t(a, b):
    return lax.dot_general(a, b, (((1,), (1,)), ((), ())), preferred_element_type=F32)


def iota(shape, axis):
    return lax.broadcasted_iota(jnp.int32, shape, axis)


def spread(factors_ref, total, rows, rank):
    groups, per, lanes = factors_ref.shape
    height = 2 * total * rows
    frame = iota((height, groups), 0) // rows % total
    factors = factors_ref[...].astype(F32)
    picked = jnp.zeros((height, lanes), F32)
    for t in range(per):
        pick = jnp.where(frame == iota((height, groups), 1) * per + t, 1.0, 0.0).astype(BF16)
        picked = picked + dot(pick, factors[:, t].astype(BF16))
    mine = iota((height, lanes), 1) // rank == iota((height, lanes), 0) // (total * rows)
    return jnp.where(mine, picked, 0.0).astype(BF16)


def image_kernel(total, rows, rank, factors_ref, spatial_ref, image_ref):
    mid = spread(factors_ref, total, rows, rank)
    lanes = mid.shape[1]
    width = rows * rank
    tile = jnp.where(iota((lanes, width), 0) % rank == iota((lanes, width), 1) % rank, 1.0, 0.0)
    wide = dot(mid, tile.astype(BF16))
    height = wide.shape[0]
    same = iota((height, width), 0) % rows == iota((height, width), 1) // rank
    wide = jnp.where(same, wide, 0.0).astype(BF16)
    product = dot(wide, spatial_ref[...])
    half = height // 2
    mid_col = product.shape[1] // 2
    image_ref[:, :mid_col] = (product[:half, :mid_col] - product[half:, mid_col:]).astype(BF16)
    image_ref[:, mid_col:] = (product[:half, mid_col:] + product[half:, :mid_col]).astype(BF16)


def image_block_kernel(total, rows, rank, factors_ref, spatial_ref, image_ref, wide, held, sems):
    groups, per, lanes = factors_ref.shape
    width = rows * rank
    half = total * rows
    source = iota((lanes, 2 * width), 1)
    source = source // width * rank + source % rank
    tile = jnp.where(iota((lanes, 2 * width), 0) == source, 1.0, 0.0).astype(BF16)
    same = iota((rows, width), 0) == iota((rows, width), 1) // rank
    factors = factors_ref[...].astype(F32)
    for t in range(per):
        lines = dot(factors[:, t].astype(BF16), tile)
        for group in range(groups):
            for part in range(2):
                line = lines[group : group + 1, part * width : (part + 1) * width]
                at = part * half + (group * per + t) * rows
                wide[at : at + rows] = jnp.where(same, line, 0.0).astype(BF16)
    spatial = spatial_ref[...]
    mid = spatial.shape[1] // 2
    copies = []
    for piece in range(2):
        place = slice(piece * half // 2, (piece + 1) * half // 2)
        real = dot(wide[place], spatial)
        imag = dot(wide[half + place.start : half + place.stop], spatial)
        held[place, :mid] = (real[:, :mid] - imag[:, mid:]).astype(BF16)
        held[place, mid:] = (real[:, mid:] + imag[:, :mid]).astype(BF16)
        copies.append(pltpu.make_async_copy(held.at[place], image_ref.at[place], sems.at[piece]))
        copies[-1].start()
    for copy in copies:
        copy.wait()


def image_rows(total, rows, rank, factors, spatial):
    shape = (total * rows, spatial.shape[1])
    if rows % 16:
        body, outs, space, scratch = image_kernel, pltpu.VMEM(shape, BF16), VMEM, []
    else:
        body, outs, space = image_block_kernel, pltpu.HBM(shape, BF16), HBM
        scratch = [
            pltpu.VMEM((2 * total * rows, rows * rank), BF16),
            pltpu.VMEM(shape, BF16),
            pltpu.SemaphoreType.DMA((2,)),
        ]
    return pl.pallas_call(
        functools.partial(body, total, rows, rank),
        in_specs=[VMEM, VMEM],
        out_specs=space,
        out_shape=outs,
        scratch_shapes=scratch,
        compiler_params=grant(12),
        name="image_rows",
    )(local(factors), spatial)


def both_parts(grad):
    half = grad.shape[1] // 2
    turned = jnp.concatenate([grad[:, half:], -grad[:, :half]], 1)
    return jnp.concatenate([grad, turned], 0)


def spatial_kernel(total, rows, rank, factors_ref, grad_ref, out_ref):
    mid = spread(factors_ref, total, rows, rank)
    lanes = mid.shape[1]
    width = rows * rank
    tile = jnp.where(iota((width, lanes), 0) % rank == iota((width, lanes), 1) % rank, 1.0, 0.0)
    wide = dot_t(tile.astype(BF16), mid)
    height = mid.shape[0]
    same = iota((width, height), 1) % rows == iota((width, height), 0) // rank
    wide = jnp.where(same, wide, 0.0).astype(BF16)
    out_ref[...] = dot(wide, both_parts(grad_ref[...]))


def temporal_kernel(total, rows, rank, spatial_ref, grad_ref, out_ref):
    product = dot_t(both_parts(grad_ref[...]), spatial_ref[...])
    height, width = product.shape
    same = iota((height, width), 0) % rows == iota((height, width), 1) // rank
    product = jnp.where(same, product, 0.0)
    lanes = 128
    fold = product[:, :lanes]
    for start in range(lanes, width, lanes):
        fold = fold + product[:, start : start + lanes]
    if rows % 8 == 0:
        fold = jnp.sum(fold.reshape(2 * total, rows, lanes), axis=1)
    else:
        pick = iota((2 * total, height), 0) == iota((2 * total, height), 1) // rows
        fold = jnp.dot(
            jnp.where(pick, 1.0, 0.0), fold, precision=lax.Precision.HIGHEST, preferred_element_type=F32
        )
    shift = lanes // 2
    while shift >= rank:
        fold = fold + pltpu.roll(fold, shift, 1)
        shift //= 2
    lane = iota((total, lanes), 1)
    both = jnp.where(lane // rank % 2 == 0, fold[:total], fold[total:])
    groups, _, span = out_ref.shape
    per = span // (2 * rank)
    copies = groups * per // total
    place = iota((1, span), 1) // (2 * rank)
    for group in range(groups // copies):
        line = both[group * per : group * per + 1, :span]
        for t in range(1, per):
            line = jnp.where(place == t, both[group * per + t : group * per + t + 1, :span], line)
        for copy in range(copies):
            out_ref[group * copies + copy] = line


def sum_kernel(parts_ref, out_ref):
    line = jnp.sum(parts_ref[...], axis=0)
    per, span = out_ref.shape
    for t in range(per):
        out_ref[t : t + 1, :] = line[:, t * span : (t + 1) * span]


def conj_sum(adjoint, sens_r, sens_i):
    half = sens_r.shape[-1]
    back_r, back_i = adjoint[..., :half], adjoint[..., half:]
    return (
        jnp.sum(sens_r * back_r + sens_i * back_i, axis=0),
        jnp.sum(sens_r * back_i - sens_i * back_r, axis=0),
    )


def stage_kernel(starts_ref, sampled_ref, block_ref, spatial_ref, sens_ref, kspace_ref,
                 mask_out, block_out, spatial_out, sens_out, kspace_out, sems):
    start = pl.multiple_of(starts_ref[1], sens_out.shape[1])
    copies = [
        pltpu.make_async_copy(spatial_ref, spatial_out, sems.at[0]),
        pltpu.make_async_copy(sampled_ref, mask_out, sems.at[1]),
        pltpu.make_async_copy(block_ref, block_out, sems.at[2]),
        pltpu.make_async_copy(sens_ref.at[:, pl.ds(start, sens_out.shape[1])], sens_out, sems.at[3]),
        pltpu.make_async_copy(kspace_ref.at[0, :, pl.ds(start, kspace_out.shape[1])], kspace_out, sems.at[4]),
    ]
    for copy in copies:
        copy.start()
    for copy in copies:
        copy.wait()


def data_plan(rows, tile):
    own = [(1, at, tile) for at in range(0, rows // 2, tile)]
    return own + [(0, 0, tile), (1, rows // 2, rows // 2), (0, tile, rows - tile)]


def data_kernel(plan, starts_ref, mask_ref, block_ref, first_ref, kspace_first_ref, kspace_ref, sens_ref,
                normal_ref, other_ref, own_ref, back, own_held, own_sem, late_held, late_sem, *held):
    frames, coils, rows, width = kspace_ref.shape
    groups, _, per, _ = own_ref.shape
    half = width // 2
    quarter = half // 2
    pieces = [held[4 * k : 4 * k + 4] for k in range(len(plan) - 1)]

    def fetch(step):
        part, at, size = plan[step]
        kspace_held, sens_held, kspace_sem, sens_sem = pieces[step - 1]
        place = pl.ds(pl.multiple_of(starts_ref[part] + at, plan[0][2]), size)
        copies = [pltpu.make_async_copy(sens_ref.at[:, place], sens_held, sens_sem)]
        for t in range(frames):
            copies.append(
                pltpu.make_async_copy(kspace_ref.at[t, :, place], kspace_held.at[t], kspace_sem.at[t])
            )
        return copies

    def begin(step):
        if step < len(plan):
            for copy in fetch(step):
                copy.start()

    late = []
    for t in range(1, frames):
        place = pl.ds(pl.multiple_of(starts_ref[plan[0][0]], plan[0][2]), plan[0][2])
        late.append(
            pltpu.make_async_copy(kspace_ref.at[t, :, place], late_held.at[t - 1], late_sem.at[t - 1])
        )
    for copy in late:
        copy.start()
    begin(1)
    block = block_ref[...]
    for t in range(frames):
        keep = mask_ref[t : t + 1, :].astype(F32)
        cosine = (block[:, :half].astype(F32) * keep).astype(BF16).T
        sine_part = (block[:, half:].astype(F32) * keep).astype(BF16).T
        back[t, :half, :half] = cosine
        back[t, :half, half:] = -sine_part
        back[t, half:, :half] = sine_part
        back[t, half:, half:] = cosine
        near = dot(block[:quarter], back[t])
        for k in range(2):
            for part in range(2):
                at = part * half
                low, high = near[:, at : at + quarter], near[:, at + quarter : at + half]
                table = (0.5 * (low + high if k == 0 else low - high)).astype(BF16)
                normal_ref[t, k, :, part * quarter : (part + 1) * quarter] = table
        if t == 0:
            begin(2)
    own_left = sum(part == 1 for part, _, _ in plan)
    leaving = pltpu.make_async_copy(own_held, own_ref, own_sem)
    for step, (part, at, size) in enumerate(plan):
        if step:
            begin(step + 2)
            for copy in fetch(step):
                copy.wait()
            kspace_held, sens_held = pieces[step - 1][:2]
        else:
            kspace_held = [kspace_first_ref] + [late_held.at[t] for t in range(frames - 1)]
            sens_held = first_ref.at[:, :size]
        sens = sens_held[...].astype(F32)
        sens_r, sens_i = sens[..., :half], sens[..., half:]
        for t in range(frames):
            if step == 0 and t:
                late[t - 1].wait()
            kspace = kspace_held[t][...] if step == 0 else kspace_held[t]
            adjoint = dot(kspace.reshape(coils * size, width), back[t])
            real, imag = conj_sum(adjoint.reshape(coils, size, width), sens_r, sens_i)
            if part:
                group = slice(at // per, (at + size) // per)
                own_held[group, t, :, :half] = real.reshape(size // per, per, half)
                own_held[group, t, :, half:] = imag.reshape(size // per, per, half)
            else:
                other_ref[t, at : at + size, :half] = real
                other_ref[t, at : at + size, half:] = imag
        own_left -= part
        if part and own_left == 0:
            leaving.start()
    leaving.wait()


def normal_kernel(part, begin, end, following, starts_ref, image_ref, first_ref, sens_ref, normal_ref, *rest):
    data_ref = rest[0] if part == 0 else None
    rest = list(rest[1:]) if part == 0 or begin else list(rest)
    if following:
        out_ref, next_ref, table, sens_held, sem, next_sem = rest
    else:
        out_ref, table, sens_held, sem = rest
    _, frames, per, width = image_ref.shape
    coils, tile, _ = first_ref.shape
    half = width // 2
    quarter = half // 2
    step_groups = tile // per
    steps = (end - begin) // tile

    def spot(which, at):
        return pl.ds(pl.multiple_of(starts_ref[which] + at, tile), tile)

    def fetch(step):
        source = sens_ref.at[:, spot(part, begin + step * tile)]
        return pltpu.make_async_copy(source, sens_held.at[step - 1], sem.at[step - 1])

    for step in range(1, steps):
        fetch(step).start()
    if following:
        staging = pltpu.make_async_copy(sens_ref.at[:, spot(*following)], next_ref, next_sem)
        staging.start()
    for t in range(frames):
        for k in range(2):
            near = normal_ref[t, k]
            table[t, k, :quarter] = near
            table[t, k, quarter:, :quarter] = -near[:, quarter:]
            table[t, k, quarter:, quarter:] = near[:, :quarter]

    def work(step, sens):
        place = pl.ds(begin + step * tile, tile)
        group = pl.ds(begin // per + step * step_groups, step_groups)
        sens = sens.astype(F32)
        sens_r, sens_i = sens[..., :half], sens[..., half:]
        for t in range(frames):
            image = image_ref[group, t].reshape(tile, width).astype(F32)
            image_r, image_i = image[:, :half], image[:, half:]
            coil_r = sens_r * image_r - sens_i * image_i
            coil_i = sens_r * image_i + sens_i * image_r
            low_r, high_r = coil_r[..., :quarter], coil_r[..., quarter:]
            low_i, high_i = coil_i[..., :quarter], coil_i[..., quarter:]
            plus = jnp.concatenate([low_r + high_r, low_i + high_i], -1).astype(BF16)
            minus = jnp.concatenate([low_r - high_r, low_i - high_i], -1).astype(BF16)
            plus = dot(plus.reshape(coils * tile, half), table[t, 0]).reshape(coils, tile, half)
            minus = dot(minus.reshape(coils * tile, half), table[t, 1]).reshape(coils, tile, half)
            for k, both in enumerate((plus + minus, plus - minus)):
                lanes = slice(k * quarter, (k + 1) * quarter)
                real, imag = conj_sum(both, sens_r[..., lanes], sens_i[..., lanes])
                low = slice(k * quarter, (k + 1) * quarter)
                high = slice(half + k * quarter, half + (k + 1) * quarter)
                if part == 0:
                    real = real - data_ref[t, place, low]
                    imag = imag - data_ref[t, place, high]
                out_ref[group, t, :, low] = real.reshape(step_groups, per, quarter)
                out_ref[group, t, :, high] = imag.reshape(step_groups, per, quarter)

    work(0, first_ref[...])

    @pl.loop(1, steps)
    def _(step):
        fetch(step).wait()
        work(step, sens_held[step - 1])

    if following:
        staging.wait()


def cost(flops, moved):
    return pl.CostEstimate(flops=int(flops), bytes_accessed=int(moved), transcendentals=0)


VMEM = pl.BlockSpec(memory_space=pltpu.VMEM)
SMEM = pl.BlockSpec(memory_space=pltpu.SMEM)
HBM = pl.BlockSpec(memory_space=pltpu.HBM)
MIB = 1 << 20


def local(array):
    return pltpu.with_memory_space_constraint(array, pltpu.VMEM)


def remote(array):
    return pltpu.with_memory_space_constraint(array, pltpu.HBM)


def grant(mib):
    return pltpu.CompilerParams(vmem_limit_bytes=mib * MIB)


def stage(starts, sampled, block, spatial, sens, kspace, tile):
    _, coils, _, width = kspace.shape
    return pl.pallas_call(
        stage_kernel,
        in_specs=[SMEM] + [HBM] * 5,
        out_specs=[VMEM] * 5,
        out_shape=[
            pltpu.VMEM(sampled.shape, jnp.int32),
            pltpu.VMEM(block.shape, BF16),
            pltpu.VMEM(spatial.shape, BF16),
            pltpu.VMEM((coils, 2 * tile, width), BF16),
            pltpu.VMEM((coils, tile, width), BF16),
        ],
        scratch_shapes=[pltpu.SemaphoreType.DMA((5,))],
        cost_estimate=cost(0, 8 * block.size),
        compiler_params=grant(12),
        name="stage",
    )(starts, remote(sampled), remote(block), remote(spatial), remote(sens), remote(kspace))


def data_term(starts, mask, block, first, kspace_first, kspace, sens, per):
    frames, coils, rows, width = kspace.shape
    own = (rows // 2 // per, frames, per, width)
    plan = data_plan(rows // 2, kspace_first.shape[1])
    scratch = [
        pltpu.VMEM((frames, width, width), BF16),
        pltpu.VMEM(own, F32),
        pltpu.SemaphoreType.DMA,
        pltpu.VMEM((max(frames - 1, 1), coils, plan[0][2], width), BF16),
        pltpu.SemaphoreType.DMA((max(frames - 1, 1),)),
    ]
    for _, _, size in plan[1:]:
        scratch += [
            pltpu.VMEM((frames, coils, size, width), BF16),
            pltpu.VMEM((coils, size, width), BF16),
            pltpu.SemaphoreType.DMA((frames,)),
            pltpu.SemaphoreType.DMA,
        ]
    return pl.pallas_call(
        functools.partial(data_kernel, plan),
        in_specs=[SMEM] + [VMEM] * 4 + [HBM] * 2,
        out_specs=[VMEM, VMEM, HBM],
        out_shape=[
            pltpu.VMEM((frames, 2, width // 4, width // 2), BF16),
            pltpu.VMEM((frames, rows // 2, width), F32),
            pltpu.HBM(own, F32),
        ],
        scratch_shapes=scratch,
        cost_estimate=cost(2 * frames * coils * rows * width * width, 2 * kspace.size),
        compiler_params=grant(36),
        name="data_term",
    )(starts, mask, block, first, kspace_first, remote(kspace), remote(sens))


def normal_term(part, begin, end, following, starts, image, first, sens, normal, more=()):
    groups, frames, per, width = image.shape
    coils, tile, _ = first.shape
    steps = (end - begin) // tile
    spare = max(steps - 1, 1)
    outs = [pltpu.VMEM((groups, frames, per, width), F32)]
    scratch = [
        pltpu.VMEM((frames, 2, width // 2, width // 2), BF16),
        pltpu.VMEM((spare, coils, tile, width), BF16),
        pltpu.SemaphoreType.DMA((spare,)),
    ]
    if following:
        outs.append(pltpu.VMEM(first.shape, BF16))
        scratch.append(pltpu.SemaphoreType.DMA)
    return pl.pallas_call(
        functools.partial(normal_kernel, part, begin, end, following),
        in_specs=[SMEM, VMEM, VMEM, HBM, VMEM] + [VMEM] * len(more),
        out_specs=[VMEM] * len(outs),
        out_shape=outs,
        scratch_shapes=scratch,
        input_output_aliases={5: 0} if part and begin else {},
        cost_estimate=cost(
            frames * coils * (end - begin) * width * width, coils * (end - begin) * width * 2
        ),
        compiler_params=grant(32),
        name="normal_term",
    )(starts, image, first, remote(sens), normal, *more)


def on_device(frame_size, coil_size, spatial, temporal, kspace, sampled, sensitivity):
    rows, rank, width = spatial.shape
    per = temporal.shape[0]
    total = per * frame_size
    half_rows = rows * frame_size
    swap = [(i, (i + 1) % coil_size) for i in range(coil_size)]
    own = lax.axis_index("coil") * half_rows
    starts = jnp.stack([(own + half_rows) % (coil_size * half_rows), own])
    spatial2 = spatial.reshape(rows * rank, width)

    factors = lax.all_to_all(
        jnp.broadcast_to(temporal[None], (frame_size, per, 2 * rank)), "frame", 0, 0, tiled=True
    )
    mask, block, near, first, kspace_first = stage(
        starts, sampled, jnp.asarray(dft_half(width // 2)), spatial2, sensitivity, kspace, 32
    )
    image = image_rows(total, rows, rank, factors, near)
    image, kspace = lax.optimization_barrier((image, kspace))
    image = lax.all_to_all(image.reshape(frame_size, per, rows, width), "frame", 0, 0, tiled=True)
    regroup = rows % 16 != 0
    normal, data_other, data_own = data_term(
        starts, mask, block, first, kspace_first, kspace, sensitivity, 16 if regroup else rows
    )
    image, normal = lax.optimization_barrier((image, normal))
    if regroup:
        image = image.transpose(1, 0, 2, 3).reshape(per, half_rows // 16, 16, width).transpose(1, 0, 2, 3)
    image_other = lax.ppermute(image, "coil", swap)
    middle = half_rows // 2
    image = local(image)
    keep_own, first = normal_term(1, 0, middle, (0, 0), starts, image, first, sensitivity, normal)
    image_other, keep_own = lax.optimization_barrier((image_other, keep_own))
    send, first = normal_term(
        0, 0, half_rows, (1, middle), starts, local(image_other), first, sensitivity, normal, (data_other,)
    )
    received = lax.ppermute(send, "coil", swap)
    (keep_own,) = normal_term(
        1, middle, half_rows, None, starts, image, first, sensitivity, normal, (keep_own,)
    )
    grad = (keep_own + received - data_own).astype(BF16)
    if regroup:
        grad = grad.transpose(1, 0, 2, 3).reshape(per, frame_size, rows, width).transpose(1, 0, 2, 3)
    grad = lax.all_to_all(grad, "frame", 0, 0, tiled=True).reshape(total * rows, width)
    grad = local(grad)

    partial = pl.pallas_call(
        functools.partial(temporal_kernel, total, rows, rank),
        in_specs=[VMEM, VMEM],
        out_specs=VMEM,
        out_shape=pltpu.VMEM((frame_size * coil_size, 1, per * 2 * rank), F32),
        compiler_params=grant(12),
        name="temporal_rows",
    )(local(spatial2), grad)
    partial = lax.all_to_all(partial, ("frame", "coil"), 0, 0, tiled=True)
    spatial_grad = pl.pallas_call(
        functools.partial(spatial_kernel, total, rows, rank),
        in_specs=[VMEM, VMEM],
        out_specs=VMEM,
        out_shape=jax.ShapeDtypeStruct((rows * rank, width), F32),
        compiler_params=grant(12),
        name="spatial_rows",
    )(local(factors), grad)
    temporal_grad = pl.pallas_call(
        sum_kernel,
        in_specs=[VMEM],
        out_specs=VMEM,
        out_shape=jax.ShapeDtypeStruct((per, 2 * rank), F32),
        compiler_params=grant(2),
        name="temporal_sum",
    )(partial)
    return (spatial_grad.reshape(rows, rank, width), temporal_grad)


def solution(mesh):
    placed = (
        P(("cuts", "coil", "frame"), None, None),
        P(("cuts", "frame"), None),
        P(("cuts", "frame"), "coil", None, None),
        P(("cuts", "frame"), None),
        P(("cuts", "coil"), None, None),
    )
    return jax.shard_map(
        functools.partial(on_device, mesh.shape["frame"], mesh.shape["coil"]),
        mesh=mesh,
        in_specs=placed,
        out_specs=(P(("cuts", "coil", "frame"), None, None), P(("cuts", "frame"), None)),
        check_vma=False,
    )
```

```python
import functools
import math

import jax
import jax.numpy as jnp
import numpy as np
from jax import lax
from jax.experimental import pallas as pl
from jax.experimental.pallas import tpu as pltpu
from jax.sharding import PartitionSpec as P


F32 = jnp.float32
BF16 = jnp.bfloat16


def dft_tables(length):
    index = np.arange(length)
    angles = (index[:, None] * index[None, :] % length) * (2.0 * math.pi / length)
    cosine = np.cos(angles) / math.sqrt(length)
    sine_part = -np.sin(angles) / math.sqrt(length)
    block = np.block([[cosine, sine_part], [-sine_part, cosine]]).astype(np.float32)
    middle = length // 2
    left, right = [], []
    for odd in range(2):
        lines = np.concatenate([index[odd::2], length + index[odd::2]])
        near = np.concatenate([index[:middle], length + index[:middle]])
        left.append(block[:middle][:, lines])
        right.append(block.T[lines][:, near])
    order = np.concatenate([index[0::2], index[1::2]])
    picks = (index[:, None] == order[None, :]).astype(np.float32)
    return [np.asarray(a).astype(BF16) for a in (block[:length], np.stack(left), np.stack(right), picks)]


def dot(a, b):
    return jnp.dot(a, b, preferred_element_type=F32)


def dot_t(a, b):
    return lax.dot_general(a, b, (((1,), (1,)), ((), ())), preferred_element_type=F32)


def iota(shape, axis):
    return lax.broadcasted_iota(jnp.int32, shape, axis)


def spread(factors_ref, total, rows, rank):
    groups, per, lanes = factors_ref.shape
    height = 2 * total * rows
    frame = iota((height, groups), 0) // rows % total
    factors = factors_ref[...].astype(F32)
    picked = jnp.zeros((height, lanes), F32)
    for t in range(per):
        pick = jnp.where(frame == iota((height, groups), 1) * per + t, 1.0, 0.0).astype(BF16)
        picked = picked + dot(pick, factors[:, t].astype(BF16))
    mine = iota((height, lanes), 1) // rank == iota((height, lanes), 0) // (total * rows)
    return jnp.where(mine, picked, 0.0).astype(BF16)


def image_kernel(total, rows, rank, factors_ref, spatial_ref, image_ref):
    mid = spread(factors_ref, total, rows, rank)
    lanes = mid.shape[1]
    width = rows * rank
    tile = jnp.where(iota((lanes, width), 0) % rank == iota((lanes, width), 1) % rank, 1.0, 0.0)
    wide = dot(mid, tile.astype(BF16))
    height = wide.shape[0]
    same = iota((height, width), 0) % rows == iota((height, width), 1) // rank
    wide = jnp.where(same, wide, 0.0).astype(BF16)
    product = dot(wide, spatial_ref[...])
    half = height // 2
    mid_col = product.shape[1] // 2
    image_ref[:, :mid_col] = (product[:half, :mid_col] - product[half:, mid_col:]).astype(BF16)
    image_ref[:, mid_col:] = (product[:half, mid_col:] + product[half:, :mid_col]).astype(BF16)


def image_block_kernel(total, rows, rank, factors_ref, spatial_ref, image_ref, wide, held, sems):
    groups, per, lanes = factors_ref.shape
    width = rows * rank
    half = total * rows
    source = iota((lanes, 2 * width), 1)
    source = source // width * rank + source % rank
    tile = jnp.where(iota((lanes, 2 * width), 0) == source, 1.0, 0.0).astype(BF16)
    same = iota((rows, width), 0) == iota((rows, width), 1) // rank
    factors = factors_ref[...].astype(F32)
    for t in range(per):
        lines = dot(factors[:, t].astype(BF16), tile)
        for group in range(groups):
            for part in range(2):
                line = lines[group : group + 1, part * width : (part + 1) * width]
                at = part * half + (group * per + t) * rows
                wide[at : at + rows] = jnp.where(same, line, 0.0).astype(BF16)
    spatial = spatial_ref[...]
    mid = spatial.shape[1] // 2
    copies = []
    for piece in range(2):
        place = slice(piece * half // 2, (piece + 1) * half // 2)
        real = dot(wide[place], spatial)
        imag = dot(wide[half + place.start : half + place.stop], spatial)
        held[place, :mid] = (real[:, :mid] - imag[:, mid:]).astype(BF16)
        held[place, mid:] = (real[:, mid:] + imag[:, :mid]).astype(BF16)
        copies.append(pltpu.make_async_copy(held.at[place], image_ref.at[place], sems.at[piece]))
        copies[-1].start()
    for copy in copies:
        copy.wait()


def image_rows(total, rows, rank, factors, spatial):
    shape = (total * rows, spatial.shape[1])
    if rows % 16:
        body, outs, space, scratch = image_kernel, pltpu.VMEM(shape, BF16), VMEM, []
    else:
        body, outs, space = image_block_kernel, pltpu.HBM(shape, BF16), HBM
        scratch = [
            pltpu.VMEM((2 * total * rows, rows * rank), BF16),
            pltpu.VMEM(shape, BF16),
            pltpu.SemaphoreType.DMA((2,)),
        ]
    return pl.pallas_call(
        functools.partial(body, total, rows, rank),
        in_specs=[VMEM, VMEM],
        out_specs=space,
        out_shape=outs,
        scratch_shapes=scratch,
        compiler_params=grant(12),
        name="image_rows",
    )(local(factors), spatial)


def both_parts(grad):
    half = grad.shape[1] // 2
    turned = jnp.concatenate([grad[:, half:], -grad[:, :half]], 1)
    return jnp.concatenate([grad, turned], 0)


def spatial_kernel(total, rows, rank, factors_ref, grad_ref, out_ref):
    mid = spread(factors_ref, total, rows, rank)
    lanes = mid.shape[1]
    width = rows * rank
    tile = jnp.where(iota((width, lanes), 0) % rank == iota((width, lanes), 1) % rank, 1.0, 0.0)
    wide = dot_t(tile.astype(BF16), mid)
    height = mid.shape[0]
    same = iota((width, height), 1) % rows == iota((width, height), 0) // rank
    wide = jnp.where(same, wide, 0.0).astype(BF16)
    out_ref[...] = dot(wide, both_parts(grad_ref[...]))


def temporal_kernel(total, rows, rank, spatial_ref, grad_ref, out_ref):
    product = dot_t(both_parts(grad_ref[...]), spatial_ref[...])
    height, width = product.shape
    same = iota((height, width), 0) % rows == iota((height, width), 1) // rank
    product = jnp.where(same, product, 0.0)
    lanes = 128
    fold = product[:, :lanes]
    for start in range(lanes, width, lanes):
        fold = fold + product[:, start : start + lanes]
    if rows % 8 == 0:
        fold = jnp.sum(fold.reshape(2 * total, rows, lanes), axis=1)
    else:
        pick = iota((2 * total, height), 0) == iota((2 * total, height), 1) // rows
        fold = jnp.dot(
            jnp.where(pick, 1.0, 0.0), fold, precision=lax.Precision.HIGHEST, preferred_element_type=F32
        )
    shift = lanes // 2
    while shift >= rank:
        fold = fold + pltpu.roll(fold, shift, 1)
        shift //= 2
    lane = iota((total, lanes), 1)
    both = jnp.where(lane // rank % 2 == 0, fold[:total], fold[total:])
    groups, _, span = out_ref.shape
    per = span // (2 * rank)
    copies = groups * per // total
    place = iota((1, span), 1) // (2 * rank)
    for group in range(groups // copies):
        line = both[group * per : group * per + 1, :span]
        for t in range(1, per):
            line = jnp.where(place == t, both[group * per + t : group * per + t + 1, :span], line)
        for copy in range(copies):
            out_ref[group * copies + copy] = line


def sum_kernel(parts_ref, out_ref):
    line = jnp.sum(parts_ref[...], axis=0)
    per, span = out_ref.shape
    for t in range(per):
        out_ref[t : t + 1, :] = line[:, t * span : (t + 1) * span]


def conj_sum(adjoint, sens_r, sens_i):
    half = sens_r.shape[-1]
    back_r, back_i = adjoint[..., :half], adjoint[..., half:]
    return (
        jnp.sum(sens_r * back_r + sens_i * back_i, axis=0),
        jnp.sum(sens_r * back_i - sens_i * back_r, axis=0),
    )


def data_plan(rows, tile):
    own = [(1, at, tile) for at in range(0, rows // 2, tile)]
    return own + [(0, 0, tile), (1, rows // 2, rows // 2), (0, tile, rows - tile)]


def data_kernel(plan, starts_ref, sampled_ref, block_ref, spatial_ref, kspace_ref, sens_ref,
                other_ref, own_ref, spatial_out, mask, block, back, sems, *held):
    frames, coils, _, width = kspace_ref.shape
    _, _, per, _ = own_ref.shape
    half = width // 2
    pieces = [held[4 * k : 4 * k + 4] for k in range(len(plan))]

    def begin(step):
        if step < len(plan):
            for copy in fetch(step):
                copy.start()

    def fetch(step):
        part, at, size = plan[step]
        kspace_held, sens_held, kspace_sem, sens_sem = pieces[step]
        place = pl.ds(pl.multiple_of(starts_ref[part] + at, plan[0][2]), size)
        return (
            pltpu.make_async_copy(sens_ref.at[:, place], sens_held, sens_sem),
            pltpu.make_async_copy(kspace_ref.at[:, :, place], kspace_held, kspace_sem),
        )

    tables = [
        pltpu.make_async_copy(sampled_ref, mask, sems.at[0]),
        pltpu.make_async_copy(block_ref, block, sems.at[1]),
    ]
    staging = [pltpu.make_async_copy(spatial_ref, spatial_out, sems.at[2])]
    for copy in tables:
        copy.start()
    begin(0)
    for copy in tables:
        copy.wait()
    begin(1)
    for t in range(frames):
        keep = mask[t : t + 1, :].astype(F32)
        cosine = (block[:, :half].astype(F32) * keep).astype(BF16).T
        sine_part = (block[:, half:].astype(F32) * keep).astype(BF16).T
        back[t, :half, :half] = cosine
        back[t, :half, half:] = -sine_part
        back[t, half:, :half] = sine_part
        back[t, half:, half:] = cosine
    for step, (part, at, size) in enumerate(plan):
        begin(step + 2)
        if step == 1:
            for copy in staging:
                copy.start()
        for copy in fetch(step):
            copy.wait()
        kspace_held, sens_held = pieces[step][:2]
        sens = sens_held[...].astype(F32)
        sens_r, sens_i = sens[..., :half], sens[..., half:]
        out_ref = own_ref if part else other_ref
        group = slice(at // per, (at + size) // per)
        for t in range(frames):
            adjoint = dot(kspace_held[t].reshape(coils * size, width), back[t])
            real, imag = conj_sum(adjoint.reshape(coils, size, width), sens_r, sens_i)
            out_ref[group, t, :, :half] = real.reshape(size // per, per, half)
            out_ref[group, t, :, half:] = imag.reshape(size // per, per, half)
    for copy in staging:
        copy.wait()


def normal_kernel(starts_ref, message_ref, own_ref, other_ref, sens_ref, left_ref, right_ref, picks_ref,
                  own_out, other_out, masks, table, wide, held, sems):
    groups, per, _ = message_ref.shape
    _, coils, rows, width = held.shape
    copies = []
    for part in range(2):
        place = pl.ds(pl.multiple_of(starts_ref[2 + part], rows), rows)
        copies.append(pltpu.make_async_copy(sens_ref.at[:, place], held.at[part], sems.at[part]))
        copies[part].start()
    half = width // 2
    quarter = half // 2
    message = message_ref[...].astype(F32)
    for t in range(per):
        masks[t] = dot(message[:, t, :half].astype(BF16), picks_ref[...])

    @pl.loop(0, groups)
    def _(group):
        for t in range(per):
            keep = masks[t, pl.ds(group, 1), :]
            for k in range(2):
                lines = keep[:, k * quarter : (k + 1) * quarter]
                left = (left_ref[k].astype(F32) * jnp.concatenate([lines, lines], 1)).astype(BF16)
                near = dot(left, right_ref[k]).astype(BF16)
                table[group, t, k, :quarter] = near
                table[group, t, k, quarter:, :quarter] = -near[:, quarter:]
                table[group, t, k, quarter:, quarter:] = near[:, :quarter]

    for copy in copies:
        copy.wait()
    wide[...] = held[...].astype(F32)

    @pl.loop(0, groups)
    def _(group):
        for t in range(per):
            place = pl.ds(pl.multiple_of((group * per + t) * rows, rows), rows)
            plus, minus = [], []
            for part, image_ref in enumerate((own_ref, other_ref)):
                image = image_ref[place, :].astype(F32)
                image_r, image_i = image[:, :half], image[:, half:]
                sens_r, sens_i = wide[part, :, :, :half], wide[part, :, :, half:]
                coil_r = sens_r * image_r - sens_i * image_i
                coil_i = sens_r * image_i + sens_i * image_r
                low_r, high_r = coil_r[..., :quarter], coil_r[..., quarter:]
                low_i, high_i = coil_i[..., :quarter], coil_i[..., quarter:]
                shape = (coils * rows, half)
                plus.append(jnp.concatenate([low_r + high_r, low_i + high_i], -1).astype(BF16).reshape(shape))
                minus.append(jnp.concatenate([low_r - high_r, low_i - high_i], -1).astype(BF16).reshape(shape))
            shape = (2, coils, rows, half)
            plus = dot(jnp.concatenate(plus, 0), table[group, t, 0]).reshape(shape)
            minus = dot(jnp.concatenate(minus, 0), table[group, t, 1]).reshape(shape)
            for k, both in enumerate((plus + minus, plus - minus)):
                low = slice(k * quarter, (k + 1) * quarter)
                high = slice(half + k * quarter, half + (k + 1) * quarter)
                for part, out_ref in enumerate((own_out, other_out)):
                    real, imag = conj_sum(both[part], wide[part, :, :, low], wide[part, :, :, high])
                    out_ref[place, low] = real
                    out_ref[place, high] = imag


def normal_plain(message, images, sens, left, right):
    half = left.shape[2]
    quarter = half // 2
    flat = message.reshape(-1, message.shape[-1])[:, :half]
    frames = flat.shape[0]
    outs = []
    for image, own in zip(images, sens):
        image = image.reshape(frames, 1, -1, 2 * half).astype(F32)
        own = own.astype(F32)[None]
        coil_r = own[..., :half] * image[..., :half] - own[..., half:] * image[..., half:]
        coil_i = own[..., :half] * image[..., half:] + own[..., half:] * image[..., :half]
        low = [coil_r[..., :quarter], coil_i[..., :quarter]]
        high = [coil_r[..., quarter:], coil_i[..., quarter:]]
        sums = []
        for k, sign in enumerate((1, -1)):
            lines = flat[:, k::2]
            keep = jnp.concatenate([lines, lines], 1)
            near = jnp.einsum("yk,tk,kz->tyz", left[k], keep, right[k], preferred_element_type=F32)
            turned = jnp.concatenate([-near[..., quarter:], near[..., :quarter]], -1)
            table = jnp.concatenate([near, turned], 1).astype(BF16)
            mixed = jnp.concatenate([a + sign * b for a, b in zip(low, high)], -1).astype(BF16)
            sums.append(jnp.einsum("tcxy,tyz->tcxz", mixed, table, preferred_element_type=F32))
        both = [sums[0] + sums[1], sums[0] - sums[1]]
        real = jnp.concatenate([b[..., :quarter] for b in both], -1)
        imag = jnp.concatenate([b[..., quarter:] for b in both], -1)
        out_r = jnp.sum(own[..., :half] * real + own[..., half:] * imag, 1)
        out_i = jnp.sum(own[..., :half] * imag - own[..., half:] * real, 1)
        outs.append(jnp.concatenate([out_r, out_i], -1).reshape(-1, 2 * half))
    return outs


def cost(flops, moved):
    return pl.CostEstimate(flops=int(flops), bytes_accessed=int(moved), transcendentals=0)


VMEM = pl.BlockSpec(memory_space=pltpu.VMEM)
SMEM = pl.BlockSpec(memory_space=pltpu.SMEM)
HBM = pl.BlockSpec(memory_space=pltpu.HBM)
MIB = 1 << 20


def local(array):
    return pltpu.with_memory_space_constraint(array, pltpu.VMEM)


def remote(array):
    return pltpu.with_memory_space_constraint(array, pltpu.HBM)


def grant(mib):
    return pltpu.CompilerParams(vmem_limit_bytes=mib * MIB)


def data_term(starts, sampled, block, spatial, kspace, sens, per):
    frames, coils, rows, width = kspace.shape
    own = (rows // 2 // per, frames, per, width)
    plan = data_plan(rows // 2, 32)
    scratch = [
        pltpu.VMEM(sampled.shape, jnp.int32),
        pltpu.VMEM(block.shape, BF16),
        pltpu.VMEM((frames, width, width), BF16),
        pltpu.SemaphoreType.DMA((3,)),
    ]
    for _, _, size in plan:
        scratch += [
            pltpu.VMEM((frames, coils, size, width), BF16),
            pltpu.VMEM((coils, size, width), BF16),
            pltpu.SemaphoreType.DMA,
            pltpu.SemaphoreType.DMA,
        ]
    return pl.pallas_call(
        functools.partial(data_kernel, plan),
        in_specs=[SMEM] + [HBM] * 5,
        out_specs=[VMEM] * 3,
        out_shape=[
            pltpu.VMEM(own, F32),
            pltpu.VMEM(own, F32),
            pltpu.VMEM(spatial.shape, BF16),
        ],
        scratch_shapes=scratch,
        cost_estimate=cost(2 * frames * coils * rows * width * width, 2 * kspace.size),
        compiler_params=grant(44),
        name="data_term",
    )(starts, remote(sampled), remote(block), remote(spatial), remote(kspace), remote(sens))


def normal_term(starts, message, own, other, sens, left, right, picks):
    groups, per, _ = message.shape
    coils, _, width = sens.shape
    rows = own.shape[0] // (groups * per)
    half = width // 2
    return pl.pallas_call(
        normal_kernel,
        in_specs=[SMEM] + [VMEM] * 3 + [HBM] + [VMEM] * 3,
        out_specs=[VMEM] * 2,
        out_shape=[pltpu.VMEM(own.shape, F32)] * 2,
        scratch_shapes=[
            pltpu.VMEM((per, groups, half), F32),
            pltpu.VMEM((groups, per, 2, half, half), BF16),
            pltpu.VMEM((2, coils, rows, width), F32),
            pltpu.VMEM((2, coils, rows, width), BF16),
            pltpu.SemaphoreType.DMA((2,)),
        ],
        cost_estimate=cost(2 * groups * per * coils * rows * width * width, 4 * own.size),
        compiler_params=grant(40),
        name="normal_term",
    )(starts, message, local(own), local(other), remote(sens), local(left), local(right), local(picks))


def on_device(frame_size, coil_size, spatial, temporal, kspace, sampled, sensitivity):
    rows, rank, width = spatial.shape
    per = temporal.shape[0]
    total = per * frame_size
    half_rows = rows * frame_size
    half = width // 2
    swap = [(i, (i + 1) % coil_size) for i in range(coil_size)]
    own = lax.axis_index("coil") * half_rows
    other = (own + half_rows) % (coil_size * half_rows)
    row = lax.axis_index("frame") * rows
    starts = jnp.stack([other, own, own + row, other + row])
    spatial2 = spatial.reshape(rows * rank, width)
    block, left, right, picks = [jnp.asarray(table) for table in dft_tables(half)]

    message = jnp.concatenate([sampled.astype(BF16), temporal], 1)
    message = lax.all_to_all(
        jnp.broadcast_to(message[None], (frame_size, *message.shape)), "frame", 0, 0, tiled=True
    )
    regroup = rows % 16 != 0
    data_other, data_own, near = data_term(
        starts, sampled, block, spatial2, kspace, sensitivity, 16 if regroup else rows
    )
    message, data_other = lax.optimization_barrier((message, data_other))
    received = lax.ppermute(data_other, "coil", swap)
    image = image_rows(total, rows, rank, message[:, :, half:], near)
    image_other = lax.ppermute(image, "coil", swap)
    data = (data_own + received).astype(BF16)
    if regroup:
        data = data.transpose(1, 0, 2, 3).reshape(per, frame_size, rows, width).transpose(1, 0, 2, 3)
    image, image_other, data = lax.optimization_barrier((image, image_other, data))
    data = lax.all_to_all(data, "frame", 0, 0, tiled=True)
    data = data.reshape(total * rows, width)
    if regroup:
        sens = [lax.dynamic_slice_in_dim(sensitivity, at + row, rows, 1) for at in (own, other)]
        keep_own, send = normal_plain(message, (image, image_other), sens, left, right)
    else:
        keep_own, send = normal_term(starts, message, image, image_other, sensitivity, left, right, picks)
    grad = (keep_own + lax.ppermute(send, "coil", swap) - data.astype(F32)).astype(BF16)
    grad = local(grad)

    partial = pl.pallas_call(
        functools.partial(temporal_kernel, total, rows, rank),
        in_specs=[VMEM, VMEM],
        out_specs=VMEM,
        out_shape=pltpu.VMEM((frame_size * coil_size, 1, per * 2 * rank), F32),
        compiler_params=grant(12),
        name="temporal_rows",
    )(local(spatial2), grad)
    partial = lax.all_to_all(partial, ("frame", "coil"), 0, 0, tiled=True)
    spatial_grad = pl.pallas_call(
        functools.partial(spatial_kernel, total, rows, rank),
        in_specs=[VMEM, VMEM],
        out_specs=VMEM,
        out_shape=jax.ShapeDtypeStruct((rows * rank, width), F32),
        compiler_params=grant(12),
        name="spatial_rows",
    )(local(message[:, :, half:]), grad)
    temporal_grad = pl.pallas_call(
        sum_kernel,
        in_specs=[VMEM],
        out_specs=VMEM,
        out_shape=jax.ShapeDtypeStruct((per, 2 * rank), F32),
        compiler_params=grant(2),
        name="temporal_sum",
    )(partial)
    return (spatial_grad.reshape(rows, rank, width), temporal_grad)


def solution(mesh):
    placed = (
        P(("cuts", "coil", "frame"), None, None),
        P(("cuts", "frame"), None),
        P(("cuts", "frame"), "coil", None, None),
        P(("cuts", "frame"), None),
        P(("cuts", "coil"), None, None),
    )

    def body(*arrays):
        return on_device(mesh.shape["frame"], mesh.shape["coil"], *arrays)

    return jax.shard_map(
        body,
        mesh=mesh,
        in_specs=placed,
        out_specs=(P(("cuts", "coil", "frame"), None, None), P(("cuts", "frame"), None)),
        check_vma=False,
    )
```

```python
import functools
import math

import jax
import jax.numpy as jnp
import numpy as np
from jax import lax
from jax.experimental import pallas as pl
from jax.experimental.pallas import tpu as pltpu
from jax.sharding import PartitionSpec as P


F32 = jnp.float32
BF16 = jnp.bfloat16


def dft_tables(length):
    index = np.arange(length)
    angles = (index[:, None] * index[None, :] % length) * (2.0 * math.pi / length)
    cosine = np.cos(angles) / math.sqrt(length)
    sine_part = -np.sin(angles) / math.sqrt(length)
    block = np.block([[cosine, sine_part], [-sine_part, cosine]]).astype(np.float32)
    middle = length // 2
    left, right = [], []
    for odd in range(2):
        lines = np.concatenate([index[odd::2], length + index[odd::2]])
        near = np.concatenate([index[:middle], length + index[:middle]])
        left.append(block[:middle][:, lines])
        right.append(block.T[lines][:, near])
    order = np.concatenate([index[0::2], index[1::2]])
    picks = (index[:, None] == order[None, :]).astype(np.float32)
    return [np.asarray(a).astype(BF16) for a in (block[:length], np.stack(left), np.stack(right), picks)]


def dot(a, b):
    return jnp.dot(a, b, preferred_element_type=F32)


def dot_t(a, b):
    return lax.dot_general(a, b, (((1,), (1,)), ((), ())), preferred_element_type=F32)


def iota(shape, axis):
    return lax.broadcasted_iota(jnp.int32, shape, axis)


def spread(factors_ref, total, rows, rank):
    groups, per, lanes = factors_ref.shape
    height = 2 * total * rows
    frame = iota((height, groups), 0) // rows % total
    factors = factors_ref[...].astype(F32)
    picked = jnp.zeros((height, lanes), F32)
    for t in range(per):
        pick = jnp.where(frame == iota((height, groups), 1) * per + t, 1.0, 0.0).astype(BF16)
        picked = picked + dot(pick, factors[:, t].astype(BF16))
    mine = iota((height, lanes), 1) // rank == iota((height, lanes), 0) // (total * rows)
    return jnp.where(mine, picked, 0.0).astype(BF16)


def image_kernel(total, rows, rank, factors_ref, spatial_ref, image_ref):
    mid = spread(factors_ref, total, rows, rank)
    lanes = mid.shape[1]
    width = rows * rank
    tile = jnp.where(iota((lanes, width), 0) % rank == iota((lanes, width), 1) % rank, 1.0, 0.0)
    wide = dot(mid, tile.astype(BF16))
    height = wide.shape[0]
    same = iota((height, width), 0) % rows == iota((height, width), 1) // rank
    wide = jnp.where(same, wide, 0.0).astype(BF16)
    product = dot(wide, spatial_ref[...])
    half = height // 2
    mid_col = product.shape[1] // 2
    image_ref[:, :mid_col] = (product[:half, :mid_col] - product[half:, mid_col:]).astype(BF16)
    image_ref[:, mid_col:] = (product[:half, mid_col:] + product[half:, :mid_col]).astype(BF16)


def image_block_kernel(total, rows, rank, factors_ref, spatial_ref, image_ref, wide):
    groups, per, lanes = factors_ref.shape
    width = rows * rank
    half = total * rows
    source = iota((lanes, 2 * width), 1)
    source = source // width * rank + source % rank
    tile = jnp.where(iota((lanes, 2 * width), 0) == source, 1.0, 0.0).astype(BF16)
    same = iota((rows, width), 0) == iota((rows, width), 1) // rank
    factors = factors_ref[...].astype(F32)
    for t in range(per):
        lines = dot(factors[:, t].astype(BF16), tile)
        for group in range(groups):
            for part in range(2):
                line = lines[group : group + 1, part * width : (part + 1) * width]
                at = part * half + (group * per + t) * rows
                wide[at : at + rows] = jnp.where(same, line, 0.0).astype(BF16)
    spatial = spatial_ref[...]
    mid = spatial.shape[1] // 2
    real = dot(wide[:half], spatial)
    imag = dot(wide[half:], spatial)
    image_ref[:, :mid] = (real[:, :mid] - imag[:, mid:]).astype(BF16)
    image_ref[:, mid:] = (real[:, mid:] + imag[:, :mid]).astype(BF16)


def image_rows(total, rows, rank, factors, spatial):
    shape = (total * rows, spatial.shape[1])
    if rows % 16:
        body, scratch = image_kernel, []
    else:
        body, scratch = image_block_kernel, [pltpu.VMEM((2 * total * rows, rows * rank), BF16)]
    return pl.pallas_call(
        functools.partial(body, total, rows, rank),
        in_specs=[VMEM, VMEM],
        out_specs=VMEM,
        out_shape=pltpu.VMEM(shape, BF16),
        scratch_shapes=scratch,
        compiler_params=grant(12),
        name="image_rows",
    )(local(factors), spatial)


def both_parts(grad):
    half = grad.shape[1] // 2
    turned = jnp.concatenate([grad[:, half:], -grad[:, :half]], 1)
    return jnp.concatenate([grad, turned], 0)


def spatial_kernel(total, rows, rank, factors_ref, grad_ref, out_ref):
    mid = spread(factors_ref, total, rows, rank)
    lanes = mid.shape[1]
    width = rows * rank
    tile = jnp.where(iota((width, lanes), 0) % rank == iota((width, lanes), 1) % rank, 1.0, 0.0)
    wide = dot_t(tile.astype(BF16), mid)
    height = mid.shape[0]
    same = iota((width, height), 1) % rows == iota((width, height), 0) // rank
    wide = jnp.where(same, wide, 0.0).astype(BF16)
    out_ref[...] = dot(wide, both_parts(grad_ref[...]))


def temporal_kernel(total, rows, rank, spatial_ref, grad_ref, out_ref):
    product = dot_t(both_parts(grad_ref[...]), spatial_ref[...])
    height, width = product.shape
    same = iota((height, width), 0) % rows == iota((height, width), 1) // rank
    product = jnp.where(same, product, 0.0)
    lanes = 128
    fold = product[:, :lanes]
    for start in range(lanes, width, lanes):
        fold = fold + product[:, start : start + lanes]
    if rows % 8 == 0:
        fold = jnp.sum(fold.reshape(2 * total, rows, lanes), axis=1)
    else:
        pick = iota((2 * total, height), 0) == iota((2 * total, height), 1) // rows
        fold = jnp.dot(
            jnp.where(pick, 1.0, 0.0), fold, precision=lax.Precision.HIGHEST, preferred_element_type=F32
        )
    shift = lanes // 2
    while shift >= rank:
        fold = fold + pltpu.roll(fold, shift, 1)
        shift //= 2
    lane = iota((total, lanes), 1)
    both = jnp.where(lane // rank % 2 == 0, fold[:total], fold[total:])
    groups, _, span = out_ref.shape
    per = span // (2 * rank)
    copies = groups * per // total
    place = iota((1, span), 1) // (2 * rank)
    for group in range(groups // copies):
        line = both[group * per : group * per + 1, :span]
        for t in range(1, per):
            line = jnp.where(place == t, both[group * per + t : group * per + t + 1, :span], line)
        for copy in range(copies):
            out_ref[group * copies + copy] = line


def sum_kernel(parts_ref, out_ref):
    line = jnp.sum(parts_ref[...], axis=0)
    per, span = out_ref.shape
    for t in range(per):
        out_ref[t : t + 1, :] = line[:, t * span : (t + 1) * span]


def conj_sum(adjoint, sens_r, sens_i):
    half = sens_r.shape[-1]
    back_r, back_i = adjoint[..., :half], adjoint[..., half:]
    return (
        jnp.sum(sens_r * back_r + sens_i * back_i, axis=0),
        jnp.sum(sens_r * back_i - sens_i * back_r, axis=0),
    )


def data_plan(rows, tile):
    own = [(1, at, tile) for at in range(0, rows // 2, tile)]
    return own + [(0, 0, tile), (1, rows // 2, rows // 2), (0, tile, rows - tile)]


def data_kernel(plan, starts_ref, sampled_ref, block_ref, spatial_ref, kspace_ref, sens_ref,
                other_ref, own_ref, spatial_out, mask, block, back, sems, *held):
    frames, coils, _, width = kspace_ref.shape
    _, _, per, _ = own_ref.shape
    half = width // 2
    pieces = [held[4 * k : 4 * k + 4] for k in range(len(plan))]

    def begin(step):
        if step < len(plan):
            for copy in fetch(step):
                copy.start()

    def fetch(step):
        part, at, size = plan[step]
        kspace_held, sens_held, kspace_sem, sens_sem = pieces[step]
        place = pl.ds(pl.multiple_of(starts_ref[part] + at, plan[0][2]), size)
        return (
            pltpu.make_async_copy(sens_ref.at[:, place], sens_held, sens_sem),
            pltpu.make_async_copy(kspace_ref.at[:, :, place], kspace_held, kspace_sem),
        )

    tables = [
        pltpu.make_async_copy(sampled_ref, mask, sems.at[0]),
        pltpu.make_async_copy(block_ref, block, sems.at[1]),
    ]
    staging = [pltpu.make_async_copy(spatial_ref, spatial_out, sems.at[2])]
    for copy in tables:
        copy.start()
    begin(0)
    for copy in tables:
        copy.wait()
    begin(1)
    for t in range(frames):
        keep = mask[t : t + 1, :].astype(F32)
        cosine = (block[:, :half].astype(F32) * keep).astype(BF16).T
        sine_part = (block[:, half:].astype(F32) * keep).astype(BF16).T
        back[t, :half, :half] = cosine
        back[t, :half, half:] = -sine_part
        back[t, half:, :half] = sine_part
        back[t, half:, half:] = cosine
    for step, (part, at, size) in enumerate(plan):
        begin(step + 2)
        if step == 1:
            for copy in staging:
                copy.start()
        for copy in fetch(step):
            copy.wait()
        kspace_held, sens_held = pieces[step][:2]
        sens = sens_held[...].astype(F32)
        sens_r, sens_i = sens[..., :half], sens[..., half:]
        out_ref = own_ref if part else other_ref
        group = slice(at // per, (at + size) // per)
        for t in range(frames):
            adjoint = dot(kspace_held[t].reshape(coils * size, width), back[t])
            real, imag = conj_sum(adjoint.reshape(coils, size, width), sens_r, sens_i)
            out_ref[group, t, :, :half] = real.reshape(size // per, per, half)
            out_ref[group, t, :, half:] = imag.reshape(size // per, per, half)
    for copy in staging:
        copy.wait()


def normal_kernel(starts_ref, message_ref, own_ref, other_ref, sens_ref, left_ref, right_ref, picks_ref,
                  own_out, other_out, masks, table, wide, held, sems):
    groups, per, _ = message_ref.shape
    _, coils, rows, width = held.shape
    copies = []
    for part in range(2):
        place = pl.ds(pl.multiple_of(starts_ref[2 + part], rows), rows)
        copies.append(pltpu.make_async_copy(sens_ref.at[:, place], held.at[part], sems.at[part]))
        copies[part].start()
    half = width // 2
    quarter = half // 2
    message = message_ref[...].astype(F32)
    for t in range(per):
        masks[t] = dot(message[:, t, :half].astype(BF16), picks_ref[...])

    @pl.loop(0, groups, unroll=4)
    def _(group):
        for t in range(per):
            keep = masks[t, pl.ds(group, 1), :]
            for k in range(2):
                lines = keep[:, k * quarter : (k + 1) * quarter]
                left = (left_ref[k].astype(F32) * jnp.concatenate([lines, lines], 1)).astype(BF16)
                near = dot(left, right_ref[k]).astype(BF16)
                table[group, t, k, :quarter] = near
                table[group, t, k, quarter:, :quarter] = -near[:, quarter:]
                table[group, t, k, quarter:, quarter:] = near[:, :quarter]

    for copy in copies:
        copy.wait()
    wide[...] = held[...].astype(F32)

    @pl.loop(0, groups, unroll=2)
    def _(group):
        for t in range(per):
            place = pl.ds(pl.multiple_of((group * per + t) * rows, rows), rows)
            plus, minus = [], []
            for part, image_ref in enumerate((own_ref, other_ref)):
                image = image_ref[place, :].astype(F32)
                image_r, image_i = image[:, :half], image[:, half:]
                sens_r, sens_i = wide[part, :, :, :half], wide[part, :, :, half:]
                coil_r = sens_r * image_r - sens_i * image_i
                coil_i = sens_r * image_i + sens_i * image_r
                low_r, high_r = coil_r[..., :quarter], coil_r[..., quarter:]
                low_i, high_i = coil_i[..., :quarter], coil_i[..., quarter:]
                shape = (coils * rows, half)
                plus.append(jnp.concatenate([low_r + high_r, low_i + high_i], -1).astype(BF16).reshape(shape))
                minus.append(jnp.concatenate([low_r - high_r, low_i - high_i], -1).astype(BF16).reshape(shape))
            shape = (2, coils, rows, half)
            plus = dot(jnp.concatenate(plus, 0), table[group, t, 0]).reshape(shape)
            minus = dot(jnp.concatenate(minus, 0), table[group, t, 1]).reshape(shape)
            for k, both in enumerate((plus + minus, plus - minus)):
                low = slice(k * quarter, (k + 1) * quarter)
                high = slice(half + k * quarter, half + (k + 1) * quarter)
                for part, out_ref in enumerate((own_out, other_out)):
                    real, imag = conj_sum(both[part], wide[part, :, :, low], wide[part, :, :, high])
                    out_ref[place, low] = real
                    out_ref[place, high] = imag


def normal_plain(message, images, sens, left, right):
    half = left.shape[2]
    quarter = half // 2
    flat = message.reshape(-1, message.shape[-1])[:, :half]
    frames = flat.shape[0]
    outs = []
    for image, own in zip(images, sens):
        image = image.reshape(frames, 1, -1, 2 * half).astype(F32)
        own = own.astype(F32)[None]
        coil_r = own[..., :half] * image[..., :half] - own[..., half:] * image[..., half:]
        coil_i = own[..., :half] * image[..., half:] + own[..., half:] * image[..., :half]
        low = [coil_r[..., :quarter], coil_i[..., :quarter]]
        high = [coil_r[..., quarter:], coil_i[..., quarter:]]
        sums = []
        for k, sign in enumerate((1, -1)):
            lines = flat[:, k::2]
            keep = jnp.concatenate([lines, lines], 1)
            near = jnp.einsum("yk,tk,kz->tyz", left[k], keep, right[k], preferred_element_type=F32)
            turned = jnp.concatenate([-near[..., quarter:], near[..., :quarter]], -1)
            table = jnp.concatenate([near, turned], 1).astype(BF16)
            mixed = jnp.concatenate([a + sign * b for a, b in zip(low, high)], -1).astype(BF16)
            sums.append(jnp.einsum("tcxy,tyz->tcxz", mixed, table, preferred_element_type=F32))
        both = [sums[0] + sums[1], sums[0] - sums[1]]
        real = jnp.concatenate([b[..., :quarter] for b in both], -1)
        imag = jnp.concatenate([b[..., quarter:] for b in both], -1)
        out_r = jnp.sum(own[..., :half] * real + own[..., half:] * imag, 1)
        out_i = jnp.sum(own[..., :half] * imag - own[..., half:] * real, 1)
        outs.append(jnp.concatenate([out_r, out_i], -1).reshape(-1, 2 * half))
    return outs


def cost(flops, moved):
    return pl.CostEstimate(flops=int(flops), bytes_accessed=int(moved), transcendentals=0)


VMEM = pl.BlockSpec(memory_space=pltpu.VMEM)
SMEM = pl.BlockSpec(memory_space=pltpu.SMEM)
HBM = pl.BlockSpec(memory_space=pltpu.HBM)
MIB = 1 << 20


def local(array):
    return pltpu.with_memory_space_constraint(array, pltpu.VMEM)


def remote(array):
    return pltpu.with_memory_space_constraint(array, pltpu.HBM)


def grant(mib):
    return pltpu.CompilerParams(vmem_limit_bytes=mib * MIB)


def data_term(starts, sampled, block, spatial, kspace, sens, per):
    frames, coils, rows, width = kspace.shape
    own = (rows // 2 // per, frames, per, width)
    plan = data_plan(rows // 2, 32)
    scratch = [
        pltpu.VMEM(sampled.shape, jnp.int32),
        pltpu.VMEM(block.shape, BF16),
        pltpu.VMEM((frames, width, width), BF16),
        pltpu.SemaphoreType.DMA((3,)),
    ]
    for _, _, size in plan:
        scratch += [
            pltpu.VMEM((frames, coils, size, width), BF16),
            pltpu.VMEM((coils, size, width), BF16),
            pltpu.SemaphoreType.DMA,
            pltpu.SemaphoreType.DMA,
        ]
    return pl.pallas_call(
        functools.partial(data_kernel, plan),
        in_specs=[SMEM] + [HBM] * 5,
        out_specs=[VMEM] * 3,
        out_shape=[
            pltpu.VMEM(own, F32),
            pltpu.VMEM(own, F32),
            pltpu.VMEM(spatial.shape, BF16),
        ],
        scratch_shapes=scratch,
        cost_estimate=cost(2 * frames * coils * rows * width * width, 2 * kspace.size),
        compiler_params=grant(44),
        name="data_term",
    )(starts, remote(sampled), remote(block), remote(spatial), remote(kspace), remote(sens))


def normal_term(starts, message, own, other, sens, left, right, picks):
    groups, per, _ = message.shape
    coils, _, width = sens.shape
    rows = own.shape[0] // (groups * per)
    half = width // 2
    return pl.pallas_call(
        normal_kernel,
        in_specs=[SMEM] + [VMEM] * 3 + [HBM] + [VMEM] * 3,
        out_specs=[VMEM] * 2,
        out_shape=[pltpu.VMEM(own.shape, F32)] * 2,
        scratch_shapes=[
            pltpu.VMEM((per, groups, half), F32),
            pltpu.VMEM((groups, per, 2, half, half), BF16),
            pltpu.VMEM((2, coils, rows, width), F32),
            pltpu.VMEM((2, coils, rows, width), BF16),
            pltpu.SemaphoreType.DMA((2,)),
        ],
        cost_estimate=cost(2 * groups * per * coils * rows * width * width, 4 * own.size),
        compiler_params=grant(40),
        name="normal_term",
    )(starts, message, local(own), local(other), remote(sens), local(left), local(right), local(picks))


def on_device(frame_size, coil_size, spatial, temporal, kspace, sampled, sensitivity):
    rows, rank, width = spatial.shape
    per = temporal.shape[0]
    total = per * frame_size
    half_rows = rows * frame_size
    half = width // 2
    swap = [(i, (i + 1) % coil_size) for i in range(coil_size)]
    own = lax.axis_index("coil") * half_rows
    other = (own + half_rows) % (coil_size * half_rows)
    row = lax.axis_index("frame") * rows
    starts = jnp.stack([other, own, own + row, other + row])
    spatial2 = spatial.reshape(rows * rank, width)
    block, left, right, picks = [jnp.asarray(table) for table in dft_tables(half)]

    message = jnp.pad(sampled, ((0, 0), (0, 2 * rank))).astype(F32)
    message = (message + jnp.pad(temporal, ((0, 0), (half, 0))).astype(F32)).astype(BF16)
    message = lax.all_to_all(
        jnp.broadcast_to(message[None], (frame_size, *message.shape)), "frame", 0, 0, tiled=True
    )
    regroup = rows % 16 != 0
    data_other, data_own, near = data_term(
        starts, sampled, block, spatial2, kspace, sensitivity, 16 if regroup else rows
    )
    message, data_other = lax.optimization_barrier((message, data_other))
    received = lax.ppermute(data_other, "coil", swap)
    image = image_rows(total, rows, rank, message[:, :, half:], near)
    image_other = lax.ppermute(image, "coil", swap)
    data = (data_own + received).astype(BF16)
    if regroup:
        data = data.transpose(1, 0, 2, 3).reshape(per, frame_size, rows, width).transpose(1, 0, 2, 3)
    image, image_other, data = lax.optimization_barrier((image, image_other, data))
    data = lax.all_to_all(data, "frame", 0, 0, tiled=True)
    data = data.reshape(total * rows, width)
    if regroup:
        sens = [lax.dynamic_slice_in_dim(sensitivity, at + row, rows, 1) for at in (own, other)]
        keep_own, send = normal_plain(message, (image, image_other), sens, left, right)
    else:
        keep_own, send = normal_term(starts, message, image, image_other, sensitivity, left, right, picks)
    grad = (keep_own + lax.ppermute(send, "coil", swap) - data.astype(F32)).astype(BF16)
    grad = local(grad)

    partial = pl.pallas_call(
        functools.partial(temporal_kernel, total, rows, rank),
        in_specs=[VMEM, VMEM],
        out_specs=VMEM,
        out_shape=pltpu.VMEM((frame_size * coil_size, 1, per * 2 * rank), F32),
        compiler_params=grant(12),
        name="temporal_rows",
    )(local(spatial2), grad)
    partial = lax.all_to_all(partial, ("frame", "coil"), 0, 0, tiled=True)
    spatial_grad = pl.pallas_call(
        functools.partial(spatial_kernel, total, rows, rank),
        in_specs=[VMEM, VMEM],
        out_specs=VMEM,
        out_shape=jax.ShapeDtypeStruct((rows * rank, width), F32),
        compiler_params=grant(12),
        name="spatial_rows",
    )(local(message[:, :, half:]), grad)
    temporal_grad = pl.pallas_call(
        sum_kernel,
        in_specs=[VMEM],
        out_specs=VMEM,
        out_shape=jax.ShapeDtypeStruct((per, 2 * rank), F32),
        compiler_params=grant(2),
        name="temporal_sum",
    )(partial)
    return (spatial_grad.reshape(rows, rank, width), temporal_grad)


def solution(mesh):
    placed = (
        P(("cuts", "coil", "frame"), None, None),
        P(("cuts", "frame"), None),
        P(("cuts", "frame"), "coil", None, None),
        P(("cuts", "frame"), None),
        P(("cuts", "coil"), None, None),
    )

    def body(*arrays):
        return on_device(mesh.shape["frame"], mesh.shape["coil"], *arrays)

    return jax.shard_map(
        body,
        mesh=mesh,
        in_specs=placed,
        out_specs=(P(("cuts", "coil", "frame"), None, None), P(("cuts", "frame"), None)),
        check_vma=False,
    )
```

```python
import functools
import math

import jax
import jax.numpy as jnp
import numpy as np
from jax import lax
from jax.experimental import pallas as pl
from jax.experimental.pallas import tpu as pltpu
from jax.sharding import PartitionSpec as P


F32 = jnp.float32
BF16 = jnp.bfloat16


def dft_tables(length):
    index = np.arange(length)
    angles = (index[:, None] * index[None, :] % length) * (2.0 * math.pi / length)
    cosine = np.cos(angles) / math.sqrt(length)
    sine_part = -np.sin(angles) / math.sqrt(length)
    block = np.block([[cosine, sine_part], [-sine_part, cosine]]).astype(np.float32)
    middle = length // 2
    left, right = [], []
    for odd in range(2):
        lines = np.concatenate([index[odd::2], length + index[odd::2]])
        near = np.concatenate([index[:middle], length + index[:middle]])
        left.append(block[:middle][:, lines])
        right.append(block.T[lines][:, near])
    order = np.concatenate([index[0::2], index[1::2]])
    picks = (index[:, None] == order[None, :]).astype(np.float32)
    return [np.asarray(a).astype(BF16) for a in (block[:length], np.stack(left), np.stack(right), picks)]


def dot(a, b):
    return jnp.dot(a, b, preferred_element_type=F32)


def dot_t(a, b):
    return lax.dot_general(a, b, (((1,), (1,)), ((), ())), preferred_element_type=F32)


def iota(shape, axis):
    return lax.broadcasted_iota(jnp.int32, shape, axis)


def spread(factors_ref, total, rows, rank):
    groups, per, lanes = factors_ref.shape
    height = 2 * total * rows
    frame = iota((height, groups), 0) // rows % total
    factors = factors_ref[...].astype(F32)
    picked = jnp.zeros((height, lanes), F32)
    for t in range(per):
        pick = jnp.where(frame == iota((height, groups), 1) * per + t, 1.0, 0.0).astype(BF16)
        picked = picked + dot(pick, factors[:, t].astype(BF16))
    mine = iota((height, lanes), 1) // rank == iota((height, lanes), 0) // (total * rows)
    return jnp.where(mine, picked, 0.0).astype(BF16)


def image_kernel(total, rows, rank, factors_ref, spatial_ref, image_ref):
    mid = spread(factors_ref, total, rows, rank)
    lanes = mid.shape[1]
    width = rows * rank
    tile = jnp.where(iota((lanes, width), 0) % rank == iota((lanes, width), 1) % rank, 1.0, 0.0)
    wide = dot(mid, tile.astype(BF16))
    height = wide.shape[0]
    same = iota((height, width), 0) % rows == iota((height, width), 1) // rank
    wide = jnp.where(same, wide, 0.0).astype(BF16)
    product = dot(wide, spatial_ref[...])
    half = height // 2
    mid_col = product.shape[1] // 2
    image_ref[:, :mid_col] = (product[:half, :mid_col] - product[half:, mid_col:]).astype(BF16)
    image_ref[:, mid_col:] = (product[:half, mid_col:] + product[half:, :mid_col]).astype(BF16)


def image_block_kernel(total, rows, rank, factors_ref, spatial_ref, image_ref, wide):
    groups, per, lanes = factors_ref.shape
    width = rows * rank
    half = total * rows
    source = iota((lanes, 2 * width), 1)
    source = source // width * rank + source % rank
    tile = jnp.where(iota((lanes, 2 * width), 0) == source, 1.0, 0.0).astype(BF16)
    same = iota((rows, width), 0) == iota((rows, width), 1) // rank
    factors = factors_ref[...].astype(F32)
    for t in range(per):
        lines = dot(factors[:, t].astype(BF16), tile)
        for group in range(groups):
            for part in range(2):
                line = lines[group : group + 1, part * width : (part + 1) * width]
                at = part * half + (group * per + t) * rows
                wide[at : at + rows] = jnp.where(same, line, 0.0).astype(BF16)
    spatial = spatial_ref[...]
    mid = spatial.shape[1] // 2
    real = dot(wide[:half], spatial)
    imag = dot(wide[half:], spatial)
    image_ref[:, :mid] = (real[:, :mid] - imag[:, mid:]).astype(BF16)
    image_ref[:, mid:] = (real[:, mid:] + imag[:, :mid]).astype(BF16)


def image_rows(total, rows, rank, factors, spatial):
    shape = (total * rows, spatial.shape[1])
    if rows % 16:
        body, scratch = image_kernel, []
    else:
        body, scratch = image_block_kernel, [pltpu.VMEM((2 * total * rows, rows * rank), BF16)]
    return pl.pallas_call(
        functools.partial(body, total, rows, rank),
        in_specs=[VMEM, VMEM],
        out_specs=VMEM,
        out_shape=pltpu.VMEM(shape, BF16),
        scratch_shapes=scratch,
        compiler_params=grant(12),
        name="image_rows",
    )(local(factors), spatial)


def both_parts(grad):
    half = grad.shape[1] // 2
    turned = jnp.concatenate([grad[:, half:], -grad[:, :half]], 1)
    return jnp.concatenate([grad, turned], 0)


def spatial_kernel(total, rows, rank, factors_ref, grad_ref, out_ref):
    mid = spread(factors_ref, total, rows, rank)
    lanes = mid.shape[1]
    width = rows * rank
    tile = jnp.where(iota((width, lanes), 0) % rank == iota((width, lanes), 1) % rank, 1.0, 0.0)
    wide = dot_t(tile.astype(BF16), mid)
    height = mid.shape[0]
    same = iota((width, height), 1) % rows == iota((width, height), 0) // rank
    wide = jnp.where(same, wide, 0.0).astype(BF16)
    out_ref[...] = dot(wide, both_parts(grad_ref[...]))


def temporal_kernel(total, rows, rank, spatial_ref, grad_ref, out_ref):
    product = dot_t(both_parts(grad_ref[...]), spatial_ref[...])
    height, width = product.shape
    same = iota((height, width), 0) % rows == iota((height, width), 1) // rank
    product = jnp.where(same, product, 0.0)
    lanes = 128
    fold = product[:, :lanes]
    for start in range(lanes, width, lanes):
        fold = fold + product[:, start : start + lanes]
    if rows % 8 == 0:
        fold = jnp.sum(fold.reshape(2 * total, rows, lanes), axis=1)
    else:
        pick = iota((2 * total, height), 0) == iota((2 * total, height), 1) // rows
        fold = jnp.dot(
            jnp.where(pick, 1.0, 0.0), fold, precision=lax.Precision.HIGHEST, preferred_element_type=F32
        )
    shift = lanes // 2
    while shift >= rank:
        fold = fold + pltpu.roll(fold, shift, 1)
        shift //= 2
    lane = iota((total, lanes), 1)
    both = jnp.where(lane // rank % 2 == 0, fold[:total], fold[total:])
    groups, _, span = out_ref.shape
    per = span // (2 * rank)
    copies = groups * per // total
    place = iota((1, span), 1) // (2 * rank)
    for group in range(groups // copies):
        line = both[group * per : group * per + 1, :span]
        for t in range(1, per):
            line = jnp.where(place == t, both[group * per + t : group * per + t + 1, :span], line)
        for copy in range(copies):
            out_ref[group * copies + copy] = line


def sum_kernel(parts_ref, out_ref):
    line = jnp.sum(parts_ref[...], axis=0)
    per, span = out_ref.shape
    for t in range(per):
        out_ref[t : t + 1, :] = line[:, t * span : (t + 1) * span]


def conj_sum(adjoint, sens_r, sens_i):
    half = sens_r.shape[-1]
    back_r, back_i = adjoint[..., :half], adjoint[..., half:]
    return (
        jnp.sum(sens_r * back_r + sens_i * back_i, axis=0),
        jnp.sum(sens_r * back_i - sens_i * back_r, axis=0),
    )


def data_plan(rows, tile):
    own = [(1, at, tile) for at in range(0, rows // 2, tile)]
    return own + [(part, at, rows // 2) for part, at in ((1, rows // 2), (0, 0), (0, rows // 2))]


def data_kernel(plan, starts_ref, sampled_ref, block_ref, spatial_ref, kspace_ref, sens_ref,
                other_ref, own_ref, spatial_out, mask, block, back, sems, *held):
    frames, coils, _, width = kspace_ref.shape
    _, _, per, _ = own_ref.shape
    half = width // 2
    pieces = [held[4 * k : 4 * k + 4] for k in range(len(plan))]

    def begin(step):
        if step < len(plan):
            for copy in fetch(step):
                copy.start()

    def fetch(step):
        part, at, size = plan[step]
        kspace_held, sens_held, kspace_sem, sens_sem = pieces[step]
        place = pl.ds(pl.multiple_of(starts_ref[part] + at, plan[0][2]), size)
        return (
            pltpu.make_async_copy(sens_ref.at[:, place], sens_held, sens_sem),
            pltpu.make_async_copy(kspace_ref.at[:, :, place], kspace_held, kspace_sem),
        )

    tables = [
        pltpu.make_async_copy(sampled_ref, mask, sems.at[0]),
        pltpu.make_async_copy(block_ref, block, sems.at[1]),
    ]
    staging = [pltpu.make_async_copy(spatial_ref, spatial_out, sems.at[2])]
    for copy in tables:
        copy.start()
    begin(0)
    for copy in tables:
        copy.wait()
    begin(1)
    for t in range(frames):
        keep = mask[t : t + 1, :].astype(F32)
        cosine = (block[:, :half].astype(F32) * keep).astype(BF16).T
        sine_part = (block[:, half:].astype(F32) * keep).astype(BF16).T
        back[t, :half, :half] = cosine
        back[t, :half, half:] = -sine_part
        back[t, half:, :half] = sine_part
        back[t, half:, half:] = cosine
    for step, (part, at, size) in enumerate(plan):
        begin(step + 2)
        if step == 1:
            for copy in staging:
                copy.start()
        for copy in fetch(step):
            copy.wait()
        kspace_held, sens_held = pieces[step][:2]
        sens = sens_held[...].astype(F32)
        sens_r, sens_i = sens[..., :half], sens[..., half:]
        out_ref = own_ref if part else other_ref
        group = slice(at // per, (at + size) // per)
        for t in range(frames):
            adjoint = dot(kspace_held[t].reshape(coils * size, width), back[t])
            real, imag = conj_sum(adjoint.reshape(coils, size, width), sens_r, sens_i)
            out_ref[group, t, :, :half] = real.reshape(size // per, per, half).astype(out_ref.dtype)
            out_ref[group, t, :, half:] = imag.reshape(size // per, per, half).astype(out_ref.dtype)
    for copy in staging:
        copy.wait()


def normal_kernel(starts_ref, message_ref, own_ref, other_ref, sens_ref, left_ref, right_ref, picks_ref,
                  own_out, other_out, masks, table, wide, held, sems):
    groups, per, _ = message_ref.shape
    _, coils, rows, width = held.shape
    copies = []
    for part in range(2):
        place = pl.ds(pl.multiple_of(starts_ref[2 + part], rows), rows)
        copies.append(pltpu.make_async_copy(sens_ref.at[:, place], held.at[part], sems.at[part]))
        copies[part].start()
    half = width // 2
    quarter = half // 2
    message = message_ref[...].astype(F32)
    for t in range(per):
        masks[t] = dot(message[:, t, :half].astype(BF16), picks_ref[...])

    @pl.loop(0, groups, unroll=4)
    def _(group):
        for t in range(per):
            keep = masks[t, pl.ds(group, 1), :]
            for k in range(2):
                lines = keep[:, k * quarter : (k + 1) * quarter]
                left = (left_ref[k].astype(F32) * jnp.concatenate([lines, lines], 1)).astype(BF16)
                near = dot(left, right_ref[k]).astype(BF16)
                table[group, t, k, :quarter] = near
                table[group, t, k, quarter:, :quarter] = -near[:, quarter:]
                table[group, t, k, quarter:, quarter:] = near[:, :quarter]

    for copy in copies:
        copy.wait()
    wide[...] = held[...].astype(F32)

    @pl.loop(0, groups, unroll=2)
    def _(group):
        for t in range(per):
            place = pl.ds(pl.multiple_of((group * per + t) * rows, rows), rows)
            plus, minus = [], []
            for part, image_ref in enumerate((own_ref, other_ref)):
                image = image_ref[place, :].astype(F32)
                image_r, image_i = image[:, :half], image[:, half:]
                sens_r, sens_i = wide[part, :, :, :half], wide[part, :, :, half:]
                coil_r = sens_r * image_r - sens_i * image_i
                coil_i = sens_r * image_i + sens_i * image_r
                low_r, high_r = coil_r[..., :quarter], coil_r[..., quarter:]
                low_i, high_i = coil_i[..., :quarter], coil_i[..., quarter:]
                shape = (coils * rows, half)
                plus.append(jnp.concatenate([low_r + high_r, low_i + high_i], -1).astype(BF16).reshape(shape))
                minus.append(jnp.concatenate([low_r - high_r, low_i - high_i], -1).astype(BF16).reshape(shape))
            shape = (2, coils, rows, half)
            plus = dot(jnp.concatenate(plus, 0), table[group, t, 0]).reshape(shape)
            minus = dot(jnp.concatenate(minus, 0), table[group, t, 1]).reshape(shape)
            for k, both in enumerate((plus + minus, plus - minus)):
                low = slice(k * quarter, (k + 1) * quarter)
                high = slice(half + k * quarter, half + (k + 1) * quarter)
                for part, out_ref in enumerate((own_out, other_out)):
                    real, imag = conj_sum(both[part], wide[part, :, :, low], wide[part, :, :, high])
                    out_ref[place, low] = real.astype(out_ref.dtype)
                    out_ref[place, high] = imag.astype(out_ref.dtype)


def normal_plain(message, images, sens, left, right):
    half = left.shape[2]
    quarter = half // 2
    flat = message.reshape(-1, message.shape[-1])[:, :half]
    frames = flat.shape[0]
    outs = []
    for image, own in zip(images, sens):
        image = image.reshape(frames, 1, -1, 2 * half).astype(F32)
        own = own.astype(F32)[None]
        coil_r = own[..., :half] * image[..., :half] - own[..., half:] * image[..., half:]
        coil_i = own[..., :half] * image[..., half:] + own[..., half:] * image[..., :half]
        low = [coil_r[..., :quarter], coil_i[..., :quarter]]
        high = [coil_r[..., quarter:], coil_i[..., quarter:]]
        sums = []
        for k, sign in enumerate((1, -1)):
            lines = flat[:, k::2]
            keep = jnp.concatenate([lines, lines], 1)
            near = jnp.einsum("yk,tk,kz->tyz", left[k], keep, right[k], preferred_element_type=F32)
            turned = jnp.concatenate([-near[..., quarter:], near[..., :quarter]], -1)
            table = jnp.concatenate([near, turned], 1).astype(BF16)
            mixed = jnp.concatenate([a + sign * b for a, b in zip(low, high)], -1).astype(BF16)
            sums.append(jnp.einsum("tcxy,tyz->tcxz", mixed, table, preferred_element_type=F32))
        both = [sums[0] + sums[1], sums[0] - sums[1]]
        real = jnp.concatenate([b[..., :quarter] for b in both], -1)
        imag = jnp.concatenate([b[..., quarter:] for b in both], -1)
        out_r = jnp.sum(own[..., :half] * real + own[..., half:] * imag, 1)
        out_i = jnp.sum(own[..., :half] * imag - own[..., half:] * real, 1)
        outs.append(jnp.concatenate([out_r, out_i], -1).reshape(-1, 2 * half))
    return outs


def cost(flops, moved):
    return pl.CostEstimate(flops=int(flops), bytes_accessed=int(moved), transcendentals=0)


VMEM = pl.BlockSpec(memory_space=pltpu.VMEM)
SMEM = pl.BlockSpec(memory_space=pltpu.SMEM)
HBM = pl.BlockSpec(memory_space=pltpu.HBM)
MIB = 1 << 20


def local(array):
    return pltpu.with_memory_space_constraint(array, pltpu.VMEM)


def remote(array):
    return pltpu.with_memory_space_constraint(array, pltpu.HBM)


def grant(mib):
    return pltpu.CompilerParams(vmem_limit_bytes=mib * MIB)


def data_term(starts, sampled, block, spatial, kspace, sens, per):
    frames, coils, rows, width = kspace.shape
    own = (rows // 2 // per, frames, per, width)
    plan = data_plan(rows // 2, 32)
    scratch = [
        pltpu.VMEM(sampled.shape, jnp.int32),
        pltpu.VMEM(block.shape, BF16),
        pltpu.VMEM((frames, width, width), BF16),
        pltpu.SemaphoreType.DMA((3,)),
    ]
    for _, _, size in plan:
        scratch += [
            pltpu.VMEM((frames, coils, size, width), BF16),
            pltpu.VMEM((coils, size, width), BF16),
            pltpu.SemaphoreType.DMA,
            pltpu.SemaphoreType.DMA,
        ]
    return pl.pallas_call(
        functools.partial(data_kernel, plan),
        in_specs=[SMEM] + [HBM] * 5,
        out_specs=[VMEM] * 3,
        out_shape=[
            pltpu.VMEM(own, BF16),
            pltpu.VMEM(own, F32),
            pltpu.VMEM(spatial.shape, BF16),
        ],
        scratch_shapes=scratch,
        cost_estimate=cost(2 * frames * coils * rows * width * width, 2 * kspace.size),
        compiler_params=grant(44),
        name="data_term",
    )(starts, remote(sampled), remote(block), remote(spatial), remote(kspace), remote(sens))


def normal_term(starts, message, own, other, sens, left, right, picks):
    groups, per, _ = message.shape
    coils, _, width = sens.shape
    rows = own.shape[0] // (groups * per)
    half = width // 2
    return pl.pallas_call(
        normal_kernel,
        in_specs=[SMEM] + [VMEM] * 3 + [HBM] + [VMEM] * 3,
        out_specs=[VMEM] * 2,
        out_shape=[pltpu.VMEM(own.shape, F32), pltpu.VMEM(own.shape, BF16)],
        scratch_shapes=[
            pltpu.VMEM((per, groups, half), F32),
            pltpu.VMEM((groups, per, 2, half, half), BF16),
            pltpu.VMEM((2, coils, rows, width), F32),
            pltpu.VMEM((2, coils, rows, width), BF16),
            pltpu.SemaphoreType.DMA((2,)),
        ],
        cost_estimate=cost(2 * groups * per * coils * rows * width * width, 4 * own.size),
        compiler_params=grant(40),
        name="normal_term",
    )(starts, message, local(own), local(other), remote(sens), local(left), local(right), local(picks))


def on_device(frame_size, coil_size, spatial, temporal, kspace, sampled, sensitivity):
    rows, rank, width = spatial.shape
    per = temporal.shape[0]
    total = per * frame_size
    half_rows = rows * frame_size
    half = width // 2
    swap = [(i, (i + 1) % coil_size) for i in range(coil_size)]
    own = lax.axis_index("coil") * half_rows
    other = (own + half_rows) % (coil_size * half_rows)
    row = lax.axis_index("frame") * rows
    starts = jnp.stack([other, own, own + row, other + row])
    spatial2 = spatial.reshape(rows * rank, width)
    block, left, right, picks = [jnp.asarray(table) for table in dft_tables(half)]

    message = jnp.pad(sampled, ((0, 0), (0, 2 * rank))).astype(F32)
    message = (message + jnp.pad(temporal, ((0, 0), (half, 0))).astype(F32)).astype(BF16)
    message = lax.all_to_all(
        jnp.broadcast_to(message[None], (frame_size, *message.shape)), "frame", 0, 0, tiled=True
    )
    regroup = rows % 16 != 0
    data_other, data_own, near = data_term(
        starts, sampled, block, spatial2, kspace, sensitivity, 16 if regroup else rows
    )
    message, data_other = lax.optimization_barrier((message, data_other))
    received = lax.ppermute(data_other, "coil", swap)
    image = image_rows(total, rows, rank, message[:, :, half:], near)
    image_other = lax.ppermute(image, "coil", swap)
    data = (data_own + received).astype(BF16)
    if regroup:
        data = data.transpose(1, 0, 2, 3).reshape(per, frame_size, rows, width).transpose(1, 0, 2, 3)
    image, image_other, data = lax.optimization_barrier((image, image_other, data))
    data = lax.all_to_all(data, "frame", 0, 0, tiled=True)
    data = data.reshape(total * rows, width)
    if regroup:
        sens = [lax.dynamic_slice_in_dim(sensitivity, at + row, rows, 1) for at in (own, other)]
        keep_own, send = normal_plain(message, (image, image_other), sens, left, right)
    else:
        keep_own, send = normal_term(starts, message, image, image_other, sensitivity, left, right, picks)
    grad = (keep_own + lax.ppermute(send, "coil", swap) - data.astype(F32)).astype(BF16)
    grad = local(grad)

    partial = pl.pallas_call(
        functools.partial(temporal_kernel, total, rows, rank),
        in_specs=[VMEM, VMEM],
        out_specs=VMEM,
        out_shape=pltpu.VMEM((frame_size * coil_size, 1, per * 2 * rank), F32),
        compiler_params=grant(12),
        name="temporal_rows",
    )(local(spatial2), grad)
    partial = lax.all_to_all(partial, ("frame", "coil"), 0, 0, tiled=True)
    spatial_grad = pl.pallas_call(
        functools.partial(spatial_kernel, total, rows, rank),
        in_specs=[VMEM, VMEM],
        out_specs=VMEM,
        out_shape=jax.ShapeDtypeStruct((rows * rank, width), F32),
        compiler_params=grant(12),
        name="spatial_rows",
    )(local(message[:, :, half:]), grad)
    temporal_grad = pl.pallas_call(
        sum_kernel,
        in_specs=[VMEM],
        out_specs=VMEM,
        out_shape=jax.ShapeDtypeStruct((per, 2 * rank), F32),
        compiler_params=grant(2),
        name="temporal_sum",
    )(partial)
    return (spatial_grad.reshape(rows, rank, width), temporal_grad)


def solution(mesh):
    placed = (
        P(("cuts", "coil", "frame"), None, None),
        P(("cuts", "frame"), None),
        P(("cuts", "frame"), "coil", None, None),
        P(("cuts", "frame"), None),
        P(("cuts", "coil"), None, None),
    )

    def body(*arrays):
        return on_device(mesh.shape["frame"], mesh.shape["coil"], *arrays)

    return jax.shard_map(
        body,
        mesh=mesh,
        in_specs=placed,
        out_specs=(P(("cuts", "coil", "frame"), None, None), P(("cuts", "frame"), None)),
        check_vma=False,
    )
```

```python
import functools
import math

import jax
import jax.numpy as jnp
import numpy as np
from jax import lax
from jax.experimental import pallas as pl
from jax.experimental.pallas import tpu as pltpu
from jax.sharding import PartitionSpec as P


F32 = jnp.float32
BF16 = jnp.bfloat16


def dft_tables(length):
    index = np.arange(length)
    angles = (index[:, None] * index[None, :] % length) * (2.0 * math.pi / length)
    cosine = np.cos(angles) / math.sqrt(length)
    sine_part = -np.sin(angles) / math.sqrt(length)
    block = np.block([[cosine, sine_part], [-sine_part, cosine]]).astype(np.float32)
    middle = length // 2
    left, right = [], []
    for odd in range(2):
        lines = np.concatenate([index[odd::2], length + index[odd::2]])
        near = np.concatenate([index[:middle], length + index[:middle]])
        left.append(block[:middle][:, lines])
        right.append(block.T[lines][:, near])
    order = np.concatenate([index[0::2], index[1::2]])
    picks = (index[:, None] == order[None, :]).astype(np.float32)
    return [np.asarray(a).astype(BF16) for a in (block[:length], np.stack(left), np.stack(right), picks)]


def dot(a, b):
    return jnp.dot(a, b, preferred_element_type=F32)


def dot_t(a, b):
    return lax.dot_general(a, b, (((1,), (1,)), ((), ())), preferred_element_type=F32)


def iota(shape, axis):
    return lax.broadcasted_iota(jnp.int32, shape, axis)


def spread(factors_ref, total, rows, rank):
    groups, per, lanes = factors_ref.shape
    height = 2 * total * rows
    frame = iota((height, groups), 0) // rows % total
    factors = factors_ref[...].astype(F32)
    picked = jnp.zeros((height, lanes), F32)
    for t in range(per):
        pick = jnp.where(frame == iota((height, groups), 1) * per + t, 1.0, 0.0).astype(BF16)
        picked = picked + dot(pick, factors[:, t].astype(BF16))
    mine = iota((height, lanes), 1) // rank == iota((height, lanes), 0) // (total * rows)
    return jnp.where(mine, picked, 0.0).astype(BF16)


def image_kernel(total, rows, rank, factors_ref, spatial_ref, image_ref):
    mid = spread(factors_ref, total, rows, rank)
    lanes = mid.shape[1]
    width = rows * rank
    tile = jnp.where(iota((lanes, width), 0) % rank == iota((lanes, width), 1) % rank, 1.0, 0.0)
    wide = dot(mid, tile.astype(BF16))
    height = wide.shape[0]
    same = iota((height, width), 0) % rows == iota((height, width), 1) // rank
    wide = jnp.where(same, wide, 0.0).astype(BF16)
    product = dot(wide, spatial_ref[...])
    half = height // 2
    mid_col = product.shape[1] // 2
    image_ref[:, :mid_col] = (product[:half, :mid_col] - product[half:, mid_col:]).astype(BF16)
    image_ref[:, mid_col:] = (product[:half, mid_col:] + product[half:, :mid_col]).astype(BF16)


def image_block_kernel(total, rows, rank, factors_ref, spatial_ref, image_ref, wide):
    groups, per, lanes = factors_ref.shape
    width = rows * rank
    half = total * rows
    source = iota((lanes, 2 * width), 1)
    source = source // width * rank + source % rank
    tile = jnp.where(iota((lanes, 2 * width), 0) == source, 1.0, 0.0).astype(BF16)
    same = iota((rows, width), 0) == iota((rows, width), 1) // rank
    factors = factors_ref[...].astype(F32)
    for t in range(per):
        lines = dot(factors[:, t].astype(BF16), tile)
        for group in range(groups):
            for part in range(2):
                line = lines[group : group + 1, part * width : (part + 1) * width]
                at = part * half + (group * per + t) * rows
                wide[at : at + rows] = jnp.where(same, line, 0.0).astype(BF16)
    spatial = spatial_ref[...]
    mid = spatial.shape[1] // 2
    real = dot(wide[:half], spatial)
    imag = dot(wide[half:], spatial)
    image_ref[:, :mid] = (real[:, :mid] - imag[:, mid:]).astype(BF16)
    image_ref[:, mid:] = (real[:, mid:] + imag[:, :mid]).astype(BF16)


def image_rows(total, rows, rank, factors, spatial):
    shape = (total * rows, spatial.shape[1])
    if rows % 16:
        body, scratch = image_kernel, []
    else:
        body, scratch = image_block_kernel, [pltpu.VMEM((2 * total * rows, rows * rank), BF16)]
    return pl.pallas_call(
        functools.partial(body, total, rows, rank),
        in_specs=[VMEM, VMEM],
        out_specs=VMEM,
        out_shape=pltpu.VMEM(shape, BF16),
        scratch_shapes=scratch,
        compiler_params=grant(12),
        name="image_rows",
    )(local(factors), spatial)


def both_parts(grad):
    half = grad.shape[1] // 2
    turned = jnp.concatenate([grad[:, half:], -grad[:, :half]], 1)
    return jnp.concatenate([grad, turned], 0)


def spatial_kernel(total, rows, rank, factors_ref, grad_ref, out_ref):
    mid = spread(factors_ref, total, rows, rank)
    lanes = mid.shape[1]
    width = rows * rank
    tile = jnp.where(iota((width, lanes), 0) % rank == iota((width, lanes), 1) % rank, 1.0, 0.0)
    wide = dot_t(tile.astype(BF16), mid)
    height = mid.shape[0]
    same = iota((width, height), 1) % rows == iota((width, height), 0) // rank
    wide = jnp.where(same, wide, 0.0).astype(BF16)
    out_ref[...] = dot(wide, both_parts(grad_ref[...]))


def temporal_kernel(total, rows, rank, spatial_ref, grad_ref, out_ref):
    product = dot_t(both_parts(grad_ref[...]), spatial_ref[...])
    height, width = product.shape
    same = iota((height, width), 0) % rows == iota((height, width), 1) // rank
    product = jnp.where(same, product, 0.0)
    lanes = 128
    fold = product[:, :lanes]
    for start in range(lanes, width, lanes):
        fold = fold + product[:, start : start + lanes]
    if rows % 8 == 0:
        fold = jnp.sum(fold.reshape(2 * total, rows, lanes), axis=1)
    else:
        pick = iota((2 * total, height), 0) == iota((2 * total, height), 1) // rows
        fold = jnp.dot(
            jnp.where(pick, 1.0, 0.0), fold, precision=lax.Precision.HIGHEST, preferred_element_type=F32
        )
    shift = lanes // 2
    while shift >= rank:
        fold = fold + pltpu.roll(fold, shift, 1)
        shift //= 2
    lane = iota((total, lanes), 1)
    both = jnp.where(lane // rank % 2 == 0, fold[:total], fold[total:])
    groups, _, span = out_ref.shape
    per = span // (2 * rank)
    copies = groups * per // total
    place = iota((1, span), 1) // (2 * rank)
    for group in range(groups // copies):
        line = both[group * per : group * per + 1, :span]
        for t in range(1, per):
            line = jnp.where(place == t, both[group * per + t : group * per + t + 1, :span], line)
        for copy in range(copies):
            out_ref[group * copies + copy] = line


def sum_kernel(parts_ref, out_ref):
    line = jnp.sum(parts_ref[...], axis=0)
    per, span = out_ref.shape
    for t in range(per):
        out_ref[t : t + 1, :] = line[:, t * span : (t + 1) * span]


def conj_sum(adjoint, sens_r, sens_i):
    half = sens_r.shape[-1]
    back_r, back_i = adjoint[..., :half], adjoint[..., half:]
    return (
        jnp.sum(sens_r * back_r + sens_i * back_i, axis=0),
        jnp.sum(sens_r * back_i - sens_i * back_r, axis=0),
    )


def data_plan(rows, tile):
    own = [(1, at, tile) for at in range(0, rows // 2, tile)]
    return own + [(part, at, rows // 2) for part, at in ((1, rows // 2), (0, 0), (0, rows // 2))]


def data_kernel(plan, starts_ref, sampled_ref, block_ref, spatial_ref, kspace_ref, sens_ref,
                other_ref, own_ref, spatial_out, sens_out, mask, block, back, sems, sens_sems, *held):
    frames, coils, _, width = kspace_ref.shape
    _, _, per, _ = own_ref.shape
    half = width // 2
    pieces = [held[4 * k : 4 * k + 4] for k in range(len(plan))]

    def begin(step):
        if step < len(plan):
            for copy in fetch(step):
                copy.start()

    def fetch(step):
        part, at, size = plan[step]
        kspace_held, sens_held, kspace_sem, sens_sem = pieces[step]
        place = pl.ds(pl.multiple_of(starts_ref[part] + at, plan[0][2]), size)
        return (
            pltpu.make_async_copy(sens_ref.at[:, place], sens_held, sens_sem),
            pltpu.make_async_copy(kspace_ref.at[:, :, place], kspace_held, kspace_sem),
        )

    tables = [
        pltpu.make_async_copy(sampled_ref, mask, sems.at[0]),
        pltpu.make_async_copy(block_ref, block, sems.at[1]),
    ]
    staging = [pltpu.make_async_copy(spatial_ref, spatial_out, sems.at[2])]
    near = sens_out.shape[2]
    for part in range(2):
        place = pl.ds(pl.multiple_of(starts_ref[2 + part], near), near)
        staging.append(
            pltpu.make_async_copy(sens_ref.at[:, place], sens_out.at[part], sens_sems.at[part])
        )
    for copy in tables:
        copy.start()
    begin(0)
    for copy in tables:
        copy.wait()
    begin(1)
    for t in range(frames):
        keep = mask[t : t + 1, :].astype(F32)
        cosine = (block[:, :half].astype(F32) * keep).astype(BF16).T
        sine_part = (block[:, half:].astype(F32) * keep).astype(BF16).T
        back[t, :half, :half] = cosine
        back[t, :half, half:] = -sine_part
        back[t, half:, :half] = sine_part
        back[t, half:, half:] = cosine
    for step, (part, at, size) in enumerate(plan):
        begin(step + 2)
        if step == 1:
            for copy in staging:
                copy.start()
        for copy in fetch(step):
            copy.wait()
        kspace_held, sens_held = pieces[step][:2]
        sens = sens_held[...].astype(F32)
        sens_r, sens_i = sens[..., :half], sens[..., half:]
        out_ref = own_ref if part else other_ref
        group = slice(at // per, (at + size) // per)
        for t in range(frames):
            adjoint = dot(kspace_held[t].reshape(coils * size, width), back[t])
            real, imag = conj_sum(adjoint.reshape(coils, size, width), sens_r, sens_i)
            out_ref[group, t, :, :half] = real.reshape(size // per, per, half).astype(out_ref.dtype)
            out_ref[group, t, :, half:] = imag.reshape(size // per, per, half).astype(out_ref.dtype)
    for copy in staging:
        copy.wait()


def normal_kernel(message_ref, own_ref, other_ref, held, left_ref, right_ref, picks_ref,
                  own_out, other_out, masks, table, wide):
    groups, per, _ = message_ref.shape
    _, coils, rows, width = held.shape
    half = width // 2
    quarter = half // 2
    message = message_ref[...].astype(F32)
    for t in range(per):
        masks[t] = dot(message[:, t, :half].astype(BF16), picks_ref[...])

    @pl.loop(0, groups, unroll=4)
    def _(group):
        for t in range(per):
            keep = masks[t, pl.ds(group, 1), :]
            for k in range(2):
                lines = keep[:, k * quarter : (k + 1) * quarter]
                left = (left_ref[k].astype(F32) * jnp.concatenate([lines, lines], 1)).astype(BF16)
                near = dot(left, right_ref[k]).astype(BF16)
                table[group, t, k, :quarter] = near
                table[group, t, k, quarter:, :quarter] = -near[:, quarter:]
                table[group, t, k, quarter:, quarter:] = near[:, :quarter]

    wide[...] = held[...].astype(F32)

    @pl.loop(0, groups, unroll=4)
    def _(group):
        for t in range(per):
            place = pl.ds(pl.multiple_of((group * per + t) * rows, rows), rows)
            plus, minus = [], []
            for part, image_ref in enumerate((own_ref, other_ref)):
                image = image_ref[place, :].astype(F32)
                image_r, image_i = image[:, :half], image[:, half:]
                sens_r, sens_i = wide[part, :, :, :half], wide[part, :, :, half:]
                coil_r = sens_r * image_r - sens_i * image_i
                coil_i = sens_r * image_i + sens_i * image_r
                low_r, high_r = coil_r[..., :quarter], coil_r[..., quarter:]
                low_i, high_i = coil_i[..., :quarter], coil_i[..., quarter:]
                shape = (coils * rows, half)
                plus.append(jnp.concatenate([low_r + high_r, low_i + high_i], -1).astype(BF16).reshape(shape))
                minus.append(jnp.concatenate([low_r - high_r, low_i - high_i], -1).astype(BF16).reshape(shape))
            shape = (2, coils, rows, half)
            plus = dot(jnp.concatenate(plus, 0), table[group, t, 0]).reshape(shape)
            minus = dot(jnp.concatenate(minus, 0), table[group, t, 1]).reshape(shape)
            for k, both in enumerate((plus + minus, plus - minus)):
                low = slice(k * quarter, (k + 1) * quarter)
                high = slice(half + k * quarter, half + (k + 1) * quarter)
                for part, out_ref in enumerate((own_out, other_out)):
                    real, imag = conj_sum(both[part], wide[part, :, :, low], wide[part, :, :, high])
                    out_ref[place, low] = real.astype(out_ref.dtype)
                    out_ref[place, high] = imag.astype(out_ref.dtype)


def normal_plain(message, images, sens, left, right):
    half = left.shape[2]
    quarter = half // 2
    flat = message.reshape(-1, message.shape[-1])[:, :half]
    frames = flat.shape[0]
    outs = []
    for image, own in zip(images, sens):
        image = image.reshape(frames, 1, -1, 2 * half).astype(F32)
        own = own.astype(F32)[None]
        coil_r = own[..., :half] * image[..., :half] - own[..., half:] * image[..., half:]
        coil_i = own[..., :half] * image[..., half:] + own[..., half:] * image[..., :half]
        low = [coil_r[..., :quarter], coil_i[..., :quarter]]
        high = [coil_r[..., quarter:], coil_i[..., quarter:]]
        sums = []
        for k, sign in enumerate((1, -1)):
            lines = flat[:, k::2]
            keep = jnp.concatenate([lines, lines], 1)
            near = jnp.einsum("yk,tk,kz->tyz", left[k], keep, right[k], preferred_element_type=F32)
            turned = jnp.concatenate([-near[..., quarter:], near[..., :quarter]], -1)
            table = jnp.concatenate([near, turned], 1).astype(BF16)
            mixed = jnp.concatenate([a + sign * b for a, b in zip(low, high)], -1).astype(BF16)
            sums.append(jnp.einsum("tcxy,tyz->tcxz", mixed, table, preferred_element_type=F32))
        both = [sums[0] + sums[1], sums[0] - sums[1]]
        real = jnp.concatenate([b[..., :quarter] for b in both], -1)
        imag = jnp.concatenate([b[..., quarter:] for b in both], -1)
        out_r = jnp.sum(own[..., :half] * real + own[..., half:] * imag, 1)
        out_i = jnp.sum(own[..., :half] * imag - own[..., half:] * real, 1)
        outs.append(jnp.concatenate([out_r, out_i], -1).reshape(-1, 2 * half))
    return outs


def cost(flops, moved):
    return pl.CostEstimate(flops=int(flops), bytes_accessed=int(moved), transcendentals=0)


VMEM = pl.BlockSpec(memory_space=pltpu.VMEM)
SMEM = pl.BlockSpec(memory_space=pltpu.SMEM)
HBM = pl.BlockSpec(memory_space=pltpu.HBM)
MIB = 1 << 20


def local(array):
    return pltpu.with_memory_space_constraint(array, pltpu.VMEM)


def remote(array):
    return pltpu.with_memory_space_constraint(array, pltpu.HBM)


def grant(mib):
    return pltpu.CompilerParams(vmem_limit_bytes=mib * MIB)


def data_term(starts, sampled, block, spatial, kspace, sens, near, per):
    frames, coils, rows, width = kspace.shape
    own = (rows // 2 // per, frames, per, width)
    plan = data_plan(rows // 2, 32)
    scratch = [
        pltpu.VMEM(sampled.shape, jnp.int32),
        pltpu.VMEM(block.shape, BF16),
        pltpu.VMEM((frames, width, width), BF16),
        pltpu.SemaphoreType.DMA((3,)),
        pltpu.SemaphoreType.DMA((2,)),
    ]
    for _, _, size in plan:
        scratch += [
            pltpu.VMEM((frames, coils, size, width), BF16),
            pltpu.VMEM((coils, size, width), BF16),
            pltpu.SemaphoreType.DMA,
            pltpu.SemaphoreType.DMA,
        ]
    return pl.pallas_call(
        functools.partial(data_kernel, plan),
        in_specs=[SMEM] + [HBM] * 5,
        out_specs=[VMEM] * 4,
        out_shape=[
            pltpu.VMEM(own, BF16),
            pltpu.VMEM(own, F32),
            pltpu.VMEM(spatial.shape, BF16),
            pltpu.VMEM((2, coils, near, width), BF16),
        ],
        scratch_shapes=scratch,
        cost_estimate=cost(2 * frames * coils * rows * width * width, 2 * kspace.size),
        compiler_params=grant(44),
        name="data_term",
    )(starts, remote(sampled), remote(block), remote(spatial), remote(kspace), remote(sens))


def normal_term(message, own, other, sens, left, right, picks):
    groups, per, _ = message.shape
    _, coils, rows, width = sens.shape
    half = width // 2
    return pl.pallas_call(
        normal_kernel,
        in_specs=[VMEM] * 7,
        out_specs=[VMEM] * 2,
        out_shape=[pltpu.VMEM(own.shape, F32), pltpu.VMEM(own.shape, BF16)],
        scratch_shapes=[
            pltpu.VMEM((per, groups, half), F32),
            pltpu.VMEM((groups, per, 2, half, half), BF16),
            pltpu.VMEM((2, coils, rows, width), F32),
        ],
        cost_estimate=cost(2 * groups * per * coils * rows * width * width, 4 * own.size),
        compiler_params=grant(40),
        name="normal_term",
    )(message, local(own), local(other), sens, local(left), local(right), local(picks))


def on_device(frame_size, coil_size, spatial, temporal, kspace, sampled, sensitivity):
    rows, rank, width = spatial.shape
    per = temporal.shape[0]
    total = per * frame_size
    half_rows = rows * frame_size
    half = width // 2
    swap = [(i, (i + 1) % coil_size) for i in range(coil_size)]
    own = lax.axis_index("coil") * half_rows
    other = (own + half_rows) % (coil_size * half_rows)
    row = lax.axis_index("frame") * rows
    starts = jnp.stack([other, own, own + row, other + row])
    spatial2 = spatial.reshape(rows * rank, width)
    block, left, right, picks = [jnp.asarray(table) for table in dft_tables(half)]

    message = jnp.pad(sampled, ((0, 0), (0, 2 * rank))).astype(F32)
    message = (message + jnp.pad(temporal, ((0, 0), (half, 0))).astype(F32)).astype(BF16)
    message = lax.all_to_all(
        jnp.broadcast_to(message[None], (frame_size, *message.shape)), "frame", 0, 0, tiled=True
    )
    regroup = rows % 16 != 0
    data_other, data_own, near, sens_near = data_term(
        starts, sampled, block, spatial2, kspace, sensitivity, rows, 16 if regroup else rows
    )
    message, data_other = lax.optimization_barrier((message, data_other))
    received = lax.ppermute(data_other, "coil", swap)
    image = image_rows(total, rows, rank, message[:, :, half:], near)
    image_other = lax.ppermute(image, "coil", swap)
    data = (data_own + received).astype(BF16)
    if regroup:
        data = data.transpose(1, 0, 2, 3).reshape(per, frame_size, rows, width).transpose(1, 0, 2, 3)
    image, image_other, data = lax.optimization_barrier((image, image_other, data))
    data = lax.all_to_all(data, "frame", 0, 0, tiled=True)
    data = data.reshape(total * rows, width)
    if regroup:
        sens = [lax.dynamic_slice_in_dim(sensitivity, at + row, rows, 1) for at in (own, other)]
        keep_own, send = normal_plain(message, (image, image_other), sens, left, right)
    else:
        keep_own, send = normal_term(message, image, image_other, sens_near, left, right, picks)
    grad = (keep_own + lax.ppermute(send, "coil", swap) - data.astype(F32)).astype(BF16)
    grad = local(grad)

    partial = pl.pallas_call(
        functools.partial(temporal_kernel, total, rows, rank),
        in_specs=[VMEM, VMEM],
        out_specs=VMEM,
        out_shape=pltpu.VMEM((frame_size * coil_size, 1, per * 2 * rank), F32),
        compiler_params=grant(12),
        name="temporal_rows",
    )(local(spatial2), grad)
    partial = lax.all_to_all(partial, ("frame", "coil"), 0, 0, tiled=True)
    spatial_grad = pl.pallas_call(
        functools.partial(spatial_kernel, total, rows, rank),
        in_specs=[VMEM, VMEM],
        out_specs=VMEM,
        out_shape=jax.ShapeDtypeStruct((rows * rank, width), F32),
        compiler_params=grant(12),
        name="spatial_rows",
    )(local(message[:, :, half:]), grad)
    temporal_grad = pl.pallas_call(
        sum_kernel,
        in_specs=[VMEM],
        out_specs=VMEM,
        out_shape=jax.ShapeDtypeStruct((per, 2 * rank), F32),
        compiler_params=grant(2),
        name="temporal_sum",
    )(partial)
    return (spatial_grad.reshape(rows, rank, width), temporal_grad)


def solution(mesh):
    placed = (
        P(("cuts", "coil", "frame"), None, None),
        P(("cuts", "frame"), None),
        P(("cuts", "frame"), "coil", None, None),
        P(("cuts", "frame"), None),
        P(("cuts", "coil"), None, None),
    )

    def body(*arrays):
        return on_device(mesh.shape["frame"], mesh.shape["coil"], *arrays)

    return jax.shard_map(
        body,
        mesh=mesh,
        in_specs=placed,
        out_specs=(P(("cuts", "coil", "frame"), None, None), P(("cuts", "frame"), None)),
        check_vma=False,
    )
```
